32 devices in a mesh: dp: 8 (over y, x, core), mem: 4 (over z).
Axes of the slice: x: 2, y: 2, z: 4, core: 2. Of those that a mesh axis runs over, the one named last changes fastest.
Arguments:
- inputs: bfloat16 [32, 100, 768], P('dp'), may hold values from -6 to 6
- memory: bfloat16 [32, 1280, 768], P('dp', 'mem'), may hold values from -6 to 6
- lengths: int32 [32], P('dp'), may hold values from 1 to 1280, as said below
- self_query: bfloat16 [768, 768], P('dp'), may hold values from -0.21875 to 0.21875
- self_key: bfloat16 [768, 768], P('dp'), may hold values from -0.21875 to 0.21875
- self_value: bfloat16 [768, 768], P('dp'), may hold values from -0.21875 to 0.21875
- self_out: bfloat16 [768, 768], P('dp'), may hold values from -0.625 to 0.625
- cross_query: bfloat16 [768, 768], P('dp'), may hold values from -0.21875 to 0.21875
- cross_key: bfloat16 [768, 768], P('dp'), may hold values from -0.21875 to 0.21875
- cross_value: bfloat16 [768, 768], P('dp'), may hold values from -0.21875 to 0.21875
- cross_out: bfloat16 [768, 768], P('dp'), may hold values from -1 to 1
- expand_weight: bfloat16 [768, 3072], P('dp'), may hold values from -0.21875 to 0.21875
- contract_weight: bfloat16 [3072, 768], P('dp'), may hold values from -0.109375 to 0.109375
- gain_one: float32 [768], replicated, may hold values from 0.5 to 1.5
- shift_one: float32 [768], replicated, may hold values from -1.5 to 1.5
- gain_two: float32 [768], replicated, may hold values from 0.5 to 1.5
- shift_two: float32 [768], replicated, may hold values from -1.5 to 1.5
- gain_three: float32 [768], replicated, may hold values from 0.5 to 1.5
- shift_three: float32 [768], replicated, may hold values from -1.5 to 1.5
- cotangent: bfloat16 [32, 100, 768], P('dp'), may hold values from -6 to 6
Outputs:
- output: float32 [32, 100, 768], P('dp')
- input_grad: float32 [32, 100, 768], P('dp')
- memory_grad: float32 [32, 1280, 768], P('dp', 'mem')
- self_query_grad: float32 [768, 768], P('dp')
- self_key_grad: float32 [768, 768], P('dp')
- self_value_grad: float32 [768, 768], P('dp')
- self_out_grad: float32 [768, 768], P('dp')
- cross_query_grad: float32 [768, 768], P('dp')
- cross_key_grad: float32 [768, 768], P(('dp', 'mem'))
- cross_value_grad: float32 [768, 768], P(('dp', 'mem'))
- cross_out_grad: float32 [768, 768], P('dp')
- expand_grad: float32 [768, 3072], P('dp')
- contract_grad: float32 [3072, 768], P('dp')
- gain_one_grad: float32 [768], P('dp')
- shift_one_grad: float32 [768], P('dp')
- gain_two_grad: float32 [768], P('dp')
- shift_two_grad: float32 [768], P('dp')
- gain_three_grad: float32 [768], P('dp')
- shift_three_grad: float32 [768], P('dp')
The draws below stay inside these ranges and needn't reach their ends.
Inputs may be any that keep to these rules, and one draw needn't show every extreme that they name: `lengths`: the number of valid memory tokens of each image; in each aligned block of 4 images one image has all 1280.
All inputs are finite; a program needn't handle non-finite values.
Results may differ from the reference program's by a relative error of at most 0.023.
Values may be sent and summed in bfloat16 or wider, within the bound.
A program may use at most 320 MiB of HBM per device.

```python
import jax
import jax.numpy as jnp
from jax import lax

H = 12
HD = 64
D = 768
FF = 3072
Q = 100
MEM = 1280
IMG_DEV = 4
IMAGES = 32


def draw_lengths(key, part):
    base = jax.random.randint(jax.random.fold_in(key, 11), (IMAGES,), 1, MEM + 1)
    chosen = jax.random.randint(jax.random.fold_in(key, 12), (IMAGES // IMG_DEV,), 0, IMG_DEV)
    places = jnp.arange(IMAGES, dtype=jnp.int32) % IMG_DEV
    marked = places == jnp.repeat(chosen, IMG_DEV, total_repeat_length=IMAGES)
    return jnp.where(marked, MEM, base).astype(jnp.int32)


def block_levels(key, dims, split, smallest, top_value):
    def one(dim, parts):
        draws = jax.random.uniform(jax.random.fold_in(jax.random.fold_in(key, 6), dim), (parts,), jnp.float32, smallest / len(split), top_value / len(split))
        return jnp.repeat(jnp.exp(draws), dims[dim] // parts).reshape((-1,) + (1,) * (len(dims) - dim - 1))

    loudness = one(*split[0])
    for cut in split[1:]:
        loudness = loudness * one(*cut)
    return loudness


def bell_draw(own_key, extent, deviation, most, pieces=(), held_as=jnp.bfloat16):
    array = jax.random.normal(own_key, extent, jnp.float32) * deviation
    if len(pieces) > 0:
        array = block_levels(own_key, extent, pieces, -0.22, 0.18) * array
    return jnp.clip(array, min=-most, max=most).astype(held_as)


def setup_inputs(seed: int = 0) -> dict:
    seeds = jax.random.split(jax.random.key(seed), 21)
    inputs = bell_draw(seeds[0], (IMAGES, Q, D), 1.0, 6.0, ((0, 8),))
    memory = bell_draw(seeds[1], (IMAGES, MEM, D), 1.0, 6.0, ((0, 8), (1, 4)))
    lengths = draw_lengths(jax.random.fold_in(seeds[20], 71), 0)
    self_query = bell_draw(seeds[3], (D, D), D ** -0.5, 0.21875, ((0, 8),))
    self_key = bell_draw(seeds[4], (D, D), D ** -0.5, 0.21875, ((0, 8),))
    self_value = bell_draw(seeds[5], (D, D), D ** -0.5, 0.21875, ((0, 8),))
    self_out = bell_draw(seeds[6], (D, D), (D // 10) ** -0.5, 0.625, ((0, 8),))
    cross_query = bell_draw(seeds[7], (D, D), D ** -0.5, 0.21875, ((0, 8),))
    cross_key = bell_draw(seeds[8], (D, D), D ** -0.5, 0.21875, ((0, 8),))
    cross_value = bell_draw(seeds[9], (D, D), D ** -0.5, 0.21875, ((0, 8),))
    cross_out = bell_draw(seeds[10], (D, D), (D // 24) ** -0.5, 1.0, ((0, 8),))
    expand_weight = bell_draw(seeds[11], (D, FF), D ** -0.5, 0.21875, ((0, 8),))
    contract_weight = bell_draw(seeds[12], (FF, D), FF ** -0.5, 0.109375, ((0, 8),))
    gain_one = jnp.clip(1.0 + 0.1 * jax.random.normal(seeds[13], (D,), jnp.float32), 0.5, 1.5)
    shift_one = bell_draw(seeds[14], (D,), 0.3, 1.5, (), jnp.float32)
    gain_two = jnp.clip(1.0 + 0.1 * jax.random.normal(seeds[15], (D,), jnp.float32), 0.5, 1.5)
    shift_two = bell_draw(seeds[16], (D,), 0.3, 1.5, (), jnp.float32)
    gain_three = jnp.clip(1.0 + 0.1 * jax.random.normal(seeds[17], (D,), jnp.float32), 0.5, 1.5)
    shift_three = bell_draw(seeds[18], (D,), 0.3, 1.5, (), jnp.float32)
    cotangent = bell_draw(seeds[19], (IMAGES, Q, D), 1.0, 6.0, ((0, 8),))
    return {"inputs": inputs, "memory": memory, "lengths": lengths, "self_query": self_query, "self_key": self_key, "self_value": self_value, "self_out": self_out, "cross_query": cross_query, "cross_key": cross_key, "cross_value": cross_value, "cross_out": cross_out, "expand_weight": expand_weight, "contract_weight": contract_weight, "gain_one": gain_one, "shift_one": shift_one, "gain_two": gain_two, "shift_two": shift_two, "gain_three": gain_three, "shift_three": shift_three, "cotangent": cotangent}


@jax.custom_vjp
def low(v):
    return lax.optimization_barrier(v.astype(jnp.bfloat16)).astype(jnp.float32)

@jax.custom_vjp
def low_back(v):
    return v

def low_keep(v):
    return (low(v), None)

def low_pass(kept, grad):
    return (grad,)

def back_keep(v):
    return (v, None)

def back_low(kept, grad):
    return (low(grad),)
low.defvjp(low_keep, low_pass)
low_back.defvjp(back_keep, back_low)
highest = lax.Precision.HIGHEST

def rounded(value):
    return low(low_back(value))

def dense(inputs, weight):
    return jnp.einsum('td,df->tf', inputs, weight, precision=highest)

def layer_norm(resid, gain, shift):
    center = resid - lax.optimization_barrier(jnp.mean(resid, axis=-1, keepdims=True))
    inverse = lax.rsqrt(lax.optimization_barrier(jnp.mean(center * center, axis=-1, keepdims=True)) + 1e-05)
    return center * inverse * gain + shift

def split_heads(values):
    return values.reshape(values.shape[0], H, HD).transpose(1, 0, 2)

def join_heads(values):
    return values.transpose(1, 0, 2).reshape(values.shape[1], H * HD)

def attend(query, keys, values, valid):
    scores = low_back(jnp.einsum('hqe,hke->hqk', query, keys, precision=highest) * 0.125)
    scores = jnp.where(valid[None, None, :], scores, -1e+30)
    top_score = lax.optimization_barrier(jnp.max(scores, axis=-1, keepdims=True))
    exponent = jnp.exp(scores - top_score)
    probs = exponent / lax.optimization_barrier(jnp.sum(exponent, axis=-1, keepdims=True))
    return jnp.einsum('hqk,hke->hqe', low(probs), values, precision=highest)

def layer(inputs, memory, length, params):
    self_query, self_key, self_value, self_out, cross_query, cross_key, cross_value, cross_out, expand_weight, contract_weight, gain_one, shift_one, gain_two, shift_two, gain_three, shift_three = params
    every_key = jnp.arange(inputs.shape[0]) >= 0
    query_heads = split_heads(rounded(dense(inputs, self_query)))
    key_heads = split_heads(rounded(dense(inputs, self_key)))
    value_heads = split_heads(rounded(dense(inputs, self_value)))
    self_attn = rounded(join_heads(attend(query_heads, key_heads, value_heads, every_key)))
    self_branch = low_back(dense(self_attn, self_out))
    first = layer_norm(inputs + self_branch, gain_one, shift_one)
    first_low = low(first)
    cross_q = split_heads(rounded(dense(first_low, cross_query)))
    cross_k = split_heads(rounded(dense(memory, cross_key)))
    cross_v = split_heads(rounded(dense(memory, cross_value)))
    valid = jnp.arange(memory.shape[0]) < length
    cross_attn = rounded(join_heads(attend(cross_q, cross_k, cross_v, valid)))
    cross_branch = low_back(dense(cross_attn, cross_out))
    second = layer_norm(first + cross_branch, gain_two, shift_two)
    second_low = low(second)
    pre_act = low_back(dense(second_low, expand_weight))
    activ = low(jax.nn.gelu(pre_act, approximate=True))
    ffn_branch = low_back(dense(activ, contract_weight))
    return layer_norm(second + ffn_branch, gain_three, shift_three)

def reference(inputs, memory, lengths, self_query, self_key, self_value, self_out, cross_query, cross_key, cross_value, cross_out, expand_weight, contract_weight, gain_one, shift_one, gain_two, shift_two, gain_three, shift_three, cotangent):
    matrices = (self_query, self_key, self_value, self_out, cross_query, cross_key, cross_value, cross_out, expand_weight, contract_weight)
    params = tuple((weight.astype(jnp.float32) for weight in matrices)) + (gain_one, shift_one, gain_two, shift_two, gain_three, shift_three)

    def one_image(carry, item):
        tokens, memory_rows, length, incoming = item

        def forward(tok_in, mem_in, weights):
            return layer(tok_in, mem_in, length, weights)
        result, pull = jax.vjp(forward, tokens, memory_rows, params)
        grad_tokens, grad_memory, grad_params = pull(incoming)
        carry = jax.tree.map(jnp.add, carry, grad_params)
        return (carry, (result, grad_tokens, grad_memory))
    zeros = jax.tree.map(jnp.zeros_like, params)
    sums, (results, token_grads, memory_grads) = lax.scan(one_image, zeros, (inputs.astype(jnp.float32), memory.astype(jnp.float32), lengths, cotangent.astype(jnp.float32)))
    return (results, token_grads, memory_grads, sums[0], sums[1], sums[2], sums[3], sums[4], sums[5], sums[6], sums[7], sums[8], sums[9], sums[10], sums[11], sums[12], sums[13], sums[14], sums[15])
```

```python
import jax
import jax.numpy as jnp
from jax import lax
from jax.sharding import PartitionSpec as P

H = 12
LOW = jnp.bfloat16
WIDE = jnp.float32


def mm(a, b, dims):
    return lax.dot_general(a, b, (dims, ((), ())), preferred_element_type=WIDE)


def project(values, weight):
    return mm(values, weight, ((1,), (0,)))


def back_project(grads, weight):
    return mm(grads, weight, ((1,), (1,)))


def weight_grad(left, right):
    return mm(left, right, ((0,), (0,)))


def heads_of(values, images):
    rows, width = values.shape
    return values.reshape(images, rows // images, H, width // H)


def norm_forward(resid, gain, shift):
    center = resid - jnp.mean(resid, axis=-1, keepdims=True)
    inverse = lax.rsqrt(jnp.mean(center * center, axis=-1, keepdims=True) + 1e-05)
    normed = center * inverse
    return (normed * gain + shift, normed, inverse)


def norm_backward(incoming, normed, inverse, gain):
    scaled = incoming * gain
    grad_in = inverse * (
        scaled
        - jnp.mean(scaled, axis=-1, keepdims=True)
        - normed * jnp.mean(scaled * normed, axis=-1, keepdims=True)
    )
    return (grad_in, jnp.sum(incoming * normed, axis=0), jnp.sum(incoming, axis=0))


def scores_of(query, keys):
    return jnp.einsum("bqhe,bkhe->bhqk", query, keys, preferred_element_type=WIDE) * 0.125


def mix(probs, values):
    return jnp.einsum("bhqk,bkhe->bqhe", probs, values, preferred_element_type=WIDE)


def mix_back(probs, grads):
    return jnp.einsum("bhqk,bqhe->bkhe", probs, grads, preferred_element_type=WIDE)


def attention_backward(probs, attn, grad_attn, query, keys, values):
    row = jnp.sum(grad_attn.astype(WIDE) * attn.astype(WIDE), axis=-1).transpose(0, 2, 1)[..., None]
    grad_probs = jnp.einsum("bqhe,bkhe->bhqk", grad_attn, values, preferred_element_type=WIDE)
    grad_scores = (probs * (grad_probs - row)).astype(LOW)
    grad_query = mix(grad_scores, keys) * 0.125
    grad_keys = mix_back(grad_scores, query) * 0.125
    grad_values = mix_back(probs.astype(LOW), grad_attn)
    return (grad_query, grad_keys, grad_values)


def gelu_tanh(values):
    return jax.nn.gelu(values, approximate=True)


def on_device(
    inputs,
    memory,
    lengths,
    self_query,
    self_key,
    self_value,
    self_out,
    cross_query,
    cross_key,
    cross_value,
    cross_out,
    expand_weight,
    contract_weight,
    gain_one,
    shift_one,
    gain_two,
    shift_two,
    gain_three,
    shift_three,
    cotangent,
):
    images, queries, width = inputs.shape
    mem_rows = memory.shape[1]
    rows = images * queries
    share = self_query.shape[0]
    parts = width // share
    squares = (self_query, self_key, self_value, self_out, cross_query, cross_key, cross_value, cross_out)
    packed = lax.all_gather(jnp.stack(squares), "dp", axis=1, tiled=True)
    expand_full = lax.all_gather(expand_weight, "dp", axis=0, tiled=True)
    contract_full = lax.all_gather(contract_weight, "dp", axis=0, tiled=True)
    (query_full, key_full, value_full, out_full, cquery_full, ckey_full, cvalue_full, cout_full) = packed
    tokens = inputs.reshape(rows, width)
    memory_flat = memory.reshape(images * mem_rows, width)
    incoming = cotangent.reshape(rows, width).astype(WIDE)

    def joined(values):
        return values.reshape(-1, width)

    query_heads = heads_of(project(tokens, query_full).astype(LOW), images)
    key_heads = heads_of(project(tokens, key_full).astype(LOW), images)
    value_heads = heads_of(project(tokens, value_full).astype(LOW), images)
    self_raw = scores_of(query_heads, key_heads)
    self_exp = jnp.exp(self_raw - jnp.max(self_raw, axis=-1, keepdims=True))
    self_probs = self_exp / jnp.sum(self_exp, axis=-1, keepdims=True)
    self_attn = joined(mix(self_probs.astype(LOW), value_heads)).astype(LOW)
    first, normed_one, inverse_one = norm_forward(
        tokens.astype(WIDE) + project(self_attn, out_full), gain_one, shift_one
    )
    first_low = first.astype(LOW)
    cross_q = heads_of(project(first_low, cquery_full).astype(LOW), images)
    cross_k = heads_of(project(memory_flat, ckey_full).astype(LOW), images)
    cross_v = heads_of(project(memory_flat, cvalue_full).astype(LOW), images)
    places = lax.axis_index("mem") * mem_rows + jnp.arange(mem_rows, dtype=jnp.int32)
    valid = (places[None, :] < lengths[:, None])[:, None, None, :]
    cross_raw = jnp.where(valid, scores_of(cross_q, cross_k), -1e30)
    top = lax.pmax(jnp.max(cross_raw, axis=-1, keepdims=True), "mem")
    cross_exp = jnp.where(valid, jnp.exp(cross_raw - top), 0.0)
    total = lax.psum(jnp.sum(cross_exp, axis=-1, keepdims=True), "mem")
    cross_probs = cross_exp / total
    cross_attn = lax.psum(joined(mix(cross_probs.astype(LOW), cross_v)).astype(LOW), "mem")
    second, normed_two, inverse_two = norm_forward(
        first + project(cross_attn, cout_full), gain_two, shift_two
    )
    second_low = second.astype(LOW)
    pre_act = project(second_low, expand_full)
    activ, gelu_pull = jax.vjp(gelu_tanh, pre_act)
    activ_low = activ.astype(LOW)
    result, normed_three, inverse_three = norm_forward(
        second + project(activ_low, contract_full), gain_three, shift_three
    )
    grad_three, gain_three_part, shift_three_part = norm_backward(
        incoming, normed_three, inverse_three, gain_three
    )
    grad_ffn = grad_three.astype(LOW)

    def scattered(part, axes="dp"):
        return lax.psum_scatter(part, axes, scatter_dimension=0, tiled=True).astype(WIDE)

    contract_grad = scattered(weight_grad(activ_low, grad_ffn).astype(LOW))
    grad_pre = gelu_pull(back_project(grad_ffn, contract_full))[0].astype(LOW)
    expand_grad = scattered(weight_grad(second_low, grad_pre).astype(LOW))
    grad_second = grad_three + back_project(grad_pre, expand_full)
    grad_two, gain_two_part, shift_two_part = norm_backward(
        grad_second, normed_two, inverse_two, gain_two
    )
    grad_cross = grad_two.astype(LOW)
    cout_part = weight_grad(cross_attn, grad_cross)
    grad_cattn = heads_of(back_project(grad_cross, cout_full).astype(LOW), images)
    part_cquery, grad_ckey, grad_cvalue = attention_backward(
        cross_probs, heads_of(cross_attn, images), grad_cattn, cross_q, cross_k, cross_v
    )
    grad_cquery = lax.psum(joined(part_cquery).astype(LOW), "mem")
    grad_ckey = joined(grad_ckey).astype(LOW)
    grad_cvalue = joined(grad_cvalue).astype(LOW)
    kv_grad = scattered(
        jnp.concatenate(
            [weight_grad(memory_flat, grad_ckey), weight_grad(memory_flat, grad_cvalue)], axis=1
        ).astype(LOW),
        ("dp", "mem"),
    )
    memory_grad = back_project(grad_ckey, ckey_full) + back_project(grad_cvalue, cvalue_full)
    cquery_part = weight_grad(first_low, grad_cquery)
    grad_first = grad_two + back_project(grad_cquery, cquery_full)
    grad_one, gain_one_part, shift_one_part = norm_backward(
        grad_first, normed_one, inverse_one, gain_one
    )
    grad_self = grad_one.astype(LOW)
    out_part = weight_grad(self_attn, grad_self)
    grad_sattn = heads_of(back_project(grad_self, out_full).astype(LOW), images)
    grad_query, grad_key, grad_value = (
        joined(grad).astype(LOW)
        for grad in attention_backward(
            self_probs, heads_of(self_attn, images), grad_sattn, query_heads, key_heads, value_heads
        )
    )
    input_grad = (
        grad_one
        + back_project(grad_query, query_full)
        + back_project(grad_key, key_full)
        + back_project(grad_value, value_full)
    )
    norm_parts = jnp.stack(
        [gain_one_part, shift_one_part, gain_two_part, shift_two_part, gain_three_part, shift_three_part], axis=1
    )
    rest = scattered(
        jnp.concatenate(
            [
                weight_grad(tokens, grad_query),
                weight_grad(tokens, grad_key),
                weight_grad(tokens, grad_value),
                out_part,
                cquery_part,
                cout_part,
                jnp.pad(norm_parts, ((0, 0), (0, 122))),
            ],
            axis=1,
        ).astype(LOW)
    )
    squares_grad = [rest[:, place * width : (place + 1) * width] for place in range(6)]
    norms_grad = [rest[:, 6 * width + place] for place in range(6)]
    return (
        result.reshape(inputs.shape),
        input_grad.reshape(inputs.shape),
        memory_grad.reshape(memory.shape),
        *squares_grad[:5],
        kv_grad[:, :width],
        kv_grad[:, width:],
        squares_grad[5],
        expand_grad,
        contract_grad,
        *norms_grad,
    )


def solution(mesh):
    rows = P("dp", None)
    image = P("dp", None, None)
    token = P("dp", "mem", None)
    both = P(("dp", "mem"), None)
    return jax.shard_map(
        on_device,
        mesh=mesh,
        in_specs=(image, token, P("dp"), *[rows] * 10, *[P()] * 6, image),
        out_specs=(image, image, token, *[rows] * 5, both, both, *[rows] * 3, *[P("dp")] * 6),
        check_vma=False,
    )
```

```python
import functools
import jax
import jax.numpy as jnp
from jax import lax
from jax.experimental import pallas as pl
from jax.experimental.pallas import tpu as pltpu
from jax.sharding import PartitionSpec as P

H = 12
LOW = jnp.bfloat16
WIDE = jnp.float32


def contract(a, b, dims):
    return lax.dot_general(a, b, (dims, ((), ())), preferred_element_type=WIDE)


def project(values, weight):
    return contract(values, weight, ((1,), (0,)))


def back_project(grads, weight):
    return contract(grads, weight, ((1,), (1,)))


def weight_grad(left, right):
    return contract(left, right, ((0,), (0,)))


def heads_of(values, images):
    rows, width = values.shape
    return values.reshape(images, rows // images, H, width // H)


def norm_forward(resid, gain, shift):
    center = resid - jnp.mean(resid, axis=-1, keepdims=True)
    inverse = lax.rsqrt(jnp.mean(center * center, axis=-1, keepdims=True) + 1e-05)
    normed = center * inverse
    return (normed * gain + shift, normed, inverse)


def norm_backward(incoming, normed, inverse, gain):
    scaled = incoming * gain
    grad_in = inverse * (
        scaled
        - jnp.mean(scaled, axis=-1, keepdims=True)
        - normed * jnp.mean(scaled * normed, axis=-1, keepdims=True)
    )
    return (grad_in, jnp.sum(incoming * normed, axis=0), jnp.sum(incoming, axis=0))


def scores_of(query, keys):
    return jnp.einsum("bqhe,bkhe->bhqk", query, keys, preferred_element_type=WIDE) * 0.125


def mix(probs, values):
    return jnp.einsum("bhqk,bkhe->bqhe", probs, values, preferred_element_type=WIDE)


def mix_back(probs, grads):
    return jnp.einsum("bhqk,bqhe->bkhe", probs, grads, preferred_element_type=WIDE)


def attention_backward(probs, attn, grad_attn, query, keys, values):
    row = jnp.sum(grad_attn.astype(WIDE) * attn.astype(WIDE), axis=-1).transpose(0, 2, 1)[..., None]
    grad_probs = jnp.einsum("bqhe,bkhe->bhqk", grad_attn, values, preferred_element_type=WIDE)
    grad_scores = (probs * (grad_probs - row)).astype(LOW)
    grad_query = mix(grad_scores, keys) * 0.125
    grad_keys = mix_back(grad_scores, query) * 0.125
    grad_values = mix_back(probs.astype(LOW), grad_attn)
    return (grad_query, grad_keys, grad_values)


def gelu_tanh(values):
    return jax.nn.gelu(values, approximate=True)


def on_device(
    inputs,
    memory,
    lengths,
    self_query,
    self_key,
    self_value,
    self_out,
    cross_query,
    cross_key,
    cross_value,
    cross_out,
    expand_weight,
    contract_weight,
    gain_one,
    shift_one,
    gain_two,
    shift_two,
    gain_three,
    shift_three,
    cotangent,
):
    images, queries, width = inputs.shape
    mem_rows = memory.shape[1]
    rows = images * queries
    share = self_query.shape[0]
    parts = width // share
    squares = (self_query, self_key, self_value, self_out, cross_query, cross_key, cross_value, cross_out)
    packed = lax.all_gather(jnp.stack(squares), "dp", axis=1, tiled=True)
    expand_full = lax.all_gather(expand_weight, "dp", axis=0, tiled=True)
    contract_full = lax.all_gather(contract_weight, "dp", axis=0, tiled=True)
    (query_full, key_full, value_full, out_full, cquery_full, ckey_full, cvalue_full, cout_full) = packed
    tokens = inputs.reshape(rows, width)
    memory_flat = memory.reshape(images * mem_rows, width)
    incoming = cotangent.reshape(rows, width).astype(WIDE)

    def joined(values):
        return values.reshape(-1, width)

    query_heads = heads_of(project(tokens, query_full).astype(LOW), images)
    key_heads = heads_of(project(tokens, key_full).astype(LOW), images)
    value_heads = heads_of(project(tokens, value_full).astype(LOW), images)
    self_raw = scores_of(query_heads, key_heads)
    self_exp = jnp.exp(self_raw - jnp.max(self_raw, axis=-1, keepdims=True))
    self_probs = self_exp / jnp.sum(self_exp, axis=-1, keepdims=True)
    self_attn = joined(mix(self_probs.astype(LOW), value_heads)).astype(LOW)
    first, normed_one, inverse_one = norm_forward(
        tokens.astype(WIDE) + project(self_attn, out_full), gain_one, shift_one
    )
    first_low = first.astype(LOW)
    cross_q = heads_of(project(first_low, cquery_full).astype(LOW), images)
    cross_k = heads_of(project(memory_flat, ckey_full).astype(LOW), images)
    cross_v = heads_of(project(memory_flat, cvalue_full).astype(LOW), images)
    places = lax.axis_index("mem") * mem_rows + jnp.arange(mem_rows, dtype=jnp.int32)
    valid = (places[None, :] < lengths[:, None])[:, None, None, :]
    cross_raw = jnp.where(valid, scores_of(cross_q, cross_k), -1e30)
    top = lax.pmax(jnp.max(cross_raw, axis=-1, keepdims=True), "mem")
    cross_exp = jnp.where(valid, jnp.exp(cross_raw - top), 0.0)
    total = lax.psum(jnp.sum(cross_exp, axis=-1, keepdims=True), "mem")
    cross_probs = cross_exp / total
    cross_attn = lax.psum(joined(mix(cross_probs.astype(LOW), cross_v)).astype(LOW), "mem")
    second, normed_two, inverse_two = norm_forward(
        first + project(cross_attn, cout_full), gain_two, shift_two
    )
    second_low = second.astype(LOW)
    pre_act = project(second_low, expand_full)
    activ, gelu_pull = jax.vjp(gelu_tanh, pre_act)
    activ_low = activ.astype(LOW)
    result, normed_three, inverse_three = norm_forward(
        second + project(activ_low, contract_full), gain_three, shift_three
    )
    grad_three, gain_three_part, shift_three_part = norm_backward(
        incoming, normed_three, inverse_three, gain_three
    )
    grad_ffn = grad_three.astype(LOW)

    def scattered(part, axes="dp"):
        return lax.psum_scatter(part, axes, scatter_dimension=0, tiled=True).astype(WIDE)

    contract_grad = scattered(weight_grad(activ_low, grad_ffn).astype(LOW))
    grad_pre = gelu_pull(back_project(grad_ffn, contract_full))[0].astype(LOW)
    expand_grad = scattered(weight_grad(second_low, grad_pre).astype(LOW))
    grad_second = grad_three + back_project(grad_pre, expand_full)
    grad_two, gain_two_part, shift_two_part = norm_backward(
        grad_second, normed_two, inverse_two, gain_two
    )
    grad_cross = grad_two.astype(LOW)
    cout_part = weight_grad(cross_attn, grad_cross)
    grad_cattn = heads_of(back_project(grad_cross, cout_full).astype(LOW), images)
    part_cquery, grad_ckey, grad_cvalue = attention_backward(
        cross_probs, heads_of(cross_attn, images), grad_cattn, cross_q, cross_k, cross_v
    )
    grad_cquery = lax.psum(joined(part_cquery).astype(LOW), "mem")
    grad_ckey = joined(grad_ckey).astype(LOW)
    grad_cvalue = joined(grad_cvalue).astype(LOW)
    kv_grad = scattered(
        jnp.concatenate(
            [weight_grad(memory_flat, grad_ckey), weight_grad(memory_flat, grad_cvalue)], axis=1
        ).astype(LOW),
        ("dp", "mem"),
    )
    memory_grad = back_project(grad_ckey, ckey_full) + back_project(grad_cvalue, cvalue_full)
    cquery_part = weight_grad(first_low, grad_cquery)
    grad_first = grad_two + back_project(grad_cquery, cquery_full)
    grad_one, gain_one_part, shift_one_part = norm_backward(
        grad_first, normed_one, inverse_one, gain_one
    )
    grad_self = grad_one.astype(LOW)
    out_part = weight_grad(self_attn, grad_self)
    grad_sattn = heads_of(back_project(grad_self, out_full).astype(LOW), images)
    grad_query, grad_key, grad_value = (
        joined(grad).astype(LOW)
        for grad in attention_backward(
            self_probs, heads_of(self_attn, images), grad_sattn, query_heads, key_heads, value_heads
        )
    )
    input_grad = (
        grad_one
        + back_project(grad_query, query_full)
        + back_project(grad_key, key_full)
        + back_project(grad_value, value_full)
    )
    norm_parts = jnp.stack(
        [gain_one_part, shift_one_part, gain_two_part, shift_two_part, gain_three_part, shift_three_part], axis=1
    )
    rest = scattered(
        jnp.concatenate(
            [
                weight_grad(tokens, grad_query),
                weight_grad(tokens, grad_key),
                weight_grad(tokens, grad_value),
                out_part,
                cquery_part,
                cout_part,
                jnp.pad(norm_parts, ((0, 0), (0, 122))),
            ],
            axis=1,
        ).astype(LOW)
    )
    squares_grad = [rest[:, place * width : (place + 1) * width] for place in range(6)]
    norms_grad = [rest[:, 6 * width + place] for place in range(6)]
    return (
        result.reshape(inputs.shape),
        input_grad.reshape(inputs.shape),
        memory_grad.reshape(memory.shape),
        *squares_grad[:5],
        kv_grad[:, :width],
        kv_grad[:, width:],
        squares_grad[5],
        expand_grad,
        contract_grad,
        *norms_grad,
    )


MESH = pl.DeviceIdType.MESH
ANY = pl.BlockSpec(memory_space=pl.ANY)
INNER = pl.BlockSpec(memory_space=pltpu.VMEM)
SCALAR = pl.BlockSpec(memory_space=pltpu.SMEM)
D = 768
FF = 3072
PAIRS = 6
QP = 112
PIECES = 16
SQ, SK, SV, SO, CK, CV, CQ, CO, EX, CT = 0, 1, 2, 3, 4, 5, 6, 7, 8, 12
WINDOW = 4
VMEM_BYTES = 60 * 2**20


def mm(a, b):
    return lax.dot_general(a, b, (((1,), (0,)), ((), ())), preferred_element_type=WIDE)


def mm_nt(a, b):
    return lax.dot_general(a, b, (((1,), (1,)), ((), ())), preferred_element_type=WIDE)


def mm_tn(a, b):
    return lax.dot_general(a, b, (((0,), (0,)), ((), ())), preferred_element_type=WIDE)


def low_lanes(shape):
    return lax.broadcasted_iota(jnp.int32, shape, 1) < 64


def two_heads(pair):
    lower = low_lanes(pair.shape)
    nought = jnp.zeros_like(pair)
    return jnp.concatenate([jnp.where(lower, pair, nought), jnp.where(lower, nought, pair)], axis=0)


def one_pair(both):
    rows = both.shape[0] // 2
    upper = both[rows:]
    return jnp.where(low_lanes(upper.shape), both[:rows], upper)


def places():
    d = lax.axis_index("dp")
    c = lax.rem(d, 2)
    x = lax.rem(d // 2, 2)
    y = d // 4
    other = d + 1 - 2 * c
    beside = d + 2 - 4 * x
    above = d + 4 - 8 * y
    across = beside + 4 - 8 * y
    return d, other, beside, above, across


def weight_row(piece, owner):
    if piece < CT:
        return pl.multiple_of(piece * D + owner * 96, 96)
    return pl.multiple_of(CT * D + owner * 384 + (piece - CT) * 96, 96)


class Gather:
    def __init__(self, shards, full, local, send, recv):
        self.shards, self.full = shards, full
        self.local, self.send, self.recv = local, send, recv
        self.d, self.other, self.beside, self.above, self.across = places()
        self.z = lax.axis_index("mem")
        self.sent = []
        self.done = 0
        self.landed = [False] * PIECES

    def at(self, piece, owner):
        return self.full.at[pl.ds(weight_row(piece, owner), 96)]

    def own(self, piece):
        if piece < EX:
            return self.shards[piece]
        if piece < CT:
            return self.shards[EX].at[:, pl.ds((piece - EX) * D, D)]
        return self.shards[EX + 1].at[pl.ds((piece - CT) * 96, 96)]

    def copy(self, src, piece, owner, kind, target):
        return pltpu.make_async_remote_copy(
            src,
            self.at(piece, owner),
            self.send.at[piece, kind],
            self.recv.at[piece, kind],
            device_id=(target, self.z),
            device_id_type=MESH,
        )

    def push(self, src, piece, owner, kind, target):
        one = self.copy(src, piece, owner, kind, target)
        one.start()
        self.sent.append(one)

    def arrived(self, piece, kind):
        self.copy(self.at(piece, self.d), piece, self.d, kind, self.other).wait_recv()

    def start(self, piece):
        if piece >= PIECES:
            return
        src = self.own(piece)
        pltpu.make_async_copy(src, self.at(piece, self.d), self.local.at[piece]).start()
        self.push(src, piece, self.d, 0, self.beside)
        self.push(src, piece, self.d, 1, self.above)
        self.push(src, piece, self.d, 3, self.other)

    def begin(self):
        for piece in range(WINDOW):
            self.start(piece)

    def finish(self, piece):
        self.arrived(piece, 2)
        self.push(self.at(piece, self.across), piece, self.across, 6, self.other)

    def step(self):
        piece = self.done
        if piece > PIECES:
            return
        self.done += 1
        if piece < PIECES:
            self.arrived(piece, 0)
            if piece % 2 == 0:
                self.push(self.at(piece, self.beside), piece, self.beside, 2, self.above)
            self.push(self.at(piece, self.beside), piece, self.beside, 4, self.other)
            self.arrived(piece, 1)
            if piece % 2 == 1:
                self.push(self.at(piece, self.above), piece, self.above, 2, self.beside)
            self.push(self.at(piece, self.above), piece, self.above, 5, self.other)
            self.start(piece + WINDOW)
        if piece >= 1:
            self.finish(piece - 1)

    def ready(self, piece):
        while self.done <= piece + 1:
            self.step()
        if self.landed[piece]:
            return
        self.landed[piece] = True
        pltpu.make_async_copy(self.own(piece), self.at(piece, self.d), self.local.at[piece]).wait()
        for kind in range(3, 7):
            self.arrived(piece, kind)

    def close(self):
        for one in self.sent:
            one.wait_send()


def greet(targets):
    barrier = pltpu.get_barrier_semaphore()
    for target in targets:
        pl.semaphore_signal(barrier, 1, device_id=target, device_id_type=MESH)
    pl.semaphore_wait(barrier, len(targets))


def norm_rows(resid, gain, shift):
    center = resid - jnp.mean(resid, axis=-1, keepdims=True)
    inverse = lax.rsqrt(jnp.mean(center * center, axis=-1, keepdims=True) + 1e-05)
    normed = center * inverse
    return normed * gain + shift, normed, inverse


def forward_kernel(images, queries, mem_rows, *refs):
    (tok, mem, lens, norms, *rest) = refs
    shards = rest[:10]
    (o_result, o_full, o_acts, o_ffn, o_us, o_inv, o_kv, o_pc, o_ps, o_wst) = rest[10:20]
    (
        full, acts, ffn, us, inv, kv, pc, ps, wst, wide, stats, osend, orecv, srecv, fst,
        local, send, recv, zsend, zrecv, keep,
    ) = rest[20:]
    rows = images * QP
    z = lax.axis_index("mem")
    d = lax.axis_index("dp")
    gather = Gather(shards, full, local, send, recv)
    others = [lax.rem(z + r, 4) for r in range(1, 4)]
    greet(
        [(gather.other, z), (gather.beside, z), (gather.above, z)] + [(d, other) for other in others]
    )
    gather.begin()
    kept = []

    def save(src, dst):
        one = pltpu.make_async_copy(src, dst, keep.at[len(kept)])
        one.start()
        kept.append(one)

    def weight(piece, tile):
        return full[pl.ds(piece * D, D), pl.ds(pl.multiple_of(tile * 256, 256), 256)]

    def cols(tile):
        return pl.ds(pl.multiple_of(tile * 256, 256), 256)

    def image(i):
        return pl.ds(pl.multiple_of(i * QP, QP), QP)

    def project_rows(src, piece, dst, scale):
        def body(tile, carry):
            out = mm(src[...], weight(piece, tile)).astype(LOW)
            if scale != 1.0:
                out = out * jnp.asarray(scale, LOW)
            acts[dst, :, cols(tile)] = out
            return carry

        lax.fori_loop(0, 3, body, 0)

    gather.ready(SQ)
    project_rows(tok, SQ, 0, 0.125)
    gather.ready(SK)
    project_rows(tok, SK, 1, 1.0)
    gather.ready(SV)
    project_rows(tok, SV, 2, 1.0)

    def self_image(i, carry):
        at = image(i)
        valid = lax.broadcasted_iota(jnp.int32, (2 * QP, QP), 1) < queries
        for hp in range(PAIRS):
            lanes = pl.ds(hp * 128, 128)
            scores = mm_nt(two_heads(acts[0, at, lanes]), acts[1, at, lanes])
            scores = jnp.where(valid, scores, -1e30)
            grown = jnp.exp(scores - jnp.max(scores, axis=-1, keepdims=True))
            probs = (grown / jnp.sum(grown, axis=-1, keepdims=True)).astype(LOW)
            ps[i, hp] = probs
            acts[3, at, lanes] = one_pair(mm(probs, acts[2, at, lanes])).astype(LOW)
        return carry

    lax.fori_loop(0, images, self_image, 0)
    gather.step()

    def memory_rows(piece, dst):
        def body(i, carry):
            at = pl.ds(pl.multiple_of(i * mem_rows, mem_rows), mem_rows)

            def inner(tile, carry):
                kv[dst, at, cols(tile)] = mm(mem[at, :], weight(piece, tile)).astype(LOW)
                return carry

            return lax.fori_loop(0, 3, inner, carry)

        lax.fori_loop(0, images, body, 0)

    def add_branch(src, piece, base):
        def body(tile, carry):
            wide[0, :, cols(tile)] = base(cols(tile)) + mm(acts[src], weight(piece, tile))
            return carry

        lax.fori_loop(0, 3, body, 0)

    def normalize(which, low_dst):
        def body(i, carry):
            at = image(i)
            gain, shift = norms[pl.ds(2 * which, 1), :], norms[pl.ds(2 * which + 1, 1), :]
            out, normed, inverse = norm_rows(wide[0, at, :], gain, shift)
            us[which, at, :] = normed
            lane = lax.broadcasted_iota(jnp.int32, (QP, 128), 1)
            inv[at, :] = jnp.where(lane == which, inverse, inv[at, :])
            wide[1, at, :] = out
            if low_dst is not None:
                acts[low_dst, at, :] = out.astype(LOW)
            return carry

        lax.fori_loop(0, images, body, 0)

    inv[...] = jnp.zeros_like(inv)
    gather.ready(SO)
    add_branch(3, SO, lambda at: tok[:, at].astype(WIDE))
    normalize(0, 4)
    gather.ready(CK)
    memory_rows(CK, 0)
    gather.ready(CV)
    memory_rows(CV, 1)
    save(kv, o_kv)
    save(ps, o_ps)
    gather.ready(CQ)
    project_rows(acts.at[4], CQ, 5, 0.125)

    def cross_image(i, carry):
        at = image(i)
        tokens = pl.ds(pl.multiple_of(i * mem_rows, mem_rows), mem_rows)
        place = z * mem_rows + lax.broadcasted_iota(jnp.int32, (2 * QP, mem_rows), 1)
        valid = place < lens[i]
        lane = lax.broadcasted_iota(jnp.int32, (QP, 128), 1)
        noted = jnp.zeros((QP, 128), WIDE)
        for hp in range(PAIRS):
            lanes = pl.ds(hp * 128, 128)
            scores = mm_nt(two_heads(acts[5, at, lanes]), kv[0, tokens, lanes])
            scores = jnp.where(valid, scores, -1e30)
            top = jnp.max(scores, axis=-1, keepdims=True)
            grown = jnp.where(valid, jnp.exp(scores - top), 0.0)
            total = jnp.sum(grown, axis=-1, keepdims=True)
            probs = grown.astype(LOW)
            pc[i, hp] = probs
            osend[i, :, lanes] = one_pair(mm(probs, kv[1, tokens, lanes])).astype(LOW)
            for half in range(2):
                head = 2 * hp + half
                part = pl.ds(half * QP, QP)
                span = slice(half * QP, half * QP + QP)
                noted = jnp.where(lane == head, top[span], noted)
                noted = jnp.where(lane == 64 + head, total[span], noted)
        stats[i] = noted
        return carry

    lax.fori_loop(0, images, cross_image, 0)
    pushed = []

    def pass_on(src, dst, kind, r):
        one = pltpu.make_async_remote_copy(
            src, dst, zsend.at[kind, r - 1], zrecv.at[kind, r - 1],
            device_id=(d, others[r - 1]), device_id_type=MESH,
        )
        one.start()
        pushed.append(one)

    def taken(ref, kind, r):
        pltpu.make_async_remote_copy(
            ref, ref, zsend.at[kind, r - 1], zrecv.at[kind, r - 1],
            device_id=(d, others[r - 1]), device_id_type=MESH,
        ).wait_recv()

    for r in range(1, 4):
        pass_on(osend.at[others[r - 1]], orecv.at[r - 1], 0, r)
        pass_on(stats.at[others[r - 1]], srecv.at[r - 1], 1, r)
    save(pc, o_pc)
    gather.ready(CO)
    for r in range(1, 4):
        taken(orecv.at[r - 1], 0, r)
        taken(srecv.at[r - 1], 1, r)
    noted = [stats[z], srecv[0], srecv[1], srecv[2]]
    top = functools.reduce(jnp.maximum, noted)
    scale = [jnp.exp(one - top) for one in noted]
    total = sum(s * pltpu.roll(one, 64, 1) for s, one in zip(scale, noted))
    shrink = 1.0 / total
    lane = lax.broadcasted_iota(jnp.int32, (QP, 128), 1)
    fst[z] = jnp.where(lane < 64, top, pltpu.roll(shrink, 64, 1))
    lower = low_lanes((QP, 128))
    mine = image(z)
    for hp in range(PAIRS):
        lanes = pl.ds(hp * 128, 128)
        joined = jnp.zeros((QP, 128), WIDE)
        for r in range(4):
            share = scale[r] * shrink
            spread = jnp.where(lower, share[:, 2 * hp : 2 * hp + 1], share[:, 2 * hp + 1 : 2 * hp + 2])
            part = osend[z, :, lanes] if r == 0 else orecv[r - 1, :, lanes]
            joined = joined + spread * part.astype(WIDE)
        acts[6, mine, lanes] = joined.astype(LOW)
    for r in range(1, 4):
        pass_on(acts.at[6, mine], acts.at[6, mine], 2, r)
        pass_on(fst.at[z], fst.at[z], 3, r)
    for r in range(1, 4):
        back = lax.rem(z + 4 - r, 4)
        taken(acts.at[6, image(back)], 2, r)
        taken(fst.at[back], 3, r)
    for i in range(images):
        final = fst[i]
        wst[i] = jnp.exp(stats[i] - final) * pltpu.roll(final, 64, 1)
    save(wst, o_wst)
    add_branch(6, CO, lambda at: wide[1, :, at])
    normalize(1, 7)
    save(acts, o_acts)

    def expand(block):
        def body(tile, carry):
            pre = mm(acts[7], full[pl.ds((EX + block) * D, D), cols(tile)])
            root = 0.7978845608028654
            square = pre * pre
            bend = jnp.tanh(root * (pre + 0.044715 * (pre * square)))
            half = 0.5 * (1.0 + bend)
            slope = half + (0.5 * root) * pre * (1.0 - bend * bend) * (1.0 + 0.134145 * square)
            at = pl.ds(pl.multiple_of(block * D + tile * 256, 256), 256)
            ffn[0, :, at] = (pre * half).astype(LOW)
            ffn[1, :, at] = slope.astype(LOW)
            return carry

        lax.fori_loop(0, 3, body, 0)

    for block in range(4):
        gather.ready(EX + block)
        expand(block)
    save(ffn, o_ffn)
    for block in range(4):
        gather.ready(CT + block)
    save(full, o_full)

    def contract(tile, carry):
        wide[0, :, cols(tile)] = wide[1, :, cols(tile)] + mm(
            ffn[0], full[pl.ds(CT * D, FF), cols(tile)]
        )
        return carry

    lax.fori_loop(0, 3, contract, 0)
    normalize(2, None)
    save(wide.at[1], o_result)
    save(us, o_us)
    save(inv, o_inv)
    for one in pushed:
        one.wait_send()
    gather.close()
    for one in kept:
        one.wait()


def forward(tok, mem, lens, norms, shards, images, queries, mem_rows):
    rows = images * QP
    shape = jax.ShapeDtypeStruct
    tokens = images * mem_rows
    outs = (
        shape((rows, D), WIDE),
        shape((PIECES * D, D), LOW),
        shape((8, rows, D), LOW),
        shape((2, rows, FF), LOW),
        shape((3, rows, D), WIDE),
        shape((rows, 128), WIDE),
        shape((2, tokens, D), LOW),
        shape((images, PAIRS, 2 * QP, mem_rows), LOW),
        shape((images, PAIRS, 2 * QP, QP), LOW),
        shape((images, QP, 128), WIDE),
    )
    dma = pltpu.SemaphoreType.DMA
    return pl.pallas_call(
        functools.partial(forward_kernel, images, queries, mem_rows),
        out_shape=outs,
        in_specs=[INNER, INNER, SCALAR, INNER] + [ANY] * 10,
        out_specs=[ANY] * len(outs),
        scratch_shapes=[
            *[pltpu.VMEM(one.shape, one.dtype) for one in outs[1:]],
            pltpu.VMEM((2, rows, D), WIDE),
            pltpu.VMEM((images, QP, 128), WIDE),
            pltpu.VMEM((images, QP, D), LOW),
            pltpu.VMEM((3, QP, D), LOW),
            pltpu.VMEM((3, QP, 128), WIDE),
            pltpu.VMEM((images, QP, 128), WIDE),
            dma((PIECES,)),
            dma((PIECES, 7)),
            dma((PIECES, 7)),
            dma((4, 3)),
            dma((4, 3)),
            dma((12,)),
        ],
        compiler_params=pltpu.CompilerParams(
            collective_id=0, has_side_effects=True, vmem_limit_bytes=VMEM_BYTES
        ),
        name="forward",
    )(tok, mem, lens, norms, *(shards[place] for place in (0, 1, 2, 3, 5, 6, 4, 7, 8, 9)))


def fused_on_device(
    inputs,
    memory,
    lengths,
    self_query,
    self_key,
    self_value,
    self_out,
    cross_query,
    cross_key,
    cross_value,
    cross_out,
    expand_weight,
    contract_weight,
    gain_one,
    shift_one,
    gain_two,
    shift_two,
    gain_three,
    shift_three,
    cotangent,
):
    images, queries, width = inputs.shape
    mem_rows = memory.shape[1]
    norms = jnp.stack([gain_one, shift_one, gain_two, shift_two, gain_three, shift_three, gain_one, gain_one])
    shards = (self_query, self_key, self_value, self_out, cross_query, cross_key, cross_value, cross_out, expand_weight, contract_weight)

    def padded(values):
        wider = jnp.pad(values, ((0, 0), (0, QP - queries), (0, 0)))
        return wider.reshape(images * QP, width)

    def cut(values):
        return values.reshape(images, QP, width)[:, :queries]

    tokens = padded(inputs)
    memory_flat = memory.reshape(images * mem_rows, width)
    result, full, acts, ffn, us, inv, kv, pc, ps, wst = forward(
        tokens, memory_flat, lengths, norms, shards, images, queries, mem_rows
    )
    incoming = padded(cotangent).astype(WIDE)
    square = [full[place * D : (place + 1) * D] for place in range(8)]
    expand_full = jnp.concatenate([full[(EX + j) * D : (EX + j + 1) * D] for j in range(4)], axis=1)
    contract_full = full[CT * D :]
    (sq, sk, sv, self_attn, first_low, cq, cross_attn, second_low) = [acts[place] for place in range(8)]
    cross_probs = pc.reshape(images, H, QP, mem_rows).astype(WIDE)
    cross_probs = cross_probs * wst[:, :, :H].transpose(0, 2, 1)[..., None]
    self_probs = ps.reshape(images, H, QP, QP).astype(WIDE)

    def scattered(part, axes="dp"):
        return lax.psum_scatter(part, axes, scatter_dimension=0, tiled=True).astype(WIDE)

    def joined(values):
        return values.reshape(-1, width)

    def heads(values):
        return heads_of(values, images)

    grad_three, gain_three_part, shift_three_part = norm_backward(incoming, us[2], inv[:, 2:3], gain_three)
    grad_ffn = grad_three.astype(LOW)
    contract_grad = scattered(weight_grad(ffn[0], grad_ffn).astype(LOW))
    grad_pre = (ffn[1].astype(WIDE) * back_project(grad_ffn, contract_full)).astype(LOW)
    expand_grad = scattered(weight_grad(second_low, grad_pre).astype(LOW))
    grad_second = grad_three + back_project(grad_pre, expand_full)
    grad_two, gain_two_part, shift_two_part = norm_backward(grad_second, us[1], inv[:, 1:2], gain_two)
    grad_cross = grad_two.astype(LOW)
    cout_part = weight_grad(cross_attn, grad_cross)
    grad_cattn = heads(back_project(grad_cross, square[CO]).astype(LOW))
    cross_k, cross_v = heads(kv[0]), heads(kv[1])
    part_cquery, grad_ckey, grad_cvalue = attention_backward(
        cross_probs, heads(cross_attn), grad_cattn, heads(cq), cross_k, cross_v
    )
    grad_cquery = lax.psum(joined(part_cquery).astype(LOW), "mem")
    grad_ckey = joined(grad_ckey * 8.0).astype(LOW)
    grad_cvalue = joined(grad_cvalue).astype(LOW)
    kv_grad = scattered(
        jnp.concatenate(
            [weight_grad(memory_flat, grad_ckey), weight_grad(memory_flat, grad_cvalue)], axis=1
        ).astype(LOW),
        ("dp", "mem"),
    )
    memory_grad = back_project(grad_ckey, square[CK]) + back_project(grad_cvalue, square[CV])
    cquery_part = weight_grad(first_low, grad_cquery)
    grad_first = grad_two + back_project(grad_cquery, square[CQ])
    grad_one, gain_one_part, shift_one_part = norm_backward(grad_first, us[0], inv[:, 0:1], gain_one)
    grad_self = grad_one.astype(LOW)
    out_part = weight_grad(self_attn, grad_self)
    grad_sattn = heads(back_project(grad_self, square[SO]).astype(LOW))
    grad_query, grad_key, grad_value = attention_backward(
        self_probs, heads(self_attn), grad_sattn, heads(sq), heads(sk), heads(sv)
    )
    grad_query, grad_key, grad_value = (
        joined(grad).astype(LOW) for grad in (grad_query, grad_key * 8.0, grad_value)
    )
    input_grad = (
        grad_one
        + back_project(grad_query, square[SQ])
        + back_project(grad_key, square[SK])
        + back_project(grad_value, square[SV])
    )
    norm_parts = jnp.stack(
        [gain_one_part, shift_one_part, gain_two_part, shift_two_part, gain_three_part, shift_three_part], axis=1
    )
    rest = scattered(
        jnp.concatenate(
            [
                weight_grad(tokens, grad_query),
                weight_grad(tokens, grad_key),
                weight_grad(tokens, grad_value),
                out_part,
                cquery_part,
                cout_part,
                jnp.pad(norm_parts, ((0, 0), (0, 122))),
            ],
            axis=1,
        ).astype(LOW)
    )
    squares_grad = [rest[:, place * width : (place + 1) * width] for place in range(6)]
    norms_grad = [rest[:, 6 * width + place] for place in range(6)]
    return (
        cut(result),
        cut(input_grad),
        memory_grad.reshape(memory.shape),
        *squares_grad[:5],
        kv_grad[:, :width],
        kv_grad[:, width:],
        squares_grad[5],
        expand_grad,
        contract_grad,
        *norms_grad,
    )


def solution(mesh):
    fused = mesh.shape["dp"] == 8 and mesh.shape["mem"] == 4

    rows = P("dp", None)
    image = P("dp", None, None)
    token = P("dp", "mem", None)
    both = P(("dp", "mem"), None)
    return jax.shard_map(
        fused_on_device if fused else on_device,
        mesh=mesh,
        in_specs=(image, token, P("dp"), *[rows] * 10, *[P()] * 6, image),
        out_specs=(image, image, token, *[rows] * 5, both, both, *[rows] * 3, *[P("dp")] * 6),
        check_vma=False,
    )
```

```python
import functools
import jax
import jax.numpy as jnp
from jax import lax
from jax.experimental import pallas as pl
from jax.experimental.pallas import tpu as pltpu
from jax.sharding import PartitionSpec as P

H = 12
LOW = jnp.bfloat16
WIDE = jnp.float32


def contract(a, b, dims):
    return lax.dot_general(a, b, (dims, ((), ())), preferred_element_type=WIDE)


def project(values, weight):
    return contract(values, weight, ((1,), (0,)))


def back_project(grads, weight):
    return contract(grads, weight, ((1,), (1,)))


def weight_grad(left, right):
    return contract(left, right, ((0,), (0,)))


def heads_of(values, images):
    rows, width = values.shape
    return values.reshape(images, rows // images, H, width // H)


def norm_forward(resid, gain, shift):
    center = resid - jnp.mean(resid, axis=-1, keepdims=True)
    inverse = lax.rsqrt(jnp.mean(center * center, axis=-1, keepdims=True) + 1e-05)
    normed = center * inverse
    return (normed * gain + shift, normed, inverse)


def norm_backward(incoming, normed, inverse, gain):
    scaled = incoming * gain
    grad_in = inverse * (
        scaled
        - jnp.mean(scaled, axis=-1, keepdims=True)
        - normed * jnp.mean(scaled * normed, axis=-1, keepdims=True)
    )
    return (grad_in, jnp.sum(incoming * normed, axis=0), jnp.sum(incoming, axis=0))


def scores_of(query, keys):
    return jnp.einsum("bqhe,bkhe->bhqk", query, keys, preferred_element_type=WIDE) * 0.125


def mix(probs, values):
    return jnp.einsum("bhqk,bkhe->bqhe", probs, values, preferred_element_type=WIDE)


def mix_back(probs, grads):
    return jnp.einsum("bhqk,bqhe->bkhe", probs, grads, preferred_element_type=WIDE)


def attention_backward(probs, attn, grad_attn, query, keys, values):
    row = jnp.sum(grad_attn.astype(WIDE) * attn.astype(WIDE), axis=-1).transpose(0, 2, 1)[..., None]
    grad_probs = jnp.einsum("bqhe,bkhe->bhqk", grad_attn, values, preferred_element_type=WIDE)
    grad_scores = (probs * (grad_probs - row)).astype(LOW)
    grad_query = mix(grad_scores, keys) * 0.125
    grad_keys = mix_back(grad_scores, query) * 0.125
    grad_values = mix_back(probs.astype(LOW), grad_attn)
    return (grad_query, grad_keys, grad_values)


def gelu_tanh(values):
    return jax.nn.gelu(values, approximate=True)


def on_device(
    inputs,
    memory,
    lengths,
    self_query,
    self_key,
    self_value,
    self_out,
    cross_query,
    cross_key,
    cross_value,
    cross_out,
    expand_weight,
    contract_weight,
    gain_one,
    shift_one,
    gain_two,
    shift_two,
    gain_three,
    shift_three,
    cotangent,
):
    images, queries, width = inputs.shape
    mem_rows = memory.shape[1]
    rows = images * queries
    share = self_query.shape[0]
    parts = width // share
    squares = (self_query, self_key, self_value, self_out, cross_query, cross_key, cross_value, cross_out)
    packed = lax.all_gather(jnp.stack(squares), "dp", axis=1, tiled=True)
    expand_full = lax.all_gather(expand_weight, "dp", axis=0, tiled=True)
    contract_full = lax.all_gather(contract_weight, "dp", axis=0, tiled=True)
    (query_full, key_full, value_full, out_full, cquery_full, ckey_full, cvalue_full, cout_full) = packed
    tokens = inputs.reshape(rows, width)
    memory_flat = memory.reshape(images * mem_rows, width)
    incoming = cotangent.reshape(rows, width).astype(WIDE)

    def joined(values):
        return values.reshape(-1, width)

    query_heads = heads_of(project(tokens, query_full).astype(LOW), images)
    key_heads = heads_of(project(tokens, key_full).astype(LOW), images)
    value_heads = heads_of(project(tokens, value_full).astype(LOW), images)
    self_raw = scores_of(query_heads, key_heads)
    self_exp = jnp.exp(self_raw - jnp.max(self_raw, axis=-1, keepdims=True))
    self_probs = self_exp / jnp.sum(self_exp, axis=-1, keepdims=True)
    self_attn = joined(mix(self_probs.astype(LOW), value_heads)).astype(LOW)
    first, normed_one, inverse_one = norm_forward(
        tokens.astype(WIDE) + project(self_attn, out_full), gain_one, shift_one
    )
    first_low = first.astype(LOW)
    cross_q = heads_of(project(first_low, cquery_full).astype(LOW), images)
    cross_k = heads_of(project(memory_flat, ckey_full).astype(LOW), images)
    cross_v = heads_of(project(memory_flat, cvalue_full).astype(LOW), images)
    places = lax.axis_index("mem") * mem_rows + jnp.arange(mem_rows, dtype=jnp.int32)
    valid = (places[None, :] < lengths[:, None])[:, None, None, :]
    cross_raw = jnp.where(valid, scores_of(cross_q, cross_k), -1e30)
    top = lax.pmax(jnp.max(cross_raw, axis=-1, keepdims=True), "mem")
    cross_exp = jnp.where(valid, jnp.exp(cross_raw - top), 0.0)
    total = lax.psum(jnp.sum(cross_exp, axis=-1, keepdims=True), "mem")
    cross_probs = cross_exp / total
    cross_attn = lax.psum(joined(mix(cross_probs.astype(LOW), cross_v)).astype(LOW), "mem")
    second, normed_two, inverse_two = norm_forward(
        first + project(cross_attn, cout_full), gain_two, shift_two
    )
    second_low = second.astype(LOW)
    pre_act = project(second_low, expand_full)
    activ, gelu_pull = jax.vjp(gelu_tanh, pre_act)
    activ_low = activ.astype(LOW)
    result, normed_three, inverse_three = norm_forward(
        second + project(activ_low, contract_full), gain_three, shift_three
    )
    grad_three, gain_three_part, shift_three_part = norm_backward(
        incoming, normed_three, inverse_three, gain_three
    )
    grad_ffn = grad_three.astype(LOW)

    def scattered(part, axes="dp"):
        return lax.psum_scatter(part, axes, scatter_dimension=0, tiled=True).astype(WIDE)

    contract_grad = scattered(weight_grad(activ_low, grad_ffn).astype(LOW))
    grad_pre = gelu_pull(back_project(grad_ffn, contract_full))[0].astype(LOW)
    expand_grad = scattered(weight_grad(second_low, grad_pre).astype(LOW))
    grad_second = grad_three + back_project(grad_pre, expand_full)
    grad_two, gain_two_part, shift_two_part = norm_backward(
        grad_second, normed_two, inverse_two, gain_two
    )
    grad_cross = grad_two.astype(LOW)
    cout_part = weight_grad(cross_attn, grad_cross)
    grad_cattn = heads_of(back_project(grad_cross, cout_full).astype(LOW), images)
    part_cquery, grad_ckey, grad_cvalue = attention_backward(
        cross_probs, heads_of(cross_attn, images), grad_cattn, cross_q, cross_k, cross_v
    )
    grad_cquery = lax.psum(joined(part_cquery).astype(LOW), "mem")
    grad_ckey = joined(grad_ckey).astype(LOW)
    grad_cvalue = joined(grad_cvalue).astype(LOW)
    kv_grad = scattered(
        jnp.concatenate(
            [weight_grad(memory_flat, grad_ckey), weight_grad(memory_flat, grad_cvalue)], axis=1
        ).astype(LOW),
        ("dp", "mem"),
    )
    memory_grad = back_project(grad_ckey, ckey_full) + back_project(grad_cvalue, cvalue_full)
    cquery_part = weight_grad(first_low, grad_cquery)
    grad_first = grad_two + back_project(grad_cquery, cquery_full)
    grad_one, gain_one_part, shift_one_part = norm_backward(
        grad_first, normed_one, inverse_one, gain_one
    )
    grad_self = grad_one.astype(LOW)
    out_part = weight_grad(self_attn, grad_self)
    grad_sattn = heads_of(back_project(grad_self, out_full).astype(LOW), images)
    grad_query, grad_key, grad_value = (
        joined(grad).astype(LOW)
        for grad in attention_backward(
            self_probs, heads_of(self_attn, images), grad_sattn, query_heads, key_heads, value_heads
        )
    )
    input_grad = (
        grad_one
        + back_project(grad_query, query_full)
        + back_project(grad_key, key_full)
        + back_project(grad_value, value_full)
    )
    norm_parts = jnp.stack(
        [gain_one_part, shift_one_part, gain_two_part, shift_two_part, gain_three_part, shift_three_part], axis=1
    )
    rest = scattered(
        jnp.concatenate(
            [
                weight_grad(tokens, grad_query),
                weight_grad(tokens, grad_key),
                weight_grad(tokens, grad_value),
                out_part,
                cquery_part,
                cout_part,
                jnp.pad(norm_parts, ((0, 0), (0, 122))),
            ],
            axis=1,
        ).astype(LOW)
    )
    squares_grad = [rest[:, place * width : (place + 1) * width] for place in range(6)]
    norms_grad = [rest[:, 6 * width + place] for place in range(6)]
    return (
        result.reshape(inputs.shape),
        input_grad.reshape(inputs.shape),
        memory_grad.reshape(memory.shape),
        *squares_grad[:5],
        kv_grad[:, :width],
        kv_grad[:, width:],
        squares_grad[5],
        expand_grad,
        contract_grad,
        *norms_grad,
    )


MESH = pl.DeviceIdType.MESH
ANY = pl.BlockSpec(memory_space=pl.ANY)
INNER = pl.BlockSpec(memory_space=pltpu.VMEM)
SCALAR = pl.BlockSpec(memory_space=pltpu.SMEM)
D = 768
FF = 3072
PAIRS = 6
QP = 112
PIECES = 16
SQ, SK, SV, SO, CK, CV, CQ, CO, EX, CT = 0, 1, 2, 3, 4, 5, 6, 7, 8, 12
WINDOW = 4
VMEM_BYTES = 60 * 2**20


def mm(a, b):
    return lax.dot_general(a, b, (((1,), (0,)), ((), ())), preferred_element_type=WIDE)


def mm_nt(a, b):
    return lax.dot_general(a, b, (((1,), (1,)), ((), ())), preferred_element_type=WIDE)


def mm_tn(a, b):
    return lax.dot_general(a, b, (((0,), (0,)), ((), ())), preferred_element_type=WIDE)


def low_lanes(shape):
    return lax.broadcasted_iota(jnp.int32, shape, 1) < 64


def two_heads(pair):
    lower = low_lanes(pair.shape)
    nought = jnp.zeros_like(pair)
    return jnp.concatenate([jnp.where(lower, pair, nought), jnp.where(lower, nought, pair)], axis=0)


def one_pair(both):
    rows = both.shape[0] // 2
    upper = both[rows:]
    return jnp.where(low_lanes(upper.shape), both[:rows], upper)


def places():
    d = lax.axis_index("dp")
    c = lax.rem(d, 2)
    x = lax.rem(d // 2, 2)
    y = d // 4
    other = d + 1 - 2 * c
    beside = d + 2 - 4 * x
    above = d + 4 - 8 * y
    across = beside + 4 - 8 * y
    return d, other, beside, above, across


def weight_row(piece, owner):
    if piece < CT:
        return pl.multiple_of(piece * D + owner * 96, 96)
    return pl.multiple_of(CT * D + owner * 384 + (piece - CT) * 96, 96)


class Gather:
    def __init__(self, shards, full, local, send, recv):
        self.shards, self.full = shards, full
        self.local, self.send, self.recv = local, send, recv
        self.d, self.other, self.beside, self.above, self.across = places()
        self.z = lax.axis_index("mem")
        self.sent = []
        self.done = 0
        self.landed = [False] * PIECES

    def at(self, piece, owner):
        return self.full.at[pl.ds(weight_row(piece, owner), 96)]

    def own(self, piece):
        if piece < EX:
            return self.shards[piece]
        if piece < CT:
            return self.shards[EX].at[:, pl.ds((piece - EX) * D, D)]
        return self.shards[EX + 1].at[pl.ds((piece - CT) * 96, 96)]

    def copy(self, src, piece, owner, kind, target):
        return pltpu.make_async_remote_copy(
            src,
            self.at(piece, owner),
            self.send.at[piece, kind],
            self.recv.at[piece, kind],
            device_id=(target, self.z),
            device_id_type=MESH,
        )

    def push(self, src, piece, owner, kind, target):
        one = self.copy(src, piece, owner, kind, target)
        one.start()
        self.sent.append(one)

    def arrived(self, piece, kind):
        self.copy(self.at(piece, self.d), piece, self.d, kind, self.other).wait_recv()

    def start(self, piece):
        if piece >= PIECES:
            return
        src = self.own(piece)
        pltpu.make_async_copy(src, self.at(piece, self.d), self.local.at[piece]).start()
        self.push(src, piece, self.d, 0, self.beside)
        self.push(src, piece, self.d, 1, self.above)
        self.push(src, piece, self.d, 3, self.other)

    def begin(self):
        for piece in range(WINDOW):
            self.start(piece)

    def finish(self, piece):
        self.arrived(piece, 2)
        self.push(self.at(piece, self.across), piece, self.across, 6, self.other)

    def step(self):
        piece = self.done
        if piece > PIECES:
            return
        self.done += 1
        if piece < PIECES:
            self.arrived(piece, 0)
            if piece % 2 == 0:
                self.push(self.at(piece, self.beside), piece, self.beside, 2, self.above)
            self.push(self.at(piece, self.beside), piece, self.beside, 4, self.other)
            self.arrived(piece, 1)
            if piece % 2 == 1:
                self.push(self.at(piece, self.above), piece, self.above, 2, self.beside)
            self.push(self.at(piece, self.above), piece, self.above, 5, self.other)
            self.start(piece + WINDOW)
        if piece >= 1:
            self.finish(piece - 1)

    def ready(self, piece):
        while self.done <= piece + 1:
            self.step()
        if self.landed[piece]:
            return
        self.landed[piece] = True
        pltpu.make_async_copy(self.own(piece), self.at(piece, self.d), self.local.at[piece]).wait()
        for kind in range(3, 7):
            self.arrived(piece, kind)

    def close(self):
        for one in self.sent:
            one.wait_send()


def greet(targets):
    barrier = pltpu.get_barrier_semaphore()
    for target in targets:
        pl.semaphore_signal(barrier, 1, device_id=target, device_id_type=MESH)
    pl.semaphore_wait(barrier, len(targets))


def norm_rows(resid, gain, shift):
    center = resid - jnp.mean(resid, axis=-1, keepdims=True)
    inverse = lax.rsqrt(jnp.mean(center * center, axis=-1, keepdims=True) + 1e-05)
    normed = center * inverse
    return normed * gain + shift, normed, inverse


def forward_kernel(images, queries, mem_rows, *refs):
    (tok, mem, lens, norms, *rest) = refs
    shards = rest[:10]
    (o_result, o_full, o_acts, o_ffn, o_us, o_inv, o_kv, o_pc, o_ps, o_wst) = rest[10:20]
    (
        full, acts, ffn, us, inv, kv, pc, ps, wst, wide, stats, osend, orecv, srecv, fst,
        local, send, recv, zsend, zrecv, keep,
    ) = rest[20:]
    rows = images * QP
    z = lax.axis_index("mem")
    d = lax.axis_index("dp")
    gather = Gather(shards, full, local, send, recv)
    others = [lax.rem(z + r, 4) for r in range(1, 4)]
    greet(
        [(gather.other, z), (gather.beside, z), (gather.above, z)] + [(d, other) for other in others]
    )
    gather.begin()
    kept = []

    def save(src, dst):
        one = pltpu.make_async_copy(src, dst, keep.at[len(kept)])
        one.start()
        kept.append(one)

    def weight(piece, tile):
        return full[pl.ds(piece * D, D), pl.ds(pl.multiple_of(tile * 256, 256), 256)]

    def cols(tile):
        return pl.ds(pl.multiple_of(tile * 256, 256), 256)

    def image(i):
        return pl.ds(pl.multiple_of(i * QP, QP), QP)

    def project_rows(src, piece, dst, scale):
        def body(tile, carry):
            out = mm(src[...], weight(piece, tile)).astype(LOW)
            if scale != 1.0:
                out = out * jnp.asarray(scale, LOW)
            acts[dst, :, cols(tile)] = out
            return carry

        lax.fori_loop(0, 3, body, 0)

    gather.ready(SQ)
    project_rows(tok, SQ, 0, 0.125)
    gather.ready(SK)
    project_rows(tok, SK, 1, 1.0)
    gather.ready(SV)
    project_rows(tok, SV, 2, 1.0)

    def self_image(i, carry):
        at = image(i)
        valid = lax.broadcasted_iota(jnp.int32, (2 * QP, QP), 1) < queries
        for hp in range(PAIRS):
            lanes = pl.ds(hp * 128, 128)
            scores = mm_nt(two_heads(acts[0, at, lanes]), acts[1, at, lanes])
            scores = jnp.where(valid, scores, -1e30)
            grown = jnp.exp(scores - jnp.max(scores, axis=-1, keepdims=True))
            probs = (grown / jnp.sum(grown, axis=-1, keepdims=True)).astype(LOW)
            ps[i, hp] = probs
            acts[3, at, lanes] = one_pair(mm(probs, acts[2, at, lanes])).astype(LOW)
        return carry

    lax.fori_loop(0, images, self_image, 0)
    gather.step()

    def memory_rows(piece, dst):
        def body(i, carry):
            at = pl.ds(pl.multiple_of(i * mem_rows, mem_rows), mem_rows)

            def inner(tile, carry):
                kv[dst, at, cols(tile)] = mm(mem[at, :], weight(piece, tile)).astype(LOW)
                return carry

            return lax.fori_loop(0, 3, inner, carry)

        lax.fori_loop(0, images, body, 0)

    def add_branch(src, piece, base):
        def body(tile, carry):
            wide[0, :, cols(tile)] = base(cols(tile)) + mm(acts[src], weight(piece, tile))
            return carry

        lax.fori_loop(0, 3, body, 0)

    def normalize(which, low_dst):
        def body(i, carry):
            at = image(i)
            gain, shift = norms[pl.ds(2 * which, 1), :], norms[pl.ds(2 * which + 1, 1), :]
            out, normed, inverse = norm_rows(wide[0, at, :], gain, shift)
            us[which, at, :] = normed
            lane = lax.broadcasted_iota(jnp.int32, (QP, 128), 1)
            inv[at, :] = jnp.where(lane == which, inverse, inv[at, :])
            wide[1, at, :] = out
            if low_dst is not None:
                acts[low_dst, at, :] = out.astype(LOW)
            return carry

        lax.fori_loop(0, images, body, 0)

    inv[...] = jnp.zeros_like(inv)
    gather.ready(SO)
    add_branch(3, SO, lambda at: tok[:, at].astype(WIDE))
    normalize(0, 4)
    gather.ready(CK)
    memory_rows(CK, 0)
    gather.ready(CV)
    memory_rows(CV, 1)
    save(kv, o_kv)
    save(ps, o_ps)
    gather.ready(CQ)
    project_rows(acts.at[4], CQ, 5, 0.125)

    def cross_image(i, carry):
        at = image(i)
        tokens = pl.ds(pl.multiple_of(i * mem_rows, mem_rows), mem_rows)
        place = z * mem_rows + lax.broadcasted_iota(jnp.int32, (2 * QP, mem_rows), 1)
        valid = place < lens[i]
        lane = lax.broadcasted_iota(jnp.int32, (QP, 128), 1)
        noted = jnp.zeros((QP, 128), WIDE)
        for hp in range(PAIRS):
            lanes = pl.ds(hp * 128, 128)
            scores = mm_nt(two_heads(acts[5, at, lanes]), kv[0, tokens, lanes])
            scores = jnp.where(valid, scores, -1e30)
            top = jnp.max(scores, axis=-1, keepdims=True)
            grown = jnp.where(valid, jnp.exp(scores - top), 0.0)
            total = jnp.sum(grown, axis=-1, keepdims=True)
            probs = grown.astype(LOW)
            pc[i, hp] = probs
            osend[i, :, lanes] = one_pair(mm(probs, kv[1, tokens, lanes])).astype(LOW)
            for half in range(2):
                head = 2 * hp + half
                part = pl.ds(half * QP, QP)
                span = slice(half * QP, half * QP + QP)
                noted = jnp.where(lane == head, top[span], noted)
                noted = jnp.where(lane == 64 + head, total[span], noted)
        stats[i] = noted
        return carry

    lax.fori_loop(0, images, cross_image, 0)
    pushed = []

    def pass_on(src, dst, kind, r):
        one = pltpu.make_async_remote_copy(
            src, dst, zsend.at[kind, r - 1], zrecv.at[kind, r - 1],
            device_id=(d, others[r - 1]), device_id_type=MESH,
        )
        one.start()
        pushed.append(one)

    def taken(ref, kind, r):
        pltpu.make_async_remote_copy(
            ref, ref, zsend.at[kind, r - 1], zrecv.at[kind, r - 1],
            device_id=(d, others[r - 1]), device_id_type=MESH,
        ).wait_recv()

    for r in range(1, 4):
        pass_on(osend.at[others[r - 1]], orecv.at[r - 1], 0, r)
        pass_on(stats.at[others[r - 1]], srecv.at[r - 1], 1, r)
    save(pc, o_pc)
    gather.ready(CO)
    for r in range(1, 4):
        taken(orecv.at[r - 1], 0, r)
        taken(srecv.at[r - 1], 1, r)
    noted = [stats[z], srecv[0], srecv[1], srecv[2]]
    top = functools.reduce(jnp.maximum, noted)
    scale = [jnp.exp(one - top) for one in noted]
    total = sum(s * pltpu.roll(one, 64, 1) for s, one in zip(scale, noted))
    shrink = 1.0 / total
    lane = lax.broadcasted_iota(jnp.int32, (QP, 128), 1)
    fst[z] = jnp.where(lane < 64, top, pltpu.roll(shrink, 64, 1))
    lower = low_lanes((QP, 128))
    mine = image(z)
    for hp in range(PAIRS):
        lanes = pl.ds(hp * 128, 128)
        joined = jnp.zeros((QP, 128), WIDE)
        for r in range(4):
            share = scale[r] * shrink
            spread = jnp.where(lower, share[:, 2 * hp : 2 * hp + 1], share[:, 2 * hp + 1 : 2 * hp + 2])
            part = osend[z, :, lanes] if r == 0 else orecv[r - 1, :, lanes]
            joined = joined + spread * part.astype(WIDE)
        acts[6, mine, lanes] = joined.astype(LOW)
    for r in range(1, 4):
        pass_on(acts.at[6, mine], acts.at[6, mine], 2, r)
        pass_on(fst.at[z], fst.at[z], 3, r)
    for r in range(1, 4):
        back = lax.rem(z + 4 - r, 4)
        taken(acts.at[6, image(back)], 2, r)
        taken(fst.at[back], 3, r)
    for i in range(images):
        final = fst[i]
        wst[i] = jnp.exp(stats[i] - final) * pltpu.roll(final, 64, 1)
    save(wst, o_wst)
    add_branch(6, CO, lambda at: wide[1, :, at])
    normalize(1, 7)
    save(acts, o_acts)

    def expand(block):
        def body(tile, carry):
            pre = mm(acts[7], full[pl.ds((EX + block) * D, D), cols(tile)])
            root = 0.7978845608028654
            square = pre * pre
            bend = jnp.tanh(root * (pre + 0.044715 * (pre * square)))
            half = 0.5 * (1.0 + bend)
            slope = half + (0.5 * root) * pre * (1.0 - bend * bend) * (1.0 + 0.134145 * square)
            at = pl.ds(pl.multiple_of(block * D + tile * 256, 256), 256)
            ffn[0, :, at] = (pre * half).astype(LOW)
            ffn[1, :, at] = slope.astype(LOW)
            return carry

        lax.fori_loop(0, 3, body, 0)

    for block in range(4):
        gather.ready(EX + block)
        expand(block)
    save(ffn, o_ffn)
    for block in range(4):
        gather.ready(CT + block)
    save(full, o_full)

    def contract(tile, carry):
        wide[0, :, cols(tile)] = wide[1, :, cols(tile)] + mm(
            ffn[0], full[pl.ds(CT * D, FF), cols(tile)]
        )
        return carry

    lax.fori_loop(0, 3, contract, 0)
    normalize(2, None)
    save(wide.at[1], o_result)
    save(us, o_us)
    save(inv, o_inv)
    for one in pushed:
        one.wait_send()
    gather.close()
    for one in kept:
        one.wait()


def forward(tok, mem, lens, norms, shards, images, queries, mem_rows):
    rows = images * QP
    shape = jax.ShapeDtypeStruct
    tokens = images * mem_rows
    outs = (
        shape((rows, D), WIDE),
        shape((PIECES * D, D), LOW),
        shape((8, rows, D), LOW),
        shape((2, rows, FF), LOW),
        shape((3, rows, D), WIDE),
        shape((rows, 128), WIDE),
        shape((2, tokens, D), LOW),
        shape((images, PAIRS, 2 * QP, mem_rows), LOW),
        shape((images, PAIRS, 2 * QP, QP), LOW),
        shape((images, QP, 128), WIDE),
    )
    dma = pltpu.SemaphoreType.DMA
    return pl.pallas_call(
        functools.partial(forward_kernel, images, queries, mem_rows),
        out_shape=outs,
        in_specs=[INNER, INNER, SCALAR, INNER] + [ANY] * 10,
        out_specs=[ANY] * len(outs),
        scratch_shapes=[
            *[pltpu.VMEM(one.shape, one.dtype) for one in outs[1:]],
            pltpu.VMEM((2, rows, D), WIDE),
            pltpu.VMEM((images, QP, 128), WIDE),
            pltpu.VMEM((images, QP, D), LOW),
            pltpu.VMEM((3, QP, D), LOW),
            pltpu.VMEM((3, QP, 128), WIDE),
            pltpu.VMEM((images, QP, 128), WIDE),
            dma((PIECES,)),
            dma((PIECES, 7)),
            dma((PIECES, 7)),
            dma((4, 3)),
            dma((4, 3)),
            dma((12,)),
        ],
        compiler_params=pltpu.CompilerParams(
            collective_id=0, has_side_effects=True, vmem_limit_bytes=VMEM_BYTES
        ),
        name="forward",
    )(tok, mem, lens, norms, *(shards[place] for place in (0, 1, 2, 3, 5, 6, 4, 7, 8, 9)))


def rows_of_image(i):
    return pl.ds(pl.multiple_of(i * QP, QP), QP)


def cols_of_tile(tile):
    return pl.ds(pl.multiple_of(tile * 256, 256), 256)


class Reduce:
    def __init__(self, where, turn, grad, core_in, chip_in, core_sems, chip_sems):
        self.where, self.turn = where, turn
        self.grad, self.core_in, self.chip_in = grad, core_in, chip_in
        self.core_sems, self.chip_sems = core_sems, chip_sems
        self.sent = []
        d, other, beside, above, across = where
        self.c = lax.rem(d, 2)
        self.z = lax.axis_index("mem")

    def copy(self, src, dst, sems, place, target):
        return pltpu.make_async_remote_copy(
            src, dst, sems.at[0, self.turn, place], sems.at[1, self.turn, place],
            device_id=(target, self.z), device_id_type=MESH,
        )

    def core_stage(self):
        one = self.copy(self.grad.at[1 - self.c], self.core_in, self.core_sems, 0, self.where[1])
        one.start()
        self.sent.append(one)

    def chip_stage(self):
        self.copy(self.core_in, self.core_in, self.core_sems, 0, self.where[1]).wait_recv()
        for chip in range(4):
            both = self.grad[self.c, chip].astype(WIDE) + self.core_in[chip].astype(WIDE)
            self.grad[self.c, chip] = both.astype(LOW)
        for place, target in enumerate(self.where[2:]):
            one = self.copy(
                self.grad.at[self.c, target // 2], self.chip_in.at[place], self.chip_sems, place, target
            )
            one.start()
            self.sent.append(one)

    def total(self):
        own = self.grad[self.c, self.where[0] // 2].astype(WIDE)
        for place, target in enumerate(self.where[2:]):
            self.copy(
                self.chip_in.at[place], self.chip_in.at[place], self.chip_sems, place, target
            ).wait_recv()
            own = own + self.chip_in[place].astype(WIDE)
        return own

    def settle(self):
        for one in self.sent:
            one.wait_send()
        self.sent = []


def backward_kernel(images, queries, mem_rows, *refs):
    (
        h_norms, h_cot, h_tok, h_mem, h_full, h_acts, h_ffn, h_us, h_inv, h_kv, h_pc, h_ps, h_wst,
    ) = refs[:13]
    (o_expand, o_contract, o_rest, o_keys, o_mem, o_in, o_norms) = refs[13:20]
    (
        norms, cot, tok, mem, slots, acts, ffn, us, inv, kv, pc, ps, wst, wide, grads, nsum, nin,
        zsend, zin, mout,
        g_expand, g_contract, g_rest, c_expand, c_contract, c_rest, c_keys,
        t_expand, t_contract, t_rest, t_keys, f_expand, f_contract, f_rest, k_out, k_in,
        load, slot_sems, pc_sems, mout_sems, core_sems, chip_sems, fin_sems, local_sems, ksems, zsems, nsems,
    ) = refs[20:]
    z = lax.axis_index("mem")
    d = lax.axis_index("dp")
    where = places()
    q = lax.rem(z, 2)
    zp = z + 1 - 2 * q
    others = [lax.rem(z + r, 4) for r in range(1, 4)]
    dpeers = [lax.rem(d + r, 8) for r in range(1, 8)]

    loads = {}
    waited = set()

    def fetch(name, src, dst):
        one = pltpu.make_async_copy(src, dst, load.at[len(loads)])
        one.start()
        loads[name] = one

    order = [CT, CT + 1, CT + 2, CT + 3, EX, EX + 1, EX + 2, EX + 3, CO, CK, CV, CQ, SO, SQ, SK, SV]
    depth = 4

    def slot_copy(turn):
        return pltpu.make_async_copy(
            h_full.at[pl.ds(order[turn] * D, D)], slots.at[turn % depth], slot_sems.at[turn % depth]
        )

    def prefetch(turn):
        if turn < len(order):
            slot_copy(turn).start()

    fetch("norms", h_norms, norms)
    fetch("cot", h_cot, cot)
    fetch("inv", h_inv, inv)
    fetch("u3", h_us.at[2], us.at[0])
    for turn in range(depth):
        prefetch(turn)
    fetch("gp", h_ffn.at[1], ffn.at[1])
    fetch("act", h_ffn.at[0], ffn.at[0])
    fetch("acts", h_acts, acts)
    fetch("u2", h_us.at[1], us.at[1])
    fetch("kv", h_kv, kv)
    fetch("wst", h_wst, wst)
    fetch("ps", h_ps, ps)
    fetch("mem", h_mem, mem)
    fetch("tok", h_tok, tok)

    def have(name):
        if name not in waited:
            waited.add(name)
            loads[name].wait()

    def pc_copy(turn):
        i = lax.rem(z + turn + 1, 4)
        return pltpu.make_async_copy(h_pc.at[i], pc.at[turn % 2], pc_sems.at[turn % 2])

    pc_copy(0).start()
    pc_copy(1).start()
    greet([(peer, z) for peer in dpeers] + [(d, other) for other in others])

    nsum[...] = jnp.zeros_like(nsum)

    def norm_back(which, incoming, slot, low_dst):
        def body(i, carry):
            at = rows_of_image(i)
            above = incoming(at)
            unit = us[slot, at, :]
            inverse = inv[at, which : which + 1]
            scaled = above * norms[2 * which : 2 * which + 1, :]
            first = jnp.mean(scaled, axis=-1, keepdims=True)
            second = jnp.mean(scaled * unit, axis=-1, keepdims=True)
            grad = inverse * (scaled - first - unit * second)
            wide[0, at, :] = grad
            grads[low_dst, at, :] = grad.astype(LOW)
            row = 2 * which
            nsum[row : row + 1, :] += jnp.sum(above * unit, axis=0, keepdims=True)
            nsum[row + 1 : row + 2, :] += jnp.sum(above, axis=0, keepdims=True)
            return carry

        lax.fori_loop(0, images, body, 0)

    turn_of = {piece: turn for turn, piece in enumerate(order)}

    def slot(piece):
        turn = turn_of[piece]
        slot_copy(turn).wait()
        return slots.at[turn % depth]

    def freed(piece):
        prefetch(turn_of[piece] + depth)

    for name in ("norms", "cot", "inv", "u3"):
        have(name)
    norm_back(2, lambda at: cot[at, :].astype(WIDE), 0, 0)
    fetch("u1", h_us.at[0], us.at[0])
    have("gp")
    for block in range(4):
        weight = slot(CT + block)

        def body(tile, carry):
            at = pl.ds(pl.multiple_of(block * D + tile * 256, 256), 256)
            back = mm_nt(grads[0], weight[cols_of_tile(tile), :])
            ffn[1, :, at] = (back * ffn[1, :, at].astype(WIDE)).astype(LOW)
            return carry

        lax.fori_loop(0, 3, body, 0)
        freed(CT + block)

    def reduce_at(place, grad, core_in, chip_in):
        return Reduce(where, place, grad, core_in, chip_in, core_sems, chip_sems)

    have("acts")
    r_expand = reduce_at(0, g_expand, c_expand, t_expand)

    def expand_part(tile, carry):
        at = pl.ds(pl.multiple_of(q * 1536 + tile * 256, 256), 256)
        out = mm_tn(acts[7], ffn[1, :, at]).astype(LOW)
        for e in range(8):
            g_expand[e % 2, e // 2, :, cols_of_tile(tile)] = out[96 * e : 96 * e + 96]
        return carry

    lax.fori_loop(0, 6, expand_part, 0)
    r_expand.core_stage()
    have("act")
    r_contract = reduce_at(1, g_contract, c_contract, t_contract)

    def contract_part(e, carry):
        at = pl.ds(pl.multiple_of(e * 384, 384), 384)
        half = pl.ds(pl.multiple_of(q * 384, 384), 384)
        g_contract[lax.rem(e, 2), e // 2] = mm_tn(ffn[0, :, at], grads[0, :, half]).astype(LOW)
        return carry

    lax.fori_loop(0, 8, contract_part, 0)
    r_contract.core_stage()
    r_expand.chip_stage()
    for block in range(4):
        weight = slot(EX + block)

        def body(tile, carry):
            at = cols_of_tile(tile)
            back = mm_nt(ffn[1, :, pl.ds(block * D, D)], weight[at, :])
            wide[0, :, at] = wide[0, :, at] + back
            return carry

        lax.fori_loop(0, 3, body, 0)
        freed(EX + block)
    r_contract.chip_stage()
    have("u2")
    norm_back(1, lambda at: wide[0, at, :], 1, 1)

    def through(src, piece, dst):
        weight = slot(piece)

        def body(tile, carry):
            grads[dst, :, cols_of_tile(tile)] = mm_nt(grads[src], weight[cols_of_tile(tile), :]).astype(LOW)
            return carry

        lax.fori_loop(0, 3, body, 0)
        freed(piece)

    through(1, CO, 0)
    have("kv")
    have("wst")
    pushed = []

    def across_mem(src, dst, kind, r):
        return pltpu.make_async_remote_copy(
            src, dst, zsems.at[0, kind, r - 1], zsems.at[1, kind, r - 1],
            device_id=(d, others[r - 1]), device_id_type=MESH,
        )

    for turn in range(4):
        i = lax.rem(z + turn + 1, 4)
        pc_copy(turn).wait()
        at = rows_of_image(i)
        tokens = pl.ds(pl.multiple_of(i * mem_rows, mem_rows), mem_rows)
        factors = wst[i]

        def pair(hp, carry):
            lanes = pl.ds(pl.multiple_of(hp * 128, 128), 128)
            query = two_heads(acts[5, at, lanes])
            above = two_heads(grads[0, at, lanes])
            attn = acts[6, at, lanes].astype(WIDE)
            row = jnp.sum(above.astype(WIDE) * jnp.concatenate([attn, attn], axis=0), axis=-1, keepdims=True)
            lane = lax.broadcasted_iota(jnp.int32, (QP, 128), 1)
            factor = jnp.concatenate(
                [
                    jnp.sum(jnp.where(lane == 2 * hp + half, factors, 0.0), axis=-1, keepdims=True)
                    for half in range(2)
                ],
                axis=0,
            )
            probs = pc[turn % 2, hp].astype(WIDE) * factor
            keys, values = kv[0, tokens, lanes], kv[1, tokens, lanes]
            inner = mm_nt(above, values)
            scores = (probs * (inner - row)).astype(LOW)
            zsend[turn, :, lanes] = (one_pair(mm(scores, keys)) * 0.125).astype(LOW)
            kv[0, tokens, lanes] = mm_tn(scores, query).astype(LOW)
            kv[1, tokens, lanes] = mm_tn(probs.astype(LOW), above).astype(LOW)
            return carry

        lax.fori_loop(0, PAIRS, pair, 0)
        if turn < 2:
            pc_copy(turn + 2).start()
        if turn < 3:
            one = across_mem(zsend.at[turn], zin.at[turn], 0, turn + 1)
            one.start()
            pushed.append(one)

    have("mem")
    r_expand.settle()
    r_keys = reduce_at(2, g_expand, c_keys, t_keys)
    for which in range(2):

        def key_part(tile, carry):
            out = mm_tn(mem[...], kv[which, :, cols_of_tile(tile)]).astype(LOW)
            at = pl.ds(pl.multiple_of(which * D + tile * 256, 256), 256)
            for e in range(8):
                g_expand[e % 2, e // 2, :, at] = out[96 * e : 96 * e + 96]
            return carry

        if which == 0:
            final_expand = r_expand.total()
            f_expand[...] = final_expand.astype(LOW)
        lax.fori_loop(0, 3, key_part, 0)
    r_keys.core_stage()
    for r in range(1, 4):
        across_mem(zin.at[r - 1], zin.at[r - 1], 0, r).wait_recv()
    mine = rows_of_image(z)
    grads[3, mine, :] = (
        zsend[3].astype(WIDE) + zin[0].astype(WIDE) + zin[1].astype(WIDE) + zin[2].astype(WIDE)
    ).astype(LOW)
    for r in range(1, 4):
        one = across_mem(grads.at[3, mine], grads.at[3, mine], 1, r)
        one.start()
        pushed.append(one)

    def finals(fin, out, place):
        pltpu.make_async_copy(fin, out, local_sems.at[place]).start()
        one = pltpu.make_async_remote_copy(
            fin, out, fin_sems.at[0, place], fin_sems.at[1, place], device_id=(d, zp), device_id_type=MESH
        )
        one.start()
        return one

    ended = []
    r_keys.chip_stage()
    key_weight, value_weight = slot(CK), slot(CV)
    for i in range(images):
        at = pl.ds(i * mem_rows, mem_rows)
        if i >= 2:
            pltpu.make_async_copy(mout.at[i % 2], o_mem.at[at], mout_sems.at[i % 2]).wait()

        def body(tile, carry):
            span = cols_of_tile(tile)
            mout[i % 2, :, span] = mm_nt(kv[0, at, :], key_weight[span, :]) + mm_nt(
                kv[1, at, :], value_weight[span, :]
            )
            return carry

        lax.fori_loop(0, 3, body, 0)
        pltpu.make_async_copy(mout.at[i % 2], o_mem.at[at], mout_sems.at[i % 2]).start()
    freed(CK)
    freed(CV)
    for r in range(1, 4):
        back = lax.rem(z + 4 - r, 4)
        across_mem(grads.at[3, rows_of_image(back)], grads.at[3, rows_of_image(back)], 1, r).wait_recv()
    ended.append(finals(f_expand, o_expand.at[q], 0))
    f_contract[...] = r_contract.total().astype(LOW)
    ended.append(finals(f_contract, o_contract.at[q], 1))

    def add_back(src, piece):
        weight = slot(piece)

        def body(tile, carry):
            span = cols_of_tile(tile)
            wide[0, :, span] = wide[0, :, span] + mm_nt(src(), weight[span, :])
            return carry

        lax.fori_loop(0, 3, body, 0)
        freed(piece)

    add_back(lambda: grads[3], CQ)
    have("u1")
    norm_back(0, lambda at: wide[0, at, :], 0, 2)
    for r in range(1, 8):
        one = pltpu.make_async_remote_copy(
            nsum, nin.at[r - 1], nsems.at[0, r - 1], nsems.at[1, r - 1],
            device_id=(dpeers[r - 1], z), device_id_type=MESH,
        )
        one.start()
        pushed.append(one)
    have("tok")

    def rest_part(turn, lefts, rights):
        reducer = reduce_at(3 + turn, g_rest.at[turn], c_rest.at[turn], t_rest.at[turn])

        def work(left, right):
            def body(tile, carry):
                out = mm_tn(left(), right(cols_of_tile(tile))).astype(LOW)
                for e in range(8):
                    g_rest[turn, e % 2, e // 2, :, cols_of_tile(tile)] = out[96 * e : 96 * e + 96]
                return carry

            lax.fori_loop(0, 3, body, 0)

        @pl.when(q == 0)
        def _():
            work(lefts[0], rights[0])

        @pl.when(q == 1)
        def _():
            work(lefts[1], rights[1])

        reducer.core_stage()
        return reducer

    r_first = rest_part(
        0,
        (lambda: acts[6], lambda: acts[4]),
        (lambda at: grads[1, :, at], lambda at: grads[3, :, at]),
    )
    through(2, SO, 0)
    have("ps")
    r_first.chip_stage()

    def self_image(i, carry):
        at = rows_of_image(i)
        for hp in range(PAIRS):
            lanes = pl.ds(hp * 128, 128)
            query = two_heads(acts[0, at, lanes])
            above = two_heads(grads[0, at, lanes])
            attn = acts[3, at, lanes].astype(WIDE)
            row = jnp.sum(above.astype(WIDE) * jnp.concatenate([attn, attn], axis=0), axis=-1, keepdims=True)
            probs = ps[i, hp]
            keys, values = acts[1, at, lanes], acts[2, at, lanes]
            inner = mm_nt(above, values)
            scores = (probs.astype(WIDE) * (inner - row)).astype(LOW)
            acts[0, at, lanes] = (one_pair(mm(scores, keys)) * 0.125).astype(LOW)
            acts[1, at, lanes] = mm_tn(scores, query).astype(LOW)
            acts[2, at, lanes] = mm_tn(probs, above).astype(LOW)
        return carry

    lax.fori_loop(0, images, self_image, 0)
    r_second = rest_part(
        1,
        (lambda: acts[3], lambda: tok[...]),
        (lambda at: grads[2, :, at], lambda at: acts[0, :, at]),
    )
    r_third = rest_part(
        2,
        (lambda: tok[...], lambda: tok[...]),
        (lambda at: acts[1, :, at], lambda at: acts[2, :, at]),
    )
    r_second.chip_stage()
    r_third.chip_stage()
    quarter = 24
    keys_total = r_keys.total()
    for part in range(4):
        k_out[part] = keys_total[quarter * part : quarter * part + quarter].astype(LOW)
    for r in range(1, 4):
        one = pltpu.make_async_remote_copy(
            k_out.at[others[r - 1]], k_in.at[r - 1], ksems.at[0, r - 1], ksems.at[1, r - 1],
            device_id=(d, others[r - 1]), device_id_type=MESH,
        )
        one.start()
        pushed.append(one)
    f_rest[0] = r_first.total().astype(LOW)
    ended.append(finals(f_rest.at[0], o_rest.at[0, q], 2))
    add_back(lambda: acts[0], SQ)
    add_back(lambda: acts[1], SK)
    add_back(lambda: acts[2], SV)
    pltpu.make_async_copy(wide.at[0], o_in, load.at[15]).start()
    f_rest[1] = r_second.total().astype(LOW)
    ended.append(finals(f_rest.at[1], o_rest.at[1, q], 3))
    f_rest[2] = r_third.total().astype(LOW)
    ended.append(finals(f_rest.at[2], o_rest.at[2, q], 4))
    sums = nsum[...]
    for r in range(1, 8):
        pltpu.make_async_remote_copy(
            nsum, nin.at[r - 1], nsems.at[0, r - 1], nsems.at[1, r - 1],
            device_id=(dpeers[r - 1], z), device_id_type=MESH,
        ).wait_recv()
        sums = sums + nin[r - 1]
    o_norms[...] = sums
    total = k_out[z].astype(WIDE)
    for r in range(1, 4):
        pltpu.make_async_remote_copy(
            k_in.at[r - 1], k_in.at[r - 1], ksems.at[0, r - 1], ksems.at[1, r - 1],
            device_id=(d, others[r - 1]), device_id_type=MESH,
        ).wait_recv()
        total = total + k_in[r - 1].astype(WIDE)
    o_keys[...] = total
    for i in range(2, 4):
        at = pl.ds(i * mem_rows, mem_rows)
        pltpu.make_async_copy(mout.at[i % 2], o_mem.at[at], mout_sems.at[i % 2]).wait()
    pltpu.make_async_copy(wide.at[0], o_in, load.at[15]).wait()
    fins = (f_expand, f_contract, f_rest.at[0], f_rest.at[1], f_rest.at[2])
    outs = (
        (o_expand.at[q], o_expand.at[1 - q]),
        (o_contract.at[q], o_contract.at[1 - q]),
        (o_rest.at[0, q], o_rest.at[0, 1 - q]),
        (o_rest.at[1, q], o_rest.at[1, 1 - q]),
        (o_rest.at[2, q], o_rest.at[2, 1 - q]),
    )
    for place, (fin, (out, theirs)) in enumerate(zip(fins, outs)):
        pltpu.make_async_copy(fin, out, local_sems.at[place]).wait()
        ended[place].wait_send()
        pltpu.make_async_remote_copy(
            fin, theirs, fin_sems.at[0, place], fin_sems.at[1, place], device_id=(d, zp), device_id_type=MESH
        ).wait_recv()
    for one in pushed:
        one.wait_send()
    for reducer in (r_contract, r_keys, r_first, r_second, r_third):
        reducer.settle()


def backward(norms, cot, tok, mem, saved, images, queries, mem_rows):
    full, acts, ffn, us, inv, kv, pc, ps, wst = saved
    rows = images * QP
    tokens = images * mem_rows
    shape = jax.ShapeDtypeStruct
    outs = (
        shape((2, 96, 1536), LOW),
        shape((2, 384, 384), LOW),
        shape((3, 2, 96, D), LOW),
        shape((24, 1536), WIDE),
        shape((tokens, D), WIDE),
        shape((rows, D), WIDE),
        shape((8, D), WIDE),
    )
    dma = pltpu.SemaphoreType.DMA
    vmem = pltpu.VMEM
    return pl.pallas_call(
        functools.partial(backward_kernel, images, queries, mem_rows),
        out_shape=outs,
        in_specs=[ANY] * 13,
        out_specs=[ANY] * 3 + [INNER] + [ANY] * 2 + [INNER],
        scratch_shapes=[
            vmem((8, D), WIDE),
            vmem((rows, D), LOW),
            vmem((rows, D), LOW),
            vmem((tokens, D), LOW),
            vmem((4, D, D), LOW),
            vmem((8, rows, D), LOW),
            vmem((2, rows, FF), LOW),
            vmem((2, rows, D), WIDE),
            vmem((rows, 128), WIDE),
            vmem((2, tokens, D), LOW),
            vmem((2, PAIRS, 2 * QP, mem_rows), LOW),
            vmem((images, PAIRS, 2 * QP, QP), LOW),
            vmem((images, QP, 128), WIDE),
            vmem((1, rows, D), WIDE),
            vmem((4, rows, D), LOW),
            vmem((8, D), WIDE),
            vmem((7, 8, D), WIDE),
            vmem((4, QP, D), LOW),
            vmem((3, QP, D), LOW),
            vmem((2, mem_rows, D), WIDE),
            vmem((2, 4, 96, 1536), LOW),
            vmem((2, 4, 384, 384), LOW),
            vmem((3, 2, 4, 96, D), LOW),
            vmem((4, 96, 1536), LOW),
            vmem((4, 384, 384), LOW),
            vmem((3, 4, 96, D), LOW),
            vmem((4, 96, 1536), LOW),
            vmem((3, 96, 1536), LOW),
            vmem((3, 384, 384), LOW),
            vmem((3, 3, 96, D), LOW),
            vmem((3, 96, 1536), LOW),
            vmem((96, 1536), LOW),
            vmem((384, 384), LOW),
            vmem((3, 96, D), LOW),
            vmem((4, 24, 1536), LOW),
            vmem((3, 24, 1536), LOW),
            dma((16,)),
            dma((4,)),
            dma((2,)),
            dma((2,)),
            dma((2, 6, 1)),
            dma((2, 6, 3)),
            dma((2, 5)),
            dma((5,)),
            dma((2, 3)),
            dma((2, 2, 3)),
            dma((2, 7)),
        ],
        compiler_params=pltpu.CompilerParams(
            collective_id=1, has_side_effects=True, vmem_limit_bytes=VMEM_BYTES
        ),
        name="backward",
    )(norms, cot, tok, mem, *saved)


def fused_on_device(
    inputs,
    memory,
    lengths,
    self_query,
    self_key,
    self_value,
    self_out,
    cross_query,
    cross_key,
    cross_value,
    cross_out,
    expand_weight,
    contract_weight,
    gain_one,
    shift_one,
    gain_two,
    shift_two,
    gain_three,
    shift_three,
    cotangent,
):
    images, queries, width = inputs.shape
    mem_rows = memory.shape[1]
    norms = jnp.stack([gain_one, shift_one, gain_two, shift_two, gain_three, shift_three, gain_one, gain_one])
    shards = (self_query, self_key, self_value, self_out, cross_query, cross_key, cross_value, cross_out, expand_weight, contract_weight)

    def padded(values):
        wider = jnp.pad(values, ((0, 0), (0, QP - queries), (0, 0)))
        return wider.reshape(images * QP, width)

    def cut(values):
        return values.reshape(images, QP, width)[:, :queries]

    tokens = padded(inputs)
    memory_flat = memory.reshape(images * mem_rows, width)
    result, full, acts, ffn, us, inv, kv, pc, ps, wst = forward(
        tokens, memory_flat, lengths, norms, shards, images, queries, mem_rows
    )
    spread, contracted, rest, keys, memory_grad, input_grad, sums = backward(
        norms, padded(cotangent), tokens, memory_flat, (full, acts, ffn, us, inv, kv, pc, ps, wst),
        images, queries, mem_rows,
    )
    share = self_query.shape[0]
    sums = lax.dynamic_slice(sums, (0, lax.axis_index("dp") * share), (8, share))
    rest = rest.astype(WIDE)
    return (
        cut(result),
        cut(input_grad),
        memory_grad.reshape(memory.shape),
        rest[1, 1],
        rest[2, 0],
        rest[2, 1],
        rest[1, 0],
        rest[0, 1],
        keys[:, :width],
        keys[:, width:],
        rest[0, 0],
        jnp.concatenate([spread[0], spread[1]], axis=1).astype(WIDE),
        jnp.concatenate([contracted[0], contracted[1]], axis=1).astype(WIDE),
        *[sums[place] for place in range(6)],
    )


def solution(mesh):
    fused = mesh.shape["dp"] == 8 and mesh.shape["mem"] == 4

    rows = P("dp", None)
    image = P("dp", None, None)
    token = P("dp", "mem", None)
    both = P(("dp", "mem"), None)
    return jax.shard_map(
        fused_on_device if fused else on_device,
        mesh=mesh,
        in_specs=(image, token, P("dp"), *[rows] * 10, *[P()] * 6, image),
        out_specs=(image, image, token, *[rows] * 5, both, both, *[rows] * 3, *[P("dp")] * 6),
        check_vma=False,
    )
```

```python
import functools
import jax
import jax.numpy as jnp
from jax import lax
from jax.experimental import pallas as pl
from jax.experimental.pallas import tpu as pltpu
from jax.sharding import PartitionSpec as P

H = 12
LOW = jnp.bfloat16
WIDE = jnp.float32


def contract(a, b, dims):
    return lax.dot_general(a, b, (dims, ((), ())), preferred_element_type=WIDE)


def project(values, weight):
    return contract(values, weight, ((1,), (0,)))


def back_project(grads, weight):
    return contract(grads, weight, ((1,), (1,)))


def weight_grad(left, right):
    return contract(left, right, ((0,), (0,)))


def heads_of(values, images):
    rows, width = values.shape
    return values.reshape(images, rows // images, H, width // H)


def norm_forward(resid, gain, shift):
    center = resid - jnp.mean(resid, axis=-1, keepdims=True)
    inverse = lax.rsqrt(jnp.mean(center * center, axis=-1, keepdims=True) + 1e-05)
    normed = center * inverse
    return (normed * gain + shift, normed, inverse)


def norm_backward(incoming, normed, inverse, gain):
    scaled = incoming * gain
    grad_in = inverse * (
        scaled
        - jnp.mean(scaled, axis=-1, keepdims=True)
        - normed * jnp.mean(scaled * normed, axis=-1, keepdims=True)
    )
    return (grad_in, jnp.sum(incoming * normed, axis=0), jnp.sum(incoming, axis=0))


def scores_of(query, keys):
    return jnp.einsum("bqhe,bkhe->bhqk", query, keys, preferred_element_type=WIDE) * 0.125


def mix(probs, values):
    return jnp.einsum("bhqk,bkhe->bqhe", probs, values, preferred_element_type=WIDE)


def mix_back(probs, grads):
    return jnp.einsum("bhqk,bqhe->bkhe", probs, grads, preferred_element_type=WIDE)


def attention_backward(probs, attn, grad_attn, query, keys, values):
    row = jnp.sum(grad_attn.astype(WIDE) * attn.astype(WIDE), axis=-1).transpose(0, 2, 1)[..., None]
    grad_probs = jnp.einsum("bqhe,bkhe->bhqk", grad_attn, values, preferred_element_type=WIDE)
    grad_scores = (probs * (grad_probs - row)).astype(LOW)
    grad_query = mix(grad_scores, keys) * 0.125
    grad_keys = mix_back(grad_scores, query) * 0.125
    grad_values = mix_back(probs.astype(LOW), grad_attn)
    return (grad_query, grad_keys, grad_values)


def gelu_tanh(values):
    return jax.nn.gelu(values, approximate=True)


def on_device(
    inputs,
    memory,
    lengths,
    self_query,
    self_key,
    self_value,
    self_out,
    cross_query,
    cross_key,
    cross_value,
    cross_out,
    expand_weight,
    contract_weight,
    gain_one,
    shift_one,
    gain_two,
    shift_two,
    gain_three,
    shift_three,
    cotangent,
):
    images, queries, width = inputs.shape
    mem_rows = memory.shape[1]
    rows = images * queries
    share = self_query.shape[0]
    parts = width // share
    squares = (self_query, self_key, self_value, self_out, cross_query, cross_key, cross_value, cross_out)
    packed = lax.all_gather(jnp.stack(squares), "dp", axis=1, tiled=True)
    expand_full = lax.all_gather(expand_weight, "dp", axis=0, tiled=True)
    contract_full = lax.all_gather(contract_weight, "dp", axis=0, tiled=True)
    (query_full, key_full, value_full, out_full, cquery_full, ckey_full, cvalue_full, cout_full) = packed
    tokens = inputs.reshape(rows, width)
    memory_flat = memory.reshape(images * mem_rows, width)
    incoming = cotangent.reshape(rows, width).astype(WIDE)

    def joined(values):
        return values.reshape(-1, width)

    query_heads = heads_of(project(tokens, query_full).astype(LOW), images)
    key_heads = heads_of(project(tokens, key_full).astype(LOW), images)
    value_heads = heads_of(project(tokens, value_full).astype(LOW), images)
    self_raw = scores_of(query_heads, key_heads)
    self_exp = jnp.exp(self_raw - jnp.max(self_raw, axis=-1, keepdims=True))
    self_probs = self_exp / jnp.sum(self_exp, axis=-1, keepdims=True)
    self_attn = joined(mix(self_probs.astype(LOW), value_heads)).astype(LOW)
    first, normed_one, inverse_one = norm_forward(
        tokens.astype(WIDE) + project(self_attn, out_full), gain_one, shift_one
    )
    first_low = first.astype(LOW)
    cross_q = heads_of(project(first_low, cquery_full).astype(LOW), images)
    cross_k = heads_of(project(memory_flat, ckey_full).astype(LOW), images)
    cross_v = heads_of(project(memory_flat, cvalue_full).astype(LOW), images)
    places = lax.axis_index("mem") * mem_rows + jnp.arange(mem_rows, dtype=jnp.int32)
    valid = (places[None, :] < lengths[:, None])[:, None, None, :]
    cross_raw = jnp.where(valid, scores_of(cross_q, cross_k), -1e30)
    top = lax.pmax(jnp.max(cross_raw, axis=-1, keepdims=True), "mem")
    cross_exp = jnp.where(valid, jnp.exp(cross_raw - top), 0.0)
    total = lax.psum(jnp.sum(cross_exp, axis=-1, keepdims=True), "mem")
    cross_probs = cross_exp / total
    cross_attn = lax.psum(joined(mix(cross_probs.astype(LOW), cross_v)).astype(LOW), "mem")
    second, normed_two, inverse_two = norm_forward(
        first + project(cross_attn, cout_full), gain_two, shift_two
    )
    second_low = second.astype(LOW)
    pre_act = project(second_low, expand_full)
    activ, gelu_pull = jax.vjp(gelu_tanh, pre_act)
    activ_low = activ.astype(LOW)
    result, normed_three, inverse_three = norm_forward(
        second + project(activ_low, contract_full), gain_three, shift_three
    )
    grad_three, gain_three_part, shift_three_part = norm_backward(
        incoming, normed_three, inverse_three, gain_three
    )
    grad_ffn = grad_three.astype(LOW)

    def scattered(part, axes="dp"):
        return lax.psum_scatter(part, axes, scatter_dimension=0, tiled=True).astype(WIDE)

    contract_grad = scattered(weight_grad(activ_low, grad_ffn).astype(LOW))
    grad_pre = gelu_pull(back_project(grad_ffn, contract_full))[0].astype(LOW)
    expand_grad = scattered(weight_grad(second_low, grad_pre).astype(LOW))
    grad_second = grad_three + back_project(grad_pre, expand_full)
    grad_two, gain_two_part, shift_two_part = norm_backward(
        grad_second, normed_two, inverse_two, gain_two
    )
    grad_cross = grad_two.astype(LOW)
    cout_part = weight_grad(cross_attn, grad_cross)
    grad_cattn = heads_of(back_project(grad_cross, cout_full).astype(LOW), images)
    part_cquery, grad_ckey, grad_cvalue = attention_backward(
        cross_probs, heads_of(cross_attn, images), grad_cattn, cross_q, cross_k, cross_v
    )
    grad_cquery = lax.psum(joined(part_cquery).astype(LOW), "mem")
    grad_ckey = joined(grad_ckey).astype(LOW)
    grad_cvalue = joined(grad_cvalue).astype(LOW)
    kv_grad = scattered(
        jnp.concatenate(
            [weight_grad(memory_flat, grad_ckey), weight_grad(memory_flat, grad_cvalue)], axis=1
        ).astype(LOW),
        ("dp", "mem"),
    )
    memory_grad = back_project(grad_ckey, ckey_full) + back_project(grad_cvalue, cvalue_full)
    cquery_part = weight_grad(first_low, grad_cquery)
    grad_first = grad_two + back_project(grad_cquery, cquery_full)
    grad_one, gain_one_part, shift_one_part = norm_backward(
        grad_first, normed_one, inverse_one, gain_one
    )
    grad_self = grad_one.astype(LOW)
    out_part = weight_grad(self_attn, grad_self)
    grad_sattn = heads_of(back_project(grad_self, out_full).astype(LOW), images)
    grad_query, grad_key, grad_value = (
        joined(grad).astype(LOW)
        for grad in attention_backward(
            self_probs, heads_of(self_attn, images), grad_sattn, query_heads, key_heads, value_heads
        )
    )
    input_grad = (
        grad_one
        + back_project(grad_query, query_full)
        + back_project(grad_key, key_full)
        + back_project(grad_value, value_full)
    )
    norm_parts = jnp.stack(
        [gain_one_part, shift_one_part, gain_two_part, shift_two_part, gain_three_part, shift_three_part], axis=1
    )
    rest = scattered(
        jnp.concatenate(
            [
                weight_grad(tokens, grad_query),
                weight_grad(tokens, grad_key),
                weight_grad(tokens, grad_value),
                out_part,
                cquery_part,
                cout_part,
                jnp.pad(norm_parts, ((0, 0), (0, 122))),
            ],
            axis=1,
        ).astype(LOW)
    )
    squares_grad = [rest[:, place * width : (place + 1) * width] for place in range(6)]
    norms_grad = [rest[:, 6 * width + place] for place in range(6)]
    return (
        result.reshape(inputs.shape),
        input_grad.reshape(inputs.shape),
        memory_grad.reshape(memory.shape),
        *squares_grad[:5],
        kv_grad[:, :width],
        kv_grad[:, width:],
        squares_grad[5],
        expand_grad,
        contract_grad,
        *norms_grad,
    )


MESH = pl.DeviceIdType.MESH
ANY = pl.BlockSpec(memory_space=pl.ANY)
INNER = pl.BlockSpec(memory_space=pltpu.VMEM)
SCALAR = pl.BlockSpec(memory_space=pltpu.SMEM)
D = 768
FF = 3072
PAIRS = 6
QP = 112
PIECES = 16
SQ, SK, SV, SO, CK, CV, CQ, CO, EX, CT = 0, 1, 2, 3, 4, 5, 6, 7, 8, 12
WINDOW = 2
FIRST_DUE = 7.0
UNIT_TIME = 3.5
EXCHANGE_TIME = 16.0
VMEM_BYTES = 60 * 2**20


def mm(a, b):
    return lax.dot_general(a, b, (((1,), (0,)), ((), ())), preferred_element_type=WIDE)


def mm_nt(a, b):
    return lax.dot_general(a, b, (((1,), (1,)), ((), ())), preferred_element_type=WIDE)


def mm_tn(a, b):
    return lax.dot_general(a, b, (((0,), (0,)), ((), ())), preferred_element_type=WIDE)


def low_lanes(shape):
    return lax.broadcasted_iota(jnp.int32, shape, 1) < 64


def two_heads(pair):
    lower = low_lanes(pair.shape)
    nought = jnp.zeros_like(pair)
    return jnp.concatenate([jnp.where(lower, pair, nought), jnp.where(lower, nought, pair)], axis=0)


def one_pair(both):
    rows = both.shape[0] // 2
    upper = both[rows:]
    return jnp.where(low_lanes(upper.shape), both[:rows], upper)


def places():
    d = lax.axis_index("dp")
    c = lax.rem(d, 2)
    x = lax.rem(d // 2, 2)
    y = d // 4
    other = d + 1 - 2 * c
    beside = d + 2 - 4 * x
    above = d + 4 - 8 * y
    across = beside + 4 - 8 * y
    return d, other, beside, above, across


def weight_row(piece, owner):
    if isinstance(piece, int) and piece >= CT:
        return pl.multiple_of(CT * D + owner * 384 + (piece - CT) * 96, 96)
    return pl.multiple_of(piece * D + owner * 96, 96)


UNITS = ((SQ, SK), (SV,), (CK, CV), (SO,), (CQ,), (CO,), (8,), (9,), (10,), (11,), (12,), (13,), (14,), (15,))
LAG = 2


class Gather:
    def __init__(self, shards, full, local, send, recv, saved, save):
        self.shards, self.full, self.saved, self.save = shards, full, saved, save
        self.local, self.send, self.recv = local, send, recv
        self.d, self.other, self.beside, self.above, self.across = places()
        self.z = lax.axis_index("mem")
        self.q = lax.rem(self.z, 2)
        self.near = self.z + 1 - 2 * self.q
        self.sent = []
        self.done = 0
        self.clock = 0.0
        self.landed = [False] * PIECES
        self.unit_of = {piece: place for place, unit in enumerate(UNITS) for piece in unit}

    def at(self, piece, owner):
        return self.full.at[pl.ds(weight_row(piece, owner), 96)]

    def own(self, piece):
        if piece < EX:
            return self.shards[piece]
        if piece < CT:
            return self.shards[EX].at[:, pl.ds((piece - EX) * D, D)]
        return self.shards[EX + 1].at[pl.ds((piece - CT) * 96, 96)]

    def copy(self, src, piece, owner, kind, target, note):
        return pltpu.make_async_remote_copy(
            src,
            self.at(piece, owner),
            self.send.at[piece, note],
            self.recv.at[piece, kind],
            device_id=target,
            device_id_type=MESH,
        )

    def push(self, src, piece, owner, kind, target):
        one = self.copy(src, piece, owner, kind, (target, self.z), kind)
        one.start()
        self.sent.append(one)

    def lend(self, piece, owner, kind):
        one = self.copy(self.at(piece, owner), piece, owner, kind, (self.d, self.near), 7 + kind)
        one.start()
        self.sent.append(one)

    def arrived(self, piece, kind):
        self.copy(self.at(piece, self.d), piece, self.d, kind, (self.other, self.z), kind).wait_recv()

    def roles(self, unit):
        first, second = unit
        mine = first + self.q * (second - first)
        return mine, first + second - mine

    def local_copy(self, piece):
        return pltpu.make_async_copy(self.own(piece), self.at(piece, self.d), self.local.at[piece])

    def start(self, place):
        if place >= len(UNITS):
            return
        unit = UNITS[place]
        if len(unit) == 1:
            piece = unit[0]
            src = self.own(piece)
            self.local_copy(piece).start()
        else:
            piece, theirs = self.roles(unit)
            src = self.at(piece, self.d)
            self.push(self.at(theirs, self.d), theirs, self.d, 3, self.other)
        self.push(src, piece, self.d, 0, self.beside)
        self.push(src, piece, self.d, 1, self.above)
        self.push(src, piece, self.d, 3, self.other)

    def prepare(self):
        for unit in UNITS:
            if len(unit) == 2:
                for piece in unit:
                    self.local_copy(piece).start()

    def begin(self):
        for unit in UNITS:
            if len(unit) == 2:
                for piece in unit:
                    self.local_copy(piece).wait()
        for place in range(WINDOW):
            self.start(place)

    def relay(self, place):
        unit = UNITS[place]
        piece = unit[0] if len(unit) == 1 else self.roles(unit)[0]
        for kind, owner, side, target in ((0, self.beside, 0, self.above), (1, self.above, 1, self.beside)):
            self.arrived(piece, kind)
            if place % 2 == side:
                self.push(self.at(piece, owner), piece, owner, 2, target)
            self.push(self.at(piece, owner), piece, owner, 4 + kind, self.other)
            if len(unit) == 2:
                self.lend(piece, owner, kind)

    def finish(self, place):
        unit = UNITS[place]
        piece = unit[0] if len(unit) == 1 else self.roles(unit)[0]
        self.arrived(piece, 2)
        self.push(self.at(piece, self.across), piece, self.across, 6, self.other)
        if len(unit) == 2:
            self.lend(piece, self.across, 2)

    def borrow(self, place):
        unit = UNITS[place]
        if len(unit) == 2:
            piece = self.roles(unit)[1]
            for kind, owner in enumerate((self.beside, self.above, self.across)):
                self.arrived(piece, kind)
                self.push(self.at(piece, owner), piece, owner, 4 + kind, self.other)

    def step(self):
        place = self.done
        if place >= len(UNITS) + LAG:
            return
        self.done += 1
        if place < len(UNITS):
            self.relay(place)
            self.start(place + WINDOW)
        if 1 <= place <= len(UNITS):
            self.finish(place - 1)
        if place >= LAG:
            self.borrow(place - LAG)

    def due(self, place):
        return FIRST_DUE + UNIT_TIME * place

    def spend(self, time):
        self.wait_for(self.clock + time)

    def wait_for(self, clock):
        self.clock = max(self.clock, clock)
        while self.done < len(UNITS) + LAG and self.due(self.done) <= self.clock:
            self.step()

    def upto(self, count):
        while self.done < min(count, len(UNITS) + LAG):
            self.clock = max(self.clock, self.due(self.done))
            self.step()

    def ready(self, piece):
        place = self.unit_of[piece]
        self.upto(place + 1 + (1 if len(UNITS[place]) == 1 else LAG))
        if self.landed[piece]:
            return
        self.landed[piece] = True
        if len(UNITS[place]) == 1:
            self.local_copy(piece).wait()
        for kind in range(3, 7):
            self.arrived(piece, kind)
        if piece < CT:
            self.save(self.full.at[pl.ds(piece * D, D)], self.saved.at[pl.ds(piece * D, D)])

    def close(self):
        for one in self.sent:
            one.wait_send()


def greet(targets):
    barrier = pltpu.get_barrier_semaphore()
    for target in targets:
        pl.semaphore_signal(barrier, 1, device_id=target, device_id_type=MESH)
    pl.semaphore_wait(barrier, len(targets))


def norm_rows(resid, gain, shift):
    center = resid - jnp.mean(resid, axis=-1, keepdims=True)
    inverse = lax.rsqrt(jnp.mean(center * center, axis=-1, keepdims=True) + 1e-05)
    normed = center * inverse
    return normed * gain + shift, normed, inverse


def forward_kernel(images, queries, mem_rows, *refs):
    (raw, mem, lens, *rest) = refs
    norms, rest = rest[:6], rest[6:]
    shards = rest[:10]
    (o_result, o_full, o_acts, o_ffn, o_us, o_inv, o_kv, o_pc, o_ps, o_wst) = rest[10:20]
    (
        full, acts, ffn, us, inv, kv, pc, ps, wst, tok, wide, stats, osend, orecv, lsend, lrecv, fst,
        local, send, recv, zsend, zrecv, keep,
    ) = rest[20:]
    rows = images * QP
    z = lax.axis_index("mem")
    d = lax.axis_index("dp")
    kept = []

    def save(src, dst):
        one = pltpu.make_async_copy(src, dst, keep.at[len(kept)])
        one.start()
        kept.append(one)

    gather = Gather(shards, full, local, send, recv, o_full, save)
    others = [lax.rem(z + r, 4) for r in range(1, 4)]
    gather.prepare()
    greet(
        [(gather.other, z), (gather.beside, z), (gather.above, z)] + [(d, other) for other in others]
    )
    gather.begin()
    blank = jnp.zeros((QP - queries, D), LOW)
    for i in range(images):
        tok[pl.ds(i * QP, QP), :] = jnp.concatenate([raw[i], blank], axis=0)

    def weight(piece, tile):
        return full[pl.ds(piece * D, D), cols(tile)]

    def cols(tile):
        return pl.ds(pl.multiple_of(tile * 256, 256), 256)

    def image(i):
        return pl.ds(pl.multiple_of(i * QP, QP), QP)

    def project_rows(src, piece, dst, scale):
        def body(tile, carry):
            out = mm(src[...], weight(piece, tile)).astype(LOW)
            if scale != 1.0:
                out = out * jnp.asarray(scale, LOW)
            acts[dst, :, cols(tile)] = out
            return carry

        lax.fori_loop(0, 3, body, 0)

    gather.ready(SQ)
    project_rows(tok, SQ, 0, 0.125)
    gather.ready(SK)
    project_rows(tok, SK, 1, 1.0)
    gather.ready(SV)
    project_rows(tok, SV, 2, 1.0)

    gather.spend(2.0)
    for i in range(images):
        at = image(i)
        valid = lax.broadcasted_iota(jnp.int32, (2 * QP, QP), 1) < queries

        def self_pair(hp, carry):
            lanes = pl.ds(pl.multiple_of(hp * 128, 128), 128)
            scores = mm_nt(two_heads(acts[0, at, lanes]), acts[1, at, lanes])
            scores = jnp.where(valid, scores, -1e30)
            grown = jnp.exp(scores - jnp.max(scores, axis=-1, keepdims=True))
            probs = (grown / jnp.sum(grown, axis=-1, keepdims=True)).astype(LOW)
            ps[i, hp] = probs
            acts[3, at, lanes] = one_pair(mm(probs, acts[2, at, lanes])).astype(LOW)
            return carry

        lax.fori_loop(0, PAIRS, self_pair, 0)
        gather.spend(1.0)

    def memory_rows(piece, dst):
        for tile in range(3):
            kv[dst, :, cols(tile)] = mm(mem[...], weight(piece, tile)).astype(LOW)
            gather.spend(0.7)

    def add_branch(src, piece, base):
        def body(tile, carry):
            wide[0, :, cols(tile)] = base(cols(tile)) + mm(acts[src], weight(piece, tile))
            return carry

        lax.fori_loop(0, 3, body, 0)

    def normalize(which, low_dst):
        def body(i, carry):
            at = image(i)
            gain, shift = norms[2 * which][...][None, :], norms[2 * which + 1][...][None, :]
            out, normed, inverse = norm_rows(wide[0, at, :], gain, shift)
            us[which, at, :] = normed
            lane = lax.broadcasted_iota(jnp.int32, (QP, 128), 1)
            inv[at, :] = jnp.where(lane == which, inverse, inv[at, :])
            wide[1, at, :] = out
            if low_dst is not None:
                acts[low_dst, at, :] = out.astype(LOW)
            return carry

        lax.fori_loop(0, images, body, 0)

    inv[...] = jnp.zeros_like(inv)
    gather.ready(SO)
    add_branch(3, SO, lambda at: tok[:, at].astype(WIDE))
    normalize(0, 4)
    gather.spend(1.6)
    save(us.at[0], o_us.at[0])
    gather.ready(CK)
    memory_rows(CK, 0)
    gather.ready(CV)
    memory_rows(CV, 1)
    save(kv, o_kv)
    save(ps, o_ps)
    gather.ready(CQ)
    project_rows(acts.at[4], CQ, 5, 0.125)

    pushed = []

    def pass_on(src, dst, kind, r):
        one = pltpu.make_async_remote_copy(
            src, dst, zsend.at[kind, r - 1], zrecv.at[kind, r - 1],
            device_id=(d, others[r - 1]), device_id_type=MESH,
        )
        one.start()
        pushed.append(one)

    def taken(ref, kind, r):
        pltpu.make_async_remote_copy(
            ref, ref, zsend.at[kind, r - 1], zrecv.at[kind, r - 1],
            device_id=(d, others[r - 1]), device_id_type=MESH,
        ).wait_recv()

    lane = lax.broadcasted_iota(jnp.int32, (QP, 128), 1)

    def turned(tall):
        return jnp.concatenate([tall, jnp.zeros((128 - QP, 128), WIDE)], axis=0).T[:16]

    def returned(flat):
        return jnp.concatenate([flat, jnp.zeros((112, 128), WIDE)], axis=0).T[:QP]

    for turn in range(4):
        i = others[turn] if turn < 3 else z
        at = image(i)
        tokens = pl.ds(pl.multiple_of(i * mem_rows, mem_rows), mem_rows)
        place = z * mem_rows + lax.broadcasted_iota(jnp.int32, (2 * QP, mem_rows), 1)
        valid = place < lens[i]

        def pair(hp, noted):
            lanes = pl.ds(pl.multiple_of(hp * 128, 128), 128)
            scores = mm_nt(two_heads(acts[5, at, lanes]), kv[0, tokens, lanes])
            scores = jnp.where(valid, scores, -1e30)
            top = jnp.max(scores, axis=-1, keepdims=True)
            grown = jnp.where(valid, jnp.exp(scores - top), 0.0)
            total = jnp.sum(grown, axis=-1, keepdims=True)
            shrink = jnp.where(total > 0.0, 1.0 / total, 0.0)
            probs = grown.astype(LOW)
            pc[i, hp] = probs
            osend[turn, :, lanes] = one_pair(mm(probs, kv[1, tokens, lanes]) * shrink).astype(LOW)
            for half in range(2):
                span = slice(half * QP, half * QP + QP)
                noted = jnp.where(lane == 2 * hp + half, top[span], noted)
                noted = jnp.where(lane == 64 + 2 * hp + half, total[span], noted)
            return noted

        noted = lax.fori_loop(0, PAIRS, pair, jnp.zeros((QP, 128), WIDE))
        stats[i] = noted
        total = pltpu.roll(noted, 64, 1)
        lsend[turn] = turned(jnp.where(total > 0.0, noted + jnp.log(total), -1e30))
        if turn < 3:
            pass_on(osend.at[turn], orecv.at[turn], 0, turn + 1)
            pass_on(lsend.at[turn], lrecv.at[turn], 1, turn + 1)
        gather.spend(1.9)
    save(pc, o_pc)
    gather.wait_for(gather.clock + EXCHANGE_TIME - 5.0)
    for r in range(1, 4):
        taken(orecv.at[r - 1], 0, r)
        taken(lrecv.at[r - 1], 1, r)
    noted = [lsend[3], lrecv[0], lrecv[1], lrecv[2]]
    top = functools.reduce(jnp.maximum, noted)
    level = top + jnp.log(sum(jnp.exp(one - top) for one in noted))
    fst[z] = level
    share = [returned(jnp.exp(one - level)) for one in noted]
    lower = low_lanes((QP, 128))
    mine = image(z)
    for hp in range(PAIRS):
        lanes = pl.ds(hp * 128, 128)
        joined = jnp.zeros((QP, 128), WIDE)
        for r in range(4):
            spread = jnp.where(
                lower, share[r][:, 2 * hp : 2 * hp + 1], share[r][:, 2 * hp + 1 : 2 * hp + 2]
            )
            part = osend[3, :, lanes] if r == 0 else orecv[r - 1, :, lanes]
            joined = joined + spread * part.astype(WIDE)
        acts[6, mine, lanes] = joined.astype(LOW)
    for r in range(1, 4):
        pass_on(acts.at[6, mine], acts.at[6, mine], 2, r)
        pass_on(fst.at[z], fst.at[z], 3, r)
    gather.wait_for(gather.clock + EXCHANGE_TIME)
    gather.ready(CO)
    for r in range(1, 4):
        back = lax.rem(z + 4 - r, 4)
        taken(acts.at[6, image(back)], 2, r)
        taken(fst.at[back], 3, r)
    for i in range(images):
        wst[i] = jnp.exp(stats[i] - returned(fst[i]))
    save(wst, o_wst)
    add_branch(6, CO, lambda at: wide[1, :, at])
    normalize(1, 7)
    save(us.at[1], o_us.at[1])
    save(acts, o_acts)

    def expand(block):
        def body(tile, carry):
            pre = mm(acts[7], full[pl.ds((EX + block) * D, D), cols(tile)])
            root = 0.7978845608028654
            square = pre * pre
            bend = jnp.tanh(root * (pre + 0.044715 * (pre * square)))
            half = 0.5 * (1.0 + bend)
            slope = half + (0.5 * root) * pre * (1.0 - bend * bend) * (1.0 + 0.134145 * square)
            at = pl.ds(pl.multiple_of(block * D + tile * 256, 256), 256)
            ffn[0, :, at] = (pre * half).astype(LOW)
            ffn[1, :, at] = slope.astype(LOW)
            return carry

        lax.fori_loop(0, 3, body, 0)

    for block in range(4):
        gather.ready(EX + block)
        expand(block)
        gather.spend(1.2)
    save(ffn, o_ffn)
    for block in range(4):
        gather.ready(CT + block)
    save(full.at[pl.ds(CT * D, FF)], o_full.at[pl.ds(CT * D, FF)])

    def contract(tile, carry):
        wide[0, :, cols(tile)] = wide[1, :, cols(tile)] + mm(
            ffn[0], full[pl.ds(CT * D, FF), cols(tile)]
        )
        return carry

    lax.fori_loop(0, 3, contract, 0)
    normalize(2, None)
    save(wide.at[1], o_result)
    save(us.at[2], o_us.at[2])
    save(inv, o_inv)
    for one in pushed:
        one.wait_send()
    gather.close()
    for one in kept:
        one.wait()


def forward(tok, mem, lens, norms, shards, images, queries, mem_rows):
    rows = images * QP
    shape = jax.ShapeDtypeStruct
    tokens = images * mem_rows
    outs = (
        shape((rows, D), WIDE),
        shape((PIECES * D, D), LOW),
        shape((8, rows, D), LOW),
        shape((2, rows, FF), LOW),
        shape((3, rows, D), WIDE),
        shape((rows, 128), WIDE),
        shape((2, tokens, D), LOW),
        shape((images, PAIRS, 2 * QP, mem_rows), LOW),
        shape((images, PAIRS, 2 * QP, QP), LOW),
        shape((images, QP, 128), WIDE),
    )
    dma = pltpu.SemaphoreType.DMA
    return pl.pallas_call(
        functools.partial(forward_kernel, images, queries, mem_rows),
        out_shape=outs,
        in_specs=[INNER, INNER, SCALAR] + [INNER] * 6 + [ANY] * 10,
        out_specs=[ANY] * len(outs),
        scratch_shapes=[
            *[pltpu.VMEM(one.shape, one.dtype) for one in outs[1:]],
            pltpu.VMEM((rows, D), LOW),
            pltpu.VMEM((2, rows, D), WIDE),
            pltpu.VMEM((images, QP, 128), WIDE),
            pltpu.VMEM((4, QP, D), LOW),
            pltpu.VMEM((3, QP, D), LOW),
            pltpu.VMEM((4, 16, 128), WIDE),
            pltpu.VMEM((3, 16, 128), WIDE),
            pltpu.VMEM((images, 16, 128), WIDE),
            dma((PIECES,)),
            dma((PIECES, 10)),
            dma((PIECES, 7)),
            dma((4, 3)),
            dma((4, 3)),
            dma((28,)),
        ],
        compiler_params=pltpu.CompilerParams(
            collective_id=0, has_side_effects=True, vmem_limit_bytes=VMEM_BYTES
        ),
        name="forward",
    )(tok, mem, lens, *norms, *(shards[place] for place in (0, 1, 2, 3, 5, 6, 4, 7, 8, 9)))


def rows_of_image(i):
    return pl.ds(pl.multiple_of(i * QP, QP), QP)


def cols_of_tile(tile):
    return pl.ds(pl.multiple_of(tile * 256, 256), 256)


class Reduce:
    def __init__(self, where, turn, grad, core_in, chip_in, core_sems, chip_sems):
        self.where, self.turn = where, turn
        self.grad, self.core_in, self.chip_in = grad, core_in, chip_in
        self.core_sems, self.chip_sems = core_sems, chip_sems
        self.sent = []
        d, other, beside, above, across = where
        self.c = lax.rem(d, 2)
        self.z = lax.axis_index("mem")

    def copy(self, src, dst, sems, place, target):
        return pltpu.make_async_remote_copy(
            src, dst, sems.at[0, self.turn, place], sems.at[1, self.turn, place],
            device_id=(target, self.z), device_id_type=MESH,
        )

    def core_stage(self):
        one = self.copy(self.grad.at[1 - self.c], self.core_in, self.core_sems, 0, self.where[1])
        one.start()
        self.sent.append(one)

    def chip_stage(self):
        self.copy(self.core_in, self.core_in, self.core_sems, 0, self.where[1]).wait_recv()
        for chip in range(4):
            both = self.grad[self.c, chip].astype(WIDE) + self.core_in[chip].astype(WIDE)
            self.grad[self.c, chip] = both.astype(LOW)
        for place, target in enumerate(self.where[2:]):
            one = self.copy(
                self.grad.at[self.c, target // 2], self.chip_in.at[place], self.chip_sems, place, target
            )
            one.start()
            self.sent.append(one)

    def total(self):
        own = self.grad[self.c, self.where[0] // 2].astype(WIDE)
        for place, target in enumerate(self.where[2:]):
            self.copy(
                self.chip_in.at[place], self.chip_in.at[place], self.chip_sems, place, target
            ).wait_recv()
            own = own + self.chip_in[place].astype(WIDE)
        return own

    def settle(self):
        for one in self.sent:
            one.wait_send()
        self.sent = []


def backward_kernel(images, queries, mem_rows, *refs):
    (
        h_gain_one, h_gain_two, h_gain_three, h_cot, h_tok, h_mem, h_full, h_acts, h_ffn, h_us, h_inv, h_kv, h_pc, h_ps, h_wst,
    ) = refs[:15]
    (o_expand, o_contract, o_rest, o_keys, o_mem, o_in, o_norms) = refs[15:22]
    (
        cot, tok, mem, slots, acts, ffn, us, inv, kv, pc, ps, wst, wide, grads, nsum, nin,
        zsend, zin, mout,
        g_expand, g_contract, g_rest, c_expand, c_contract, c_rest, c_keys,
        t_expand, t_contract, t_rest, t_keys, f_expand, f_contract, f_rest, k_out, k_in,
        load, slot_sems, pc_sems, mout_sems, core_sems, chip_sems, fin_sems, local_sems, ksems, zsems, nsems,
    ) = refs[22:]
    z = lax.axis_index("mem")
    d = lax.axis_index("dp")
    where = places()
    q = lax.rem(z, 2)
    zp = z + 1 - 2 * q
    others = [lax.rem(z + r, 4) for r in range(1, 4)]
    dpeers = [lax.rem(d + r, 8) for r in range(1, 8)]

    gains = (h_gain_one, h_gain_two, h_gain_three)
    loads = {}
    waited = set()

    def fetch(name, src, dst):
        one = pltpu.make_async_copy(src, dst, load.at[len(loads)])
        one.start()
        loads[name] = one

    order = [CT, CT + 1, CT + 2, CT + 3, EX, EX + 1, EX + 2, EX + 3, CO, CK, CV, CQ, SO, SQ, SK, SV]
    depth = 4

    def slot_copy(turn):
        return pltpu.make_async_copy(
            h_full.at[pl.ds(order[turn] * D, D)], slots.at[turn % depth], slot_sems.at[turn % depth]
        )

    def prefetch(turn):
        if turn < len(order):
            slot_copy(turn).start()

    fetch("cot", h_cot, cot)
    fetch("inv", h_inv, inv)
    fetch("u3", h_us.at[2], us.at[0])
    for turn in range(depth):
        prefetch(turn)
    fetch("gp", h_ffn.at[1], ffn.at[1])
    fetch("act", h_ffn.at[0], ffn.at[0])
    fetch("acts", h_acts, acts)
    fetch("u2", h_us.at[1], us.at[1])
    fetch("kv", h_kv, kv)
    fetch("wst", h_wst, wst)
    fetch("ps", h_ps, ps)
    fetch("mem", h_mem, mem)
    fetch("tok", h_tok, tok)

    def have(name):
        if name not in waited:
            waited.add(name)
            loads[name].wait()

    def pc_copy(turn):
        i = lax.rem(z + turn + 1, 4)
        return pltpu.make_async_copy(h_pc.at[i], pc.at[turn % 2], pc_sems.at[turn % 2])

    pc_copy(0).start()
    pc_copy(1).start()
    greet([(peer, z) for peer in dpeers] + [(d, other) for other in others])

    nsum[...] = jnp.zeros_like(nsum)

    def norm_back(which, incoming, slot, low_dst):
        def body(i, carry):
            at = rows_of_image(i)
            above = incoming(at)
            unit = us[slot, at, :]
            inverse = inv[at, which : which + 1]
            scaled = above * gains[which][...][None, :]
            first = jnp.mean(scaled, axis=-1, keepdims=True)
            second = jnp.mean(scaled * unit, axis=-1, keepdims=True)
            grad = inverse * (scaled - first - unit * second)
            wide[0, at, :] = grad
            grads[low_dst, at, :] = grad.astype(LOW)
            row = 2 * which
            nsum[row : row + 1, :] += jnp.sum(above * unit, axis=0, keepdims=True)
            nsum[row + 1 : row + 2, :] += jnp.sum(above, axis=0, keepdims=True)
            return carry

        lax.fori_loop(0, images, body, 0)

    turn_of = {piece: turn for turn, piece in enumerate(order)}

    def slot(piece):
        turn = turn_of[piece]
        slot_copy(turn).wait()
        return slots.at[turn % depth]

    def freed(piece):
        prefetch(turn_of[piece] + depth)

    for name in ("cot", "inv", "u3"):
        have(name)
    norm_back(2, lambda at: cot[at, :].astype(WIDE), 0, 0)
    fetch("u1", h_us.at[0], us.at[0])
    have("gp")
    for block in range(4):
        weight = slot(CT + block)

        def body(tile, carry):
            at = pl.ds(pl.multiple_of(block * D + tile * 256, 256), 256)
            back = mm_nt(grads[0], weight[cols_of_tile(tile), :])
            ffn[1, :, at] = (back * ffn[1, :, at].astype(WIDE)).astype(LOW)
            return carry

        lax.fori_loop(0, 3, body, 0)
        freed(CT + block)

    def reduce_at(place, grad, core_in, chip_in):
        return Reduce(where, place, grad, core_in, chip_in, core_sems, chip_sems)

    have("acts")
    r_expand = reduce_at(0, g_expand, c_expand, t_expand)

    def expand_part(tile, carry):
        at = pl.ds(pl.multiple_of(q * 1536 + tile * 256, 256), 256)
        out = mm_tn(acts[7], ffn[1, :, at]).astype(LOW)
        for e in range(8):
            g_expand[e % 2, e // 2, :, cols_of_tile(tile)] = out[96 * e : 96 * e + 96]
        return carry

    lax.fori_loop(0, 6, expand_part, 0)
    r_expand.core_stage()
    have("act")
    r_contract = reduce_at(1, g_contract, c_contract, t_contract)

    def contract_part(e, carry):
        at = pl.ds(pl.multiple_of(e * 384, 384), 384)
        half = pl.ds(pl.multiple_of(q * 384, 384), 384)
        g_contract[lax.rem(e, 2), e // 2] = mm_tn(ffn[0, :, at], grads[0, :, half]).astype(LOW)
        return carry

    lax.fori_loop(0, 8, contract_part, 0)
    r_contract.core_stage()
    r_expand.chip_stage()
    for block in range(4):
        weight = slot(EX + block)

        def body(tile, carry):
            at = cols_of_tile(tile)
            back = mm_nt(ffn[1, :, pl.ds(block * D, D)], weight[at, :])
            wide[0, :, at] = wide[0, :, at] + back
            return carry

        lax.fori_loop(0, 3, body, 0)
        freed(EX + block)
    r_contract.chip_stage()
    have("u2")
    norm_back(1, lambda at: wide[0, at, :], 1, 1)

    def through(src, piece, dst):
        weight = slot(piece)

        def body(tile, carry):
            grads[dst, :, cols_of_tile(tile)] = mm_nt(grads[src], weight[cols_of_tile(tile), :]).astype(LOW)
            return carry

        lax.fori_loop(0, 3, body, 0)
        freed(piece)

    through(1, CO, 0)
    have("kv")
    have("wst")
    pushed = []

    def across_mem(src, dst, kind, r):
        return pltpu.make_async_remote_copy(
            src, dst, zsems.at[0, kind, r - 1], zsems.at[1, kind, r - 1],
            device_id=(d, others[r - 1]), device_id_type=MESH,
        )

    for turn in range(4):
        i = lax.rem(z + turn + 1, 4)
        pc_copy(turn).wait()
        at = rows_of_image(i)
        tokens = pl.ds(pl.multiple_of(i * mem_rows, mem_rows), mem_rows)
        factors = wst[i]

        def pair(hp, carry):
            lanes = pl.ds(pl.multiple_of(hp * 128, 128), 128)
            query = two_heads(acts[5, at, lanes])
            above = two_heads(grads[0, at, lanes])
            attn = acts[6, at, lanes].astype(WIDE)
            row = jnp.sum(above.astype(WIDE) * jnp.concatenate([attn, attn], axis=0), axis=-1, keepdims=True)
            lane = lax.broadcasted_iota(jnp.int32, (QP, 128), 1)
            factor = jnp.concatenate(
                [
                    jnp.sum(jnp.where(lane == 2 * hp + half, factors, 0.0), axis=-1, keepdims=True)
                    for half in range(2)
                ],
                axis=0,
            )
            probs = pc[turn % 2, hp].astype(WIDE) * factor
            keys, values = kv[0, tokens, lanes], kv[1, tokens, lanes]
            inner = mm_nt(above, values)
            scores = (probs * (inner - row)).astype(LOW)
            zsend[turn, :, lanes] = (one_pair(mm(scores, keys)) * 0.125).astype(LOW)
            kv[0, tokens, lanes] = mm_tn(scores, query).astype(LOW)
            kv[1, tokens, lanes] = mm_tn(probs.astype(LOW), above).astype(LOW)
            return carry

        lax.fori_loop(0, PAIRS, pair, 0)
        if turn < 2:
            pc_copy(turn + 2).start()
        if turn < 3:
            one = across_mem(zsend.at[turn], zin.at[turn], 0, turn + 1)
            one.start()
            pushed.append(one)

    have("mem")
    r_expand.settle()
    r_keys = reduce_at(2, g_expand, c_keys, t_keys)
    for which in range(2):

        def key_part(tile, carry):
            out = mm_tn(mem[...], kv[which, :, cols_of_tile(tile)]).astype(LOW)
            at = pl.ds(pl.multiple_of(which * D + tile * 256, 256), 256)
            for e in range(8):
                g_expand[e % 2, e // 2, :, at] = out[96 * e : 96 * e + 96]
            return carry

        if which == 0:
            final_expand = r_expand.total()
            f_expand[...] = final_expand.astype(LOW)
        lax.fori_loop(0, 3, key_part, 0)
    r_keys.core_stage()
    for r in range(1, 4):
        across_mem(zin.at[r - 1], zin.at[r - 1], 0, r).wait_recv()
    mine = rows_of_image(z)
    grads[3, mine, :] = (
        zsend[3].astype(WIDE) + zin[0].astype(WIDE) + zin[1].astype(WIDE) + zin[2].astype(WIDE)
    ).astype(LOW)
    for r in range(1, 4):
        one = across_mem(grads.at[3, mine], grads.at[3, mine], 1, r)
        one.start()
        pushed.append(one)

    def finals(fin, out, place):
        pltpu.make_async_copy(fin, out, local_sems.at[place]).start()
        one = pltpu.make_async_remote_copy(
            fin, out, fin_sems.at[0, place], fin_sems.at[1, place], device_id=(d, zp), device_id_type=MESH
        )
        one.start()
        return one

    ended = []
    r_keys.chip_stage()
    key_weight, value_weight = slot(CK), slot(CV)
    for i in range(images):
        at = pl.ds(i * mem_rows, mem_rows)
        if i >= 2:
            pltpu.make_async_copy(mout.at[i % 2], o_mem.at[at], mout_sems.at[i % 2]).wait()

        def body(tile, carry):
            span = cols_of_tile(tile)
            mout[i % 2, :, span] = (
                mm_nt(kv[0, at, :], key_weight[span, :]) + mm_nt(kv[1, at, :], value_weight[span, :])
            ).astype(LOW)
            return carry

        lax.fori_loop(0, 3, body, 0)
        pltpu.make_async_copy(mout.at[i % 2], o_mem.at[at], mout_sems.at[i % 2]).start()
    freed(CK)
    freed(CV)
    for r in range(1, 4):
        back = lax.rem(z + 4 - r, 4)
        across_mem(grads.at[3, rows_of_image(back)], grads.at[3, rows_of_image(back)], 1, r).wait_recv()
    ended.append(finals(f_expand, o_expand.at[q], 0))
    f_contract[...] = r_contract.total().astype(LOW)
    ended.append(finals(f_contract, o_contract.at[q], 1))

    def add_back(src, piece):
        weight = slot(piece)

        def body(tile, carry):
            span = cols_of_tile(tile)
            wide[0, :, span] = wide[0, :, span] + mm_nt(src(), weight[span, :])
            return carry

        lax.fori_loop(0, 3, body, 0)
        freed(piece)

    add_back(lambda: grads[3], CQ)
    have("u1")
    norm_back(0, lambda at: wide[0, at, :], 0, 2)
    for r in range(1, 8):
        one = pltpu.make_async_remote_copy(
            nsum, nin.at[r - 1], nsems.at[0, r - 1], nsems.at[1, r - 1],
            device_id=(dpeers[r - 1], z), device_id_type=MESH,
        )
        one.start()
        pushed.append(one)
    have("tok")

    def rest_part(turn, lefts, rights):
        reducer = reduce_at(3 + turn, g_rest.at[turn], c_rest.at[turn], t_rest.at[turn])

        def work(left, right):
            def body(tile, carry):
                out = mm_tn(left(), right(cols_of_tile(tile))).astype(LOW)
                for e in range(8):
                    g_rest[turn, e % 2, e // 2, :, cols_of_tile(tile)] = out[96 * e : 96 * e + 96]
                return carry

            lax.fori_loop(0, 3, body, 0)

        @pl.when(q == 0)
        def _():
            work(lefts[0], rights[0])

        @pl.when(q == 1)
        def _():
            work(lefts[1], rights[1])

        reducer.core_stage()
        return reducer

    r_first = rest_part(
        0,
        (lambda: acts[6], lambda: acts[4]),
        (lambda at: grads[1, :, at], lambda at: grads[3, :, at]),
    )
    through(2, SO, 0)
    have("ps")
    r_first.chip_stage()

    def self_image(i, carry):
        at = rows_of_image(i)
        for hp in range(PAIRS):
            lanes = pl.ds(hp * 128, 128)
            query = two_heads(acts[0, at, lanes])
            above = two_heads(grads[0, at, lanes])
            attn = acts[3, at, lanes].astype(WIDE)
            row = jnp.sum(above.astype(WIDE) * jnp.concatenate([attn, attn], axis=0), axis=-1, keepdims=True)
            probs = ps[i, hp]
            keys, values = acts[1, at, lanes], acts[2, at, lanes]
            inner = mm_nt(above, values)
            scores = (probs.astype(WIDE) * (inner - row)).astype(LOW)
            acts[0, at, lanes] = (one_pair(mm(scores, keys)) * 0.125).astype(LOW)
            acts[1, at, lanes] = mm_tn(scores, query).astype(LOW)
            acts[2, at, lanes] = mm_tn(probs, above).astype(LOW)
        return carry

    lax.fori_loop(0, images, self_image, 0)
    r_second = rest_part(
        1,
        (lambda: acts[3], lambda: tok[...]),
        (lambda at: grads[2, :, at], lambda at: acts[0, :, at]),
    )
    r_third = rest_part(
        2,
        (lambda: tok[...], lambda: tok[...]),
        (lambda at: acts[1, :, at], lambda at: acts[2, :, at]),
    )
    r_second.chip_stage()
    r_third.chip_stage()
    quarter = 24
    keys_total = r_keys.total()
    for part in range(4):
        k_out[part] = keys_total[quarter * part : quarter * part + quarter].astype(LOW)
    for r in range(1, 4):
        one = pltpu.make_async_remote_copy(
            k_out.at[others[r - 1]], k_in.at[r - 1], ksems.at[0, r - 1], ksems.at[1, r - 1],
            device_id=(d, others[r - 1]), device_id_type=MESH,
        )
        one.start()
        pushed.append(one)
    f_rest[0] = r_first.total().astype(LOW)
    ended.append(finals(f_rest.at[0], o_rest.at[0, q], 2))
    add_back(lambda: acts[0], SQ)
    add_back(lambda: acts[1], SK)
    add_back(lambda: acts[2], SV)
    pltpu.make_async_copy(wide.at[0], o_in, load.at[15]).start()
    f_rest[1] = r_second.total().astype(LOW)
    ended.append(finals(f_rest.at[1], o_rest.at[1, q], 3))
    f_rest[2] = r_third.total().astype(LOW)
    ended.append(finals(f_rest.at[2], o_rest.at[2, q], 4))
    sums = nsum[...]
    for r in range(1, 8):
        pltpu.make_async_remote_copy(
            nsum, nin.at[r - 1], nsems.at[0, r - 1], nsems.at[1, r - 1],
            device_id=(dpeers[r - 1], z), device_id_type=MESH,
        ).wait_recv()
        sums = sums + nin[r - 1]
    o_norms[...] = sums
    total = k_out[z].astype(WIDE)
    for r in range(1, 4):
        pltpu.make_async_remote_copy(
            k_in.at[r - 1], k_in.at[r - 1], ksems.at[0, r - 1], ksems.at[1, r - 1],
            device_id=(d, others[r - 1]), device_id_type=MESH,
        ).wait_recv()
        total = total + k_in[r - 1].astype(WIDE)
    o_keys[...] = total
    for i in range(2, 4):
        at = pl.ds(i * mem_rows, mem_rows)
        pltpu.make_async_copy(mout.at[i % 2], o_mem.at[at], mout_sems.at[i % 2]).wait()
    pltpu.make_async_copy(wide.at[0], o_in, load.at[15]).wait()
    fins = (f_expand, f_contract, f_rest.at[0], f_rest.at[1], f_rest.at[2])
    outs = (
        (o_expand.at[q], o_expand.at[1 - q]),
        (o_contract.at[q], o_contract.at[1 - q]),
        (o_rest.at[0, q], o_rest.at[0, 1 - q]),
        (o_rest.at[1, q], o_rest.at[1, 1 - q]),
        (o_rest.at[2, q], o_rest.at[2, 1 - q]),
    )
    for place, (fin, (out, theirs)) in enumerate(zip(fins, outs)):
        pltpu.make_async_copy(fin, out, local_sems.at[place]).wait()
        ended[place].wait_send()
        pltpu.make_async_remote_copy(
            fin, theirs, fin_sems.at[0, place], fin_sems.at[1, place], device_id=(d, zp), device_id_type=MESH
        ).wait_recv()
    for one in pushed:
        one.wait_send()
    for reducer in (r_contract, r_keys, r_first, r_second, r_third):
        reducer.settle()


def backward(gains, cot, tok, mem, saved, images, queries, mem_rows):
    full, acts, ffn, us, inv, kv, pc, ps, wst = saved
    rows = images * QP
    tokens = images * mem_rows
    shape = jax.ShapeDtypeStruct
    outs = (
        shape((2, 96, 1536), LOW),
        shape((2, 384, 384), LOW),
        shape((3, 2, 96, D), LOW),
        shape((24, 1536), WIDE),
        shape((tokens, D), LOW),
        shape((rows, D), WIDE),
        shape((8, D), WIDE),
    )
    dma = pltpu.SemaphoreType.DMA
    vmem = pltpu.VMEM
    return pl.pallas_call(
        functools.partial(backward_kernel, images, queries, mem_rows),
        out_shape=outs,
        in_specs=[INNER] * 3 + [ANY] * 12,
        out_specs=[ANY] * 3 + [INNER] + [ANY] * 2 + [INNER],
        scratch_shapes=[
            vmem((rows, D), LOW),
            vmem((rows, D), LOW),
            vmem((tokens, D), LOW),
            vmem((4, D, D), LOW),
            vmem((8, rows, D), LOW),
            vmem((2, rows, FF), LOW),
            vmem((2, rows, D), WIDE),
            vmem((rows, 128), WIDE),
            vmem((2, tokens, D), LOW),
            vmem((2, PAIRS, 2 * QP, mem_rows), LOW),
            vmem((images, PAIRS, 2 * QP, QP), LOW),
            vmem((images, QP, 128), WIDE),
            vmem((1, rows, D), WIDE),
            vmem((4, rows, D), LOW),
            vmem((8, D), WIDE),
            vmem((7, 8, D), WIDE),
            vmem((4, QP, D), LOW),
            vmem((3, QP, D), LOW),
            vmem((2, mem_rows, D), LOW),
            vmem((2, 4, 96, 1536), LOW),
            vmem((2, 4, 384, 384), LOW),
            vmem((3, 2, 4, 96, D), LOW),
            vmem((4, 96, 1536), LOW),
            vmem((4, 384, 384), LOW),
            vmem((3, 4, 96, D), LOW),
            vmem((4, 96, 1536), LOW),
            vmem((3, 96, 1536), LOW),
            vmem((3, 384, 384), LOW),
            vmem((3, 3, 96, D), LOW),
            vmem((3, 96, 1536), LOW),
            vmem((96, 1536), LOW),
            vmem((384, 384), LOW),
            vmem((3, 96, D), LOW),
            vmem((4, 24, 1536), LOW),
            vmem((3, 24, 1536), LOW),
            dma((16,)),
            dma((4,)),
            dma((2,)),
            dma((2,)),
            dma((2, 6, 1)),
            dma((2, 6, 3)),
            dma((2, 5)),
            dma((5,)),
            dma((2, 3)),
            dma((2, 2, 3)),
            dma((2, 7)),
        ],
        compiler_params=pltpu.CompilerParams(
            collective_id=1, has_side_effects=True, vmem_limit_bytes=VMEM_BYTES
        ),
        name="backward",
    )(*gains, cot, tok, mem, *saved)


def fused_on_device(
    inputs,
    memory,
    lengths,
    self_query,
    self_key,
    self_value,
    self_out,
    cross_query,
    cross_key,
    cross_value,
    cross_out,
    expand_weight,
    contract_weight,
    gain_one,
    shift_one,
    gain_two,
    shift_two,
    gain_three,
    shift_three,
    cotangent,
):
    images, queries, width = inputs.shape
    mem_rows = memory.shape[1]
    norms = (gain_one, shift_one, gain_two, shift_two, gain_three, shift_three)
    shards = (self_query, self_key, self_value, self_out, cross_query, cross_key, cross_value, cross_out, expand_weight, contract_weight)

    def padded(values):
        wider = jnp.pad(values, ((0, 0), (0, QP - queries), (0, 0)))
        return wider.reshape(images * QP, width)

    def cut(values):
        return values.reshape(images, QP, width)[:, :queries]

    tokens = padded(inputs)
    memory_flat = memory.reshape(images * mem_rows, width)
    result, full, acts, ffn, us, inv, kv, pc, ps, wst = forward(
        inputs, memory_flat, lengths, norms, shards, images, queries, mem_rows
    )
    spread, contracted, rest, keys, memory_grad, input_grad, sums = backward(
        norms[::2], padded(cotangent), tokens, memory_flat, (full, acts, ffn, us, inv, kv, pc, ps, wst),
        images, queries, mem_rows,
    )
    share = self_query.shape[0]
    sums = lax.dynamic_slice(sums, (0, lax.axis_index("dp") * share), (8, share))
    rest = rest.astype(WIDE)
    return (
        cut(result),
        cut(input_grad),
        memory_grad.reshape(memory.shape).astype(WIDE),
        rest[1, 1],
        rest[2, 0],
        rest[2, 1],
        rest[1, 0],
        rest[0, 1],
        keys[:, :width],
        keys[:, width:],
        rest[0, 0],
        jnp.concatenate([spread[0], spread[1]], axis=1).astype(WIDE),
        jnp.concatenate([contracted[0], contracted[1]], axis=1).astype(WIDE),
        *[sums[place] for place in range(6)],
    )


def solution(mesh):
    fused = mesh.shape["dp"] == 8 and mesh.shape["mem"] == 4

    rows = P("dp", None)
    image = P("dp", None, None)
    token = P("dp", "mem", None)
    both = P(("dp", "mem"), None)
    return jax.shard_map(
        fused_on_device if fused else on_device,
        mesh=mesh,
        in_specs=(image, token, P("dp"), *[rows] * 10, *[P()] * 6, image),
        out_specs=(image, image, token, *[rows] * 5, both, both, *[rows] * 3, *[P("dp")] * 6),
        check_vma=False,
    )
```

```python
import functools
import jax
import jax.numpy as jnp
from jax import lax
from jax.experimental import pallas as pl
from jax.experimental.pallas import tpu as pltpu
from jax.sharding import PartitionSpec as P

H = 12
LOW = jnp.bfloat16
WIDE = jnp.float32


def contract(a, b, dims):
    return lax.dot_general(a, b, (dims, ((), ())), preferred_element_type=WIDE)


def project(values, weight):
    return contract(values, weight, ((1,), (0,)))


def back_project(grads, weight):
    return contract(grads, weight, ((1,), (1,)))


def weight_grad(left, right):
    return contract(left, right, ((0,), (0,)))


def heads_of(values, images):
    rows, width = values.shape
    return values.reshape(images, rows // images, H, width // H)


def norm_forward(resid, gain, shift):
    center = resid - jnp.mean(resid, axis=-1, keepdims=True)
    inverse = lax.rsqrt(jnp.mean(center * center, axis=-1, keepdims=True) + 1e-05)
    normed = center * inverse
    return (normed * gain + shift, normed, inverse)


def norm_backward(incoming, normed, inverse, gain):
    scaled = incoming * gain
    grad_in = inverse * (
        scaled
        - jnp.mean(scaled, axis=-1, keepdims=True)
        - normed * jnp.mean(scaled * normed, axis=-1, keepdims=True)
    )
    return (grad_in, jnp.sum(incoming * normed, axis=0), jnp.sum(incoming, axis=0))


def scores_of(query, keys):
    return jnp.einsum("bqhe,bkhe->bhqk", query, keys, preferred_element_type=WIDE) * 0.125


def mix(probs, values):
    return jnp.einsum("bhqk,bkhe->bqhe", probs, values, preferred_element_type=WIDE)


def mix_back(probs, grads):
    return jnp.einsum("bhqk,bqhe->bkhe", probs, grads, preferred_element_type=WIDE)


def attention_backward(probs, attn, grad_attn, query, keys, values):
    row = jnp.sum(grad_attn.astype(WIDE) * attn.astype(WIDE), axis=-1).transpose(0, 2, 1)[..., None]
    grad_probs = jnp.einsum("bqhe,bkhe->bhqk", grad_attn, values, preferred_element_type=WIDE)
    grad_scores = (probs * (grad_probs - row)).astype(LOW)
    grad_query = mix(grad_scores, keys) * 0.125
    grad_keys = mix_back(grad_scores, query) * 0.125
    grad_values = mix_back(probs.astype(LOW), grad_attn)
    return (grad_query, grad_keys, grad_values)


def gelu_tanh(values):
    return jax.nn.gelu(values, approximate=True)


def on_device(
    inputs,
    memory,
    lengths,
    self_query,
    self_key,
    self_value,
    self_out,
    cross_query,
    cross_key,
    cross_value,
    cross_out,
    expand_weight,
    contract_weight,
    gain_one,
    shift_one,
    gain_two,
    shift_two,
    gain_three,
    shift_three,
    cotangent,
):
    images, queries, width = inputs.shape
    mem_rows = memory.shape[1]
    rows = images * queries
    share = self_query.shape[0]
    parts = width // share
    squares = (self_query, self_key, self_value, self_out, cross_query, cross_key, cross_value, cross_out)
    packed = lax.all_gather(jnp.stack(squares), "dp", axis=1, tiled=True)
    expand_full = lax.all_gather(expand_weight, "dp", axis=0, tiled=True)
    contract_full = lax.all_gather(contract_weight, "dp", axis=0, tiled=True)
    (query_full, key_full, value_full, out_full, cquery_full, ckey_full, cvalue_full, cout_full) = packed
    tokens = inputs.reshape(rows, width)
    memory_flat = memory.reshape(images * mem_rows, width)
    incoming = cotangent.reshape(rows, width).astype(WIDE)

    def joined(values):
        return values.reshape(-1, width)

    query_heads = heads_of(project(tokens, query_full).astype(LOW), images)
    key_heads = heads_of(project(tokens, key_full).astype(LOW), images)
    value_heads = heads_of(project(tokens, value_full).astype(LOW), images)
    self_raw = scores_of(query_heads, key_heads)
    self_exp = jnp.exp(self_raw - jnp.max(self_raw, axis=-1, keepdims=True))
    self_probs = self_exp / jnp.sum(self_exp, axis=-1, keepdims=True)
    self_attn = joined(mix(self_probs.astype(LOW), value_heads)).astype(LOW)
    first, normed_one, inverse_one = norm_forward(
        tokens.astype(WIDE) + project(self_attn, out_full), gain_one, shift_one
    )
    first_low = first.astype(LOW)
    cross_q = heads_of(project(first_low, cquery_full).astype(LOW), images)
    cross_k = heads_of(project(memory_flat, ckey_full).astype(LOW), images)
    cross_v = heads_of(project(memory_flat, cvalue_full).astype(LOW), images)
    places = lax.axis_index("mem") * mem_rows + jnp.arange(mem_rows, dtype=jnp.int32)
    valid = (places[None, :] < lengths[:, None])[:, None, None, :]
    cross_raw = jnp.where(valid, scores_of(cross_q, cross_k), -1e30)
    top = lax.pmax(jnp.max(cross_raw, axis=-1, keepdims=True), "mem")
    cross_exp = jnp.where(valid, jnp.exp(cross_raw - top), 0.0)
    total = lax.psum(jnp.sum(cross_exp, axis=-1, keepdims=True), "mem")
    cross_probs = cross_exp / total
    cross_attn = lax.psum(joined(mix(cross_probs.astype(LOW), cross_v)).astype(LOW), "mem")
    second, normed_two, inverse_two = norm_forward(
        first + project(cross_attn, cout_full), gain_two, shift_two
    )
    second_low = second.astype(LOW)
    pre_act = project(second_low, expand_full)
    activ, gelu_pull = jax.vjp(gelu_tanh, pre_act)
    activ_low = activ.astype(LOW)
    result, normed_three, inverse_three = norm_forward(
        second + project(activ_low, contract_full), gain_three, shift_three
    )
    grad_three, gain_three_part, shift_three_part = norm_backward(
        incoming, normed_three, inverse_three, gain_three
    )
    grad_ffn = grad_three.astype(LOW)

    def scattered(part, axes="dp"):
        return lax.psum_scatter(part, axes, scatter_dimension=0, tiled=True).astype(WIDE)

    contract_grad = scattered(weight_grad(activ_low, grad_ffn).astype(LOW))
    grad_pre = gelu_pull(back_project(grad_ffn, contract_full))[0].astype(LOW)
    expand_grad = scattered(weight_grad(second_low, grad_pre).astype(LOW))
    grad_second = grad_three + back_project(grad_pre, expand_full)
    grad_two, gain_two_part, shift_two_part = norm_backward(
        grad_second, normed_two, inverse_two, gain_two
    )
    grad_cross = grad_two.astype(LOW)
    cout_part = weight_grad(cross_attn, grad_cross)
    grad_cattn = heads_of(back_project(grad_cross, cout_full).astype(LOW), images)
    part_cquery, grad_ckey, grad_cvalue = attention_backward(
        cross_probs, heads_of(cross_attn, images), grad_cattn, cross_q, cross_k, cross_v
    )
    grad_cquery = lax.psum(joined(part_cquery).astype(LOW), "mem")
    grad_ckey = joined(grad_ckey).astype(LOW)
    grad_cvalue = joined(grad_cvalue).astype(LOW)
    kv_grad = scattered(
        jnp.concatenate(
            [weight_grad(memory_flat, grad_ckey), weight_grad(memory_flat, grad_cvalue)], axis=1
        ).astype(LOW),
        ("dp", "mem"),
    )
    memory_grad = back_project(grad_ckey, ckey_full) + back_project(grad_cvalue, cvalue_full)
    cquery_part = weight_grad(first_low, grad_cquery)
    grad_first = grad_two + back_project(grad_cquery, cquery_full)
    grad_one, gain_one_part, shift_one_part = norm_backward(
        grad_first, normed_one, inverse_one, gain_one
    )
    grad_self = grad_one.astype(LOW)
    out_part = weight_grad(self_attn, grad_self)
    grad_sattn = heads_of(back_project(grad_self, out_full).astype(LOW), images)
    grad_query, grad_key, grad_value = (
        joined(grad).astype(LOW)
        for grad in attention_backward(
            self_probs, heads_of(self_attn, images), grad_sattn, query_heads, key_heads, value_heads
        )
    )
    input_grad = (
        grad_one
        + back_project(grad_query, query_full)
        + back_project(grad_key, key_full)
        + back_project(grad_value, value_full)
    )
    norm_parts = jnp.stack(
        [gain_one_part, shift_one_part, gain_two_part, shift_two_part, gain_three_part, shift_three_part], axis=1
    )
    rest = scattered(
        jnp.concatenate(
            [
                weight_grad(tokens, grad_query),
                weight_grad(tokens, grad_key),
                weight_grad(tokens, grad_value),
                out_part,
                cquery_part,
                cout_part,
                jnp.pad(norm_parts, ((0, 0), (0, 122))),
            ],
            axis=1,
        ).astype(LOW)
    )
    squares_grad = [rest[:, place * width : (place + 1) * width] for place in range(6)]
    norms_grad = [rest[:, 6 * width + place] for place in range(6)]
    return (
        result.reshape(inputs.shape),
        input_grad.reshape(inputs.shape),
        memory_grad.reshape(memory.shape),
        *squares_grad[:5],
        kv_grad[:, :width],
        kv_grad[:, width:],
        squares_grad[5],
        expand_grad,
        contract_grad,
        *norms_grad,
    )


MESH = pl.DeviceIdType.MESH
ANY = pl.BlockSpec(memory_space=pl.ANY)
INNER = pl.BlockSpec(memory_space=pltpu.VMEM)
SCALAR = pl.BlockSpec(memory_space=pltpu.SMEM)
D = 768
FF = 3072
PAIRS = 6
QP = 112
PIECES = 16
SQ, SK, SV, SO, CK, CV, CQ, CO, EX, CT = 0, 1, 2, 3, 4, 5, 6, 7, 8, 12
WINDOW = 2
FIRST_DUE = 7.0
UNIT_TIME = 3.5
EXCHANGE_TIME = 16.0
VMEM_BYTES = 60 * 2**20


def mm(a, b):
    return lax.dot_general(a, b, (((1,), (0,)), ((), ())), preferred_element_type=WIDE)


def mm_nt(a, b):
    return lax.dot_general(a, b, (((1,), (1,)), ((), ())), preferred_element_type=WIDE)


def mm_tn(a, b):
    return lax.dot_general(a, b, (((0,), (0,)), ((), ())), preferred_element_type=WIDE)


def low_lanes(shape):
    return lax.broadcasted_iota(jnp.int32, shape, 1) < 64


def two_heads(pair):
    lower = low_lanes(pair.shape)
    nought = jnp.zeros_like(pair)
    return jnp.concatenate([jnp.where(lower, pair, nought), jnp.where(lower, nought, pair)], axis=0)


def one_pair(both):
    rows = both.shape[0] // 2
    upper = both[rows:]
    return jnp.where(low_lanes(upper.shape), both[:rows], upper)


def places():
    d = lax.axis_index("dp")
    c = lax.rem(d, 2)
    x = lax.rem(d // 2, 2)
    y = d // 4
    other = d + 1 - 2 * c
    beside = d + 2 - 4 * x
    above = d + 4 - 8 * y
    across = beside + 4 - 8 * y
    return d, other, beside, above, across


def weight_row(piece, owner):
    if isinstance(piece, int) and piece >= CT:
        return pl.multiple_of(CT * D + owner * 384 + (piece - CT) * 96, 96)
    return pl.multiple_of(piece * D + owner * 96, 96)


UNITS = ((SQ, SK), (SV,), (CK, CV), (SO,), (CQ,), (CO,), (8,), (9,), (10,), (11,), (12,), (13,), (14,), (15,))
LAG = 2


class Gather:
    def __init__(self, shards, full, local, send, recv, saved, save):
        self.shards, self.full, self.saved, self.save = shards, full, saved, save
        self.local, self.send, self.recv = local, send, recv
        self.d, self.other, self.beside, self.above, self.across = places()
        self.z = lax.axis_index("mem")
        self.q = lax.rem(self.z, 2)
        self.near = self.z + 1 - 2 * self.q
        self.sent = []
        self.role = {}
        self.done = 0
        self.clock = 0.0
        self.landed = [False] * PIECES
        self.unit_of = {piece: place for place, unit in enumerate(UNITS) for piece in unit}

    def at(self, piece, owner):
        return self.full.at[pl.ds(weight_row(piece, owner), 96)]

    def own(self, piece):
        if piece < EX:
            return self.shards[piece]
        if piece < CT:
            return self.shards[EX].at[:, pl.ds((piece - EX) * D, D)]
        return self.shards[EX + 1].at[pl.ds((piece - CT) * 96, 96)]

    def copy(self, src, piece, owner, kind, target, note):
        return pltpu.make_async_remote_copy(
            src,
            self.at(piece, owner),
            self.send.at[piece, note],
            self.recv.at[piece, kind],
            device_id=target,
            device_id_type=MESH,
        )

    def push(self, src, piece, owner, kind, target):
        one = self.copy(src, piece, owner, kind, (target, self.z), kind)
        one.start()
        self.sent.append(one)

    def lend(self, piece, owner, kind):
        one = self.copy(self.at(piece, owner), piece, owner, kind, (self.d, self.near), 7 + kind)
        one.start()
        self.sent.append(one)

    def arrived(self, piece, kind):
        self.copy(self.at(piece, self.d), piece, self.d, kind, (self.other, self.z), kind).wait_recv()

    def roles(self, unit):
        if unit not in self.role:
            first, second = unit
            mine = first + self.q * (second - first)
            self.role[unit] = (mine, first + second - mine)
        return self.role[unit]

    def local_copy(self, piece):
        return pltpu.make_async_copy(self.own(piece), self.at(piece, self.d), self.local.at[piece])

    def start(self, place):
        if place >= len(UNITS):
            return
        unit = UNITS[place]
        if len(unit) == 1:
            piece = unit[0]
            src = self.own(piece)
            self.local_copy(piece).start()
        else:
            piece, theirs = self.roles(unit)
            src = self.at(piece, self.d)
            self.push(self.at(theirs, self.d), theirs, self.d, 3, self.other)
        self.push(src, piece, self.d, 0, self.beside)
        self.push(src, piece, self.d, 1, self.above)
        self.push(src, piece, self.d, 3, self.other)

    def prepare(self):
        for unit in UNITS:
            if len(unit) == 2:
                for piece in unit:
                    self.local_copy(piece).start()

    def begin(self):
        for unit in UNITS:
            if len(unit) == 2:
                for piece in unit:
                    self.local_copy(piece).wait()
        for place in range(WINDOW):
            self.start(place)

    def relay(self, place):
        unit = UNITS[place]
        piece = unit[0] if len(unit) == 1 else self.roles(unit)[0]
        for kind, owner, side, target in ((0, self.beside, 0, self.above), (1, self.above, 1, self.beside)):
            self.arrived(piece, kind)
            if place % 2 == side:
                self.push(self.at(piece, owner), piece, owner, 2, target)
            self.push(self.at(piece, owner), piece, owner, 4 + kind, self.other)
            if len(unit) == 2:
                self.lend(piece, owner, kind)

    def finish(self, place):
        unit = UNITS[place]
        piece = unit[0] if len(unit) == 1 else self.roles(unit)[0]
        self.arrived(piece, 2)
        self.push(self.at(piece, self.across), piece, self.across, 6, self.other)
        if len(unit) == 2:
            self.lend(piece, self.across, 2)

    def borrow(self, place):
        unit = UNITS[place]
        if len(unit) == 2:
            piece = self.roles(unit)[1]
            for kind, owner in enumerate((self.beside, self.above, self.across)):
                self.arrived(piece, kind)
                self.push(self.at(piece, owner), piece, owner, 4 + kind, self.other)

    def step(self):
        place = self.done
        if place >= len(UNITS) + LAG:
            return
        self.done += 1
        if place < len(UNITS):
            self.relay(place)
            self.start(place + WINDOW)
        if 1 <= place <= len(UNITS):
            self.finish(place - 1)
        if place >= LAG:
            self.borrow(place - LAG)

    def due(self, place):
        return FIRST_DUE + UNIT_TIME * place

    def spend(self, time):
        self.wait_for(self.clock + time)

    def wait_for(self, clock):
        self.clock = max(self.clock, clock)
        while self.done < len(UNITS) + LAG and self.due(self.done) <= self.clock:
            self.step()

    def upto(self, count):
        while self.done < min(count, len(UNITS) + LAG):
            self.clock = max(self.clock, self.due(self.done))
            self.step()

    def ready(self, piece):
        place = self.unit_of[piece]
        self.upto(place + 1 + (1 if len(UNITS[place]) == 1 else LAG))
        if self.landed[piece]:
            return
        self.landed[piece] = True
        if len(UNITS[place]) == 1:
            self.local_copy(piece).wait()
        for kind in range(3, 7):
            self.arrived(piece, kind)
        if piece < CT:
            self.save(self.full.at[pl.ds(piece * D, D)], self.saved.at[pl.ds(piece * D, D)])

    def close(self):
        for one in self.sent:
            one.wait_send()


def greet(targets):
    barrier = pltpu.get_barrier_semaphore()
    for target in targets:
        pl.semaphore_signal(barrier, 1, device_id=target, device_id_type=MESH)
    pl.semaphore_wait(barrier, len(targets))


def norm_rows(resid, gain, shift):
    center = resid - jnp.mean(resid, axis=-1, keepdims=True)
    inverse = lax.rsqrt(jnp.mean(center * center, axis=-1, keepdims=True) + 1e-05)
    normed = center * inverse
    return normed * gain + shift, normed, inverse


def forward_kernel(images, queries, mem_rows, *refs):
    (raw, mem, lens, *rest) = refs
    norms, rest = rest[:6], rest[6:]
    shards = rest[:10]
    (o_result, o_full, o_acts, o_ffn, o_us, o_inv, o_kv, o_pc, o_ps, o_wst) = rest[10:20]
    (
        full, acts, ffn, us, inv, kv, pc, ps, wst, tok, wide, stats, osend, orecv, lsend, lrecv, fst,
        local, send, recv, zsend, zrecv, keep,
    ) = rest[20:]
    rows = images * QP
    z = lax.axis_index("mem")
    d = lax.axis_index("dp")
    kept = []

    def save(src, dst):
        one = pltpu.make_async_copy(src, dst, keep.at[len(kept)])
        one.start()
        kept.append(one)

    gather = Gather(shards, full, local, send, recv, o_full, save)
    others = [lax.rem(z + r, 4) for r in range(1, 4)]
    gather.prepare()
    greet(
        [(gather.other, z), (gather.beside, z), (gather.above, z)] + [(d, other) for other in others]
    )
    gather.begin()
    blank = jnp.zeros((QP - queries, D), LOW)
    for i in range(images):
        tok[pl.ds(i * QP, QP), :] = jnp.concatenate([raw[i], blank], axis=0)

    def weight(piece, tile):
        return full[pl.ds(piece * D, D), cols(tile)]

    def cols(tile):
        return pl.ds(pl.multiple_of(tile * 256, 256), 256)

    def image(i):
        return pl.ds(pl.multiple_of(i * QP, QP), QP)

    def project_rows(src, piece, dst, scale):
        def body(tile, carry):
            out = mm(src[...], weight(piece, tile)).astype(LOW)
            if scale != 1.0:
                out = out * jnp.asarray(scale, LOW)
            acts[dst, :, cols(tile)] = out
            return carry

        lax.fori_loop(0, 3, body, 0)

    gather.ready(SQ)
    project_rows(tok, SQ, 0, 0.125)
    gather.ready(SK)
    project_rows(tok, SK, 1, 1.0)
    gather.ready(SV)
    project_rows(tok, SV, 2, 1.0)

    gather.spend(2.0)
    for i in range(images):
        at = image(i)
        valid = lax.broadcasted_iota(jnp.int32, (2 * QP, QP), 1) < queries

        def self_pair(hp, carry):
            lanes = pl.ds(pl.multiple_of(hp * 128, 128), 128)
            scores = mm_nt(two_heads(acts[0, at, lanes]), acts[1, at, lanes])
            scores = jnp.where(valid, scores, -1e30)
            grown = jnp.exp(scores - jnp.max(scores, axis=-1, keepdims=True))
            probs = (grown / jnp.sum(grown, axis=-1, keepdims=True)).astype(LOW)
            ps[i, hp] = probs
            acts[3, at, lanes] = one_pair(mm(probs, acts[2, at, lanes])).astype(LOW)
            return carry

        lax.fori_loop(0, PAIRS, self_pair, 0)
        gather.spend(1.0)

    def memory_rows(piece, dst):
        for tile in range(3):
            kv[dst, :, cols(tile)] = mm(mem[...], weight(piece, tile)).astype(LOW)
            gather.spend(0.7)

    def add_branch(src, piece, base):
        def body(tile, carry):
            wide[0, :, cols(tile)] = base(cols(tile)) + mm(acts[src], weight(piece, tile))
            return carry

        lax.fori_loop(0, 3, body, 0)

    def normalize(which, low_dst):
        def body(i, carry):
            at = image(i)
            gain, shift = norms[2 * which][...][None, :], norms[2 * which + 1][...][None, :]
            out, normed, inverse = norm_rows(wide[0, at, :], gain, shift)
            us[which, at, :] = normed
            lane = lax.broadcasted_iota(jnp.int32, (QP, 128), 1)
            inv[at, :] = jnp.where(lane == which, inverse, inv[at, :])
            wide[1, at, :] = out
            if low_dst is not None:
                acts[low_dst, at, :] = out.astype(LOW)
            return carry

        lax.fori_loop(0, images, body, 0)

    inv[...] = jnp.zeros_like(inv)
    gather.ready(SO)
    add_branch(3, SO, lambda at: tok[:, at].astype(WIDE))
    normalize(0, 4)
    gather.spend(1.6)
    save(us.at[0], o_us.at[0])
    gather.ready(CK)
    memory_rows(CK, 0)
    gather.ready(CV)
    memory_rows(CV, 1)
    save(kv, o_kv)
    save(ps, o_ps)
    gather.ready(CQ)
    project_rows(acts.at[4], CQ, 5, 0.125)

    pushed = []

    def pass_on(src, dst, kind, r):
        one = pltpu.make_async_remote_copy(
            src, dst, zsend.at[kind, r - 1], zrecv.at[kind, r - 1],
            device_id=(d, others[r - 1]), device_id_type=MESH,
        )
        one.start()
        pushed.append(one)

    def taken(ref, kind, r):
        pltpu.make_async_remote_copy(
            ref, ref, zsend.at[kind, r - 1], zrecv.at[kind, r - 1],
            device_id=(d, others[r - 1]), device_id_type=MESH,
        ).wait_recv()

    lane = lax.broadcasted_iota(jnp.int32, (QP, 128), 1)

    def turned(tall):
        return jnp.concatenate([tall, jnp.zeros((128 - QP, 128), WIDE)], axis=0).T[:16]

    def returned(flat):
        return jnp.concatenate([flat, jnp.zeros((112, 128), WIDE)], axis=0).T[:QP]

    for turn in range(4):
        i = others[turn] if turn < 3 else z
        at = image(i)
        tokens = pl.ds(pl.multiple_of(i * mem_rows, mem_rows), mem_rows)
        place = z * mem_rows + lax.broadcasted_iota(jnp.int32, (2 * QP, mem_rows), 1)
        valid = place < lens[i]

        def pair(hp, noted):
            lanes = pl.ds(pl.multiple_of(hp * 128, 128), 128)
            scores = mm_nt(two_heads(acts[5, at, lanes]), kv[0, tokens, lanes])
            scores = jnp.where(valid, scores, -1e30)
            top = jnp.max(scores, axis=-1, keepdims=True)
            grown = jnp.where(valid, jnp.exp(scores - top), 0.0)
            total = jnp.sum(grown, axis=-1, keepdims=True)
            shrink = jnp.where(total > 0.0, 1.0 / total, 0.0)
            probs = grown.astype(LOW)
            pc[i, hp] = probs
            osend[turn, :, lanes] = one_pair(mm(probs, kv[1, tokens, lanes]) * shrink).astype(LOW)
            for half in range(2):
                span = slice(half * QP, half * QP + QP)
                noted = jnp.where(lane == 2 * hp + half, top[span], noted)
                noted = jnp.where(lane == 64 + 2 * hp + half, total[span], noted)
            return noted

        noted = lax.fori_loop(0, PAIRS, pair, jnp.zeros((QP, 128), WIDE))
        stats[i] = noted
        total = pltpu.roll(noted, 64, 1)
        lsend[turn] = turned(jnp.where(total > 0.0, noted + jnp.log(total), -1e30))
        if turn < 3:
            pass_on(osend.at[turn], orecv.at[turn], 0, turn + 1)
            pass_on(lsend.at[turn], lrecv.at[turn], 1, turn + 1)
        gather.spend(1.9)
    save(pc, o_pc)
    gather.wait_for(gather.clock + EXCHANGE_TIME - 5.0)
    for r in range(1, 4):
        taken(orecv.at[r - 1], 0, r)
        taken(lrecv.at[r - 1], 1, r)
    noted = [lsend[3], lrecv[0], lrecv[1], lrecv[2]]
    top = functools.reduce(jnp.maximum, noted)
    level = top + jnp.log(sum(jnp.exp(one - top) for one in noted))
    fst[z] = level
    share = [returned(jnp.exp(one - level)) for one in noted]
    lower = low_lanes((QP, 128))
    mine = image(z)
    for hp in range(PAIRS):
        lanes = pl.ds(hp * 128, 128)
        joined = jnp.zeros((QP, 128), WIDE)
        for r in range(4):
            spread = jnp.where(
                lower, share[r][:, 2 * hp : 2 * hp + 1], share[r][:, 2 * hp + 1 : 2 * hp + 2]
            )
            part = osend[3, :, lanes] if r == 0 else orecv[r - 1, :, lanes]
            joined = joined + spread * part.astype(WIDE)
        acts[6, mine, lanes] = joined.astype(LOW)
    for r in range(1, 4):
        pass_on(acts.at[6, mine], acts.at[6, mine], 2, r)
        pass_on(fst.at[z], fst.at[z], 3, r)
    gather.wait_for(gather.clock + EXCHANGE_TIME)
    gather.ready(CO)
    for r in range(1, 4):
        back = lax.rem(z + 4 - r, 4)
        taken(acts.at[6, image(back)], 2, r)
        taken(fst.at[back], 3, r)
    for i in range(images):
        wst[i] = jnp.exp(stats[i] - returned(fst[i]))
    save(wst, o_wst)
    add_branch(6, CO, lambda at: wide[1, :, at])
    normalize(1, 7)
    save(us.at[1], o_us.at[1])
    save(acts, o_acts)

    def expand(block):
        def body(tile, carry):
            pre = mm(acts[7], full[pl.ds((EX + block) * D, D), cols(tile)])
            root = 0.7978845608028654
            square = pre * pre
            bend = jnp.tanh(root * (pre + 0.044715 * (pre * square)))
            half = 0.5 * (1.0 + bend)
            slope = half + (0.5 * root) * pre * (1.0 - bend * bend) * (1.0 + 0.134145 * square)
            at = pl.ds(pl.multiple_of(block * D + tile * 256, 256), 256)
            ffn[0, :, at] = (pre * half).astype(LOW)
            ffn[1, :, at] = slope.astype(LOW)
            return carry

        lax.fori_loop(0, 3, body, 0)

    for block in range(4):
        gather.ready(EX + block)
        expand(block)
        gather.spend(1.2)
    save(ffn, o_ffn)
    for block in range(4):
        gather.ready(CT + block)
    save(full.at[pl.ds(CT * D, FF)], o_full.at[pl.ds(CT * D, FF)])

    def contract(tile, carry):
        wide[0, :, cols(tile)] = wide[1, :, cols(tile)] + mm(
            ffn[0], full[pl.ds(CT * D, FF), cols(tile)]
        )
        return carry

    lax.fori_loop(0, 3, contract, 0)
    normalize(2, None)
    save(wide.at[1], o_result)
    save(us.at[2], o_us.at[2])
    save(inv, o_inv)
    for one in pushed:
        one.wait_send()
    gather.close()
    for one in kept:
        one.wait()


def forward(tok, mem, lens, norms, shards, images, queries, mem_rows):
    rows = images * QP
    shape = jax.ShapeDtypeStruct
    tokens = images * mem_rows
    outs = (
        shape((rows, D), WIDE),
        shape((PIECES * D, D), LOW),
        shape((8, rows, D), LOW),
        shape((2, rows, FF), LOW),
        shape((3, rows, D), WIDE),
        shape((rows, 128), WIDE),
        shape((2, tokens, D), LOW),
        shape((images, PAIRS, 2 * QP, mem_rows), LOW),
        shape((images, PAIRS, 2 * QP, QP), LOW),
        shape((images, QP, 128), WIDE),
    )
    dma = pltpu.SemaphoreType.DMA
    return pl.pallas_call(
        functools.partial(forward_kernel, images, queries, mem_rows),
        out_shape=outs,
        in_specs=[INNER, INNER, SCALAR] + [INNER] * 6 + [ANY] * 10,
        out_specs=[ANY] * len(outs),
        scratch_shapes=[
            *[pltpu.VMEM(one.shape, one.dtype) for one in outs[1:]],
            pltpu.VMEM((rows, D), LOW),
            pltpu.VMEM((2, rows, D), WIDE),
            pltpu.VMEM((images, QP, 128), WIDE),
            pltpu.VMEM((4, QP, D), LOW),
            pltpu.VMEM((3, QP, D), LOW),
            pltpu.VMEM((4, 16, 128), WIDE),
            pltpu.VMEM((3, 16, 128), WIDE),
            pltpu.VMEM((images, 16, 128), WIDE),
            dma((PIECES,)),
            dma((PIECES, 10)),
            dma((PIECES, 7)),
            dma((4, 3)),
            dma((4, 3)),
            dma((28,)),
        ],
        compiler_params=pltpu.CompilerParams(
            collective_id=0, has_side_effects=True, vmem_limit_bytes=VMEM_BYTES
        ),
        name="forward",
    )(tok, mem, lens, *norms, *(shards[place] for place in (0, 1, 2, 3, 5, 6, 4, 7, 8, 9)))


def rows_of_image(i):
    return pl.ds(pl.multiple_of(i * QP, QP), QP)


def cols_of_tile(tile):
    return pl.ds(pl.multiple_of(tile * 256, 256), 256)


class Reduce:
    def __init__(self, where, turn, grad, core_in, chip_in, core_sems, chip_sems):
        self.where, self.turn = where, turn
        self.grad, self.core_in, self.chip_in = grad, core_in, chip_in
        self.core_sems, self.chip_sems = core_sems, chip_sems
        self.sent = []
        d, other, beside, above, across = where
        self.c = lax.rem(d, 2)
        self.z = lax.axis_index("mem")

    def copy(self, src, dst, sems, place, target):
        return pltpu.make_async_remote_copy(
            src, dst, sems.at[0, self.turn, place], sems.at[1, self.turn, place],
            device_id=(target, self.z), device_id_type=MESH,
        )

    def core_stage(self):
        one = self.copy(self.grad.at[1 - self.c], self.core_in, self.core_sems, 0, self.where[1])
        one.start()
        self.sent.append(one)

    def chip_stage(self):
        self.copy(self.core_in, self.core_in, self.core_sems, 0, self.where[1]).wait_recv()
        for chip in range(4):
            both = self.grad[self.c, chip].astype(WIDE) + self.core_in[chip].astype(WIDE)
            self.grad[self.c, chip] = both.astype(LOW)
        for place, target in enumerate(self.where[2:]):
            one = self.copy(
                self.grad.at[self.c, target // 2], self.chip_in.at[place], self.chip_sems, place, target
            )
            one.start()
            self.sent.append(one)

    def total(self):
        own = self.grad[self.c, self.where[0] // 2].astype(WIDE)
        for place, target in enumerate(self.where[2:]):
            self.copy(
                self.chip_in.at[place], self.chip_in.at[place], self.chip_sems, place, target
            ).wait_recv()
            own = own + self.chip_in[place].astype(WIDE)
        return own

    def settle(self):
        for one in self.sent:
            one.wait_send()
        self.sent = []


def backward_kernel(images, queries, mem_rows, *refs):
    (
        h_gain_one, h_gain_two, h_gain_three, h_cot, h_tok, h_mem, h_full, h_acts, h_ffn, h_us, h_inv, h_kv, h_pc, h_ps, h_wst,
    ) = refs[:15]
    (o_expand, o_contract, o_co, o_mid, o_late, o_last, o_keys, o_mem, o_in, o_norms) = refs[15:25]
    (
        cot, tok, mem, slots, acts, ffn, us, inv, kv, pc, ps, wst, wide, grads, nsum, nin,
        zsend, zin, mout,
        g_expand, g_contract, g_co, g_mid, g_late, g_last, c_expand, c_contract, c_co, c_mid, c_late, c_last, c_keys,
        t_expand, t_contract, t_co, t_mid, t_late, t_last, t_keys,
        f_expand, f_contract, f_co, f_mid, f_late, f_last, k_out, k_in,
        load, slot_sems, pc_sems, mout_sems, core_sems, chip_sems, fin_sems, local_sems, ksems, zsems, nsems,
    ) = refs[25:]
    z = lax.axis_index("mem")
    d = lax.axis_index("dp")
    where = places()
    q = lax.rem(z, 2)
    zp = z + 1 - 2 * q
    others = [lax.rem(z + r, 4) for r in range(1, 4)]
    dpeers = [lax.rem(d + r, 8) for r in range(1, 8)]

    gains = (h_gain_one, h_gain_two, h_gain_three)
    loads = {}
    waited = set()

    def fetch(name, src, dst):
        one = pltpu.make_async_copy(src, dst, load.at[len(loads)])
        one.start()
        loads[name] = one

    order = [CT, CT + 1, CT + 2, CT + 3, EX, EX + 1, EX + 2, EX + 3, CO, CK, CV, CQ, SO, SQ, SK, SV]
    depth = 4

    def slot_copy(turn):
        return pltpu.make_async_copy(
            h_full.at[pl.ds(order[turn] * D, D)], slots.at[turn % depth], slot_sems.at[turn % depth]
        )

    def prefetch(turn):
        if turn < len(order):
            slot_copy(turn).start()

    fetch("cot", h_cot, cot)
    fetch("u3", h_us.at[2], us.at[0])
    fetch("inv", h_inv, inv)
    prefetch(0)
    fetch("gp", h_ffn.at[1], ffn.at[1])

    def have(name):
        if name not in waited:
            waited.add(name)
            loads[name].wait()

    def pc_copy(turn):
        i = lax.rem(z + turn + 1, 4)
        return pltpu.make_async_copy(h_pc.at[i], pc.at[turn % 2], pc_sems.at[turn % 2])

    greet([(peer, z) for peer in dpeers] + [(d, other) for other in others])

    nsum[...] = jnp.zeros_like(nsum)

    def norm_back(which, incoming, slot, low_dst):
        def body(i, carry):
            at = rows_of_image(i)
            above = incoming(at)
            unit = us[slot, at, :]
            inverse = inv[at, which : which + 1]
            scaled = above * gains[which][...][None, :]
            first = jnp.mean(scaled, axis=-1, keepdims=True)
            second = jnp.mean(scaled * unit, axis=-1, keepdims=True)
            grad = inverse * (scaled - first - unit * second)
            wide[0, at, :] = grad
            grads[low_dst, at, :] = grad.astype(LOW)
            row = 2 * which
            nsum[row : row + 1, :] += jnp.sum(above * unit, axis=0, keepdims=True)
            nsum[row + 1 : row + 2, :] += jnp.sum(above, axis=0, keepdims=True)
            return carry

        lax.fori_loop(0, images, body, 0)

    turn_of = {piece: turn for turn, piece in enumerate(order)}

    def slot(piece):
        turn = turn_of[piece]
        slot_copy(turn).wait()
        return slots.at[turn % depth]

    def freed(piece):
        prefetch(turn_of[piece] + depth)

    for name in ("cot", "inv", "u3"):
        have(name)
    norm_back(2, lambda at: cot[at, :].astype(WIDE), 0, 0)
    for turn in range(1, depth):
        prefetch(turn)
    fetch("second_low", h_acts.at[7], acts.at[7])
    have("gp")
    for block in range(4):
        weight = slot(CT + block)

        def body(tile, carry):
            at = pl.ds(pl.multiple_of(block * D + tile * 256, 256), 256)
            back = mm_nt(grads[0], weight[cols_of_tile(tile), :])
            ffn[1, :, at] = (back * ffn[1, :, at].astype(WIDE)).astype(LOW)
            return carry

        lax.fori_loop(0, 3, body, 0)
        freed(CT + block)

    def reduce_at(place, grad, core_in, chip_in):
        return Reduce(where, place, grad, core_in, chip_in, core_sems, chip_sems)

    fetch("u2", h_us.at[1], us.at[1])
    fetch("kv", h_kv, kv)
    fetch("wst", h_wst, wst)
    fetch("acts", h_acts.at[pl.ds(0, 7)], acts.at[pl.ds(0, 7)])
    pc_copy(0).start()
    pc_copy(1).start()
    have("second_low")
    r_expand = reduce_at(0, g_expand, c_expand, t_expand)

    def expand_part(tile, carry):
        at = pl.ds(pl.multiple_of(q * 1536 + tile * 256, 256), 256)
        out = mm_tn(acts[7], ffn[1, :, at]).astype(LOW)
        for e in range(8):
            g_expand[e % 2, e // 2, :, cols_of_tile(tile)] = out[96 * e : 96 * e + 96]
        return carry

    lax.fori_loop(0, 6, expand_part, 0)
    r_expand.core_stage()
    for block in range(4):
        weight = slot(EX + block)

        def body(tile, carry):
            at = cols_of_tile(tile)
            back = mm_nt(ffn[1, :, pl.ds(block * D, D)], weight[at, :])
            wide[0, :, at] = wide[0, :, at] + back
            return carry

        lax.fori_loop(0, 3, body, 0)
        freed(EX + block)
        if block == 2:
            r_expand.chip_stage()
    have("u2")
    norm_back(1, lambda at: wide[0, at, :], 1, 1)

    def through(src, piece, dst):
        weight = slot(piece)

        def body(tile, carry):
            grads[dst, :, cols_of_tile(tile)] = mm_nt(grads[src], weight[cols_of_tile(tile), :]).astype(LOW)
            return carry

        lax.fori_loop(0, 3, body, 0)
        freed(piece)

    fetch("act", h_ffn.at[0], ffn.at[0])
    fetch("mem", h_mem, mem)
    fetch("u1", h_us.at[0], us.at[0])
    fetch("ps", h_ps, ps)
    fetch("tok", h_tok, tok)
    through(1, CO, 2)
    have("kv")
    have("wst")
    have("acts")
    pushed = []

    def across_mem(src, dst, kind, r):
        return pltpu.make_async_remote_copy(
            src, dst, zsems.at[0, kind, r - 1], zsems.at[1, kind, r - 1],
            device_id=(d, others[r - 1]), device_id_type=MESH,
        )

    for turn in range(4):
        i = lax.rem(z + turn + 1, 4)
        pc_copy(turn).wait()
        at = rows_of_image(i)
        tokens = pl.ds(pl.multiple_of(i * mem_rows, mem_rows), mem_rows)
        factors = wst[i]

        def pair(hp, carry):
            lanes = pl.ds(pl.multiple_of(hp * 128, 128), 128)
            query = two_heads(acts[5, at, lanes])
            above = two_heads(grads[2, at, lanes])
            attn = acts[6, at, lanes].astype(WIDE)
            row = jnp.sum(above.astype(WIDE) * jnp.concatenate([attn, attn], axis=0), axis=-1, keepdims=True)
            lane = lax.broadcasted_iota(jnp.int32, (QP, 128), 1)
            factor = jnp.concatenate(
                [
                    jnp.sum(jnp.where(lane == 2 * hp + half, factors, 0.0), axis=-1, keepdims=True)
                    for half in range(2)
                ],
                axis=0,
            )
            probs = pc[turn % 2, hp].astype(WIDE) * factor
            keys, values = kv[0, tokens, lanes], kv[1, tokens, lanes]
            inner = mm_nt(above, values)
            scores = (probs * (inner - row)).astype(LOW)
            zsend[turn, :, lanes] = (one_pair(mm(scores, keys)) * 0.125).astype(LOW)
            kv[0, tokens, lanes] = mm_tn(scores, query).astype(LOW)
            kv[1, tokens, lanes] = mm_tn(probs.astype(LOW), above).astype(LOW)
            return carry

        lax.fori_loop(0, PAIRS, pair, 0)
        if turn < 2:
            pc_copy(turn + 2).start()
        if turn < 3:
            one = across_mem(zsend.at[turn], zin.at[turn], 0, turn + 1)
            one.start()
            pushed.append(one)
        if turn == 1:
            have("act")
            r_contract = reduce_at(1, g_contract, c_contract, t_contract)

            def contract_part(e, carry):
                at = pl.ds(pl.multiple_of(e * 384, 384), 384)
                half = pl.ds(pl.multiple_of(q * 384, 384), 384)
                g_contract[lax.rem(e, 2), e // 2] = mm_tn(ffn[0, :, at], grads[0, :, half]).astype(LOW)
                return carry

            lax.fori_loop(0, 8, contract_part, 0)
            r_contract.core_stage()
        if turn == 3:
            r_contract.chip_stage()

    have("mem")
    f_expand[...] = r_expand.total().astype(LOW)
    r_expand.settle()
    r_keys = reduce_at(2, g_expand, c_keys, t_keys)

    def key_parts(which):
        def key_part(tile, carry):
            out = mm_tn(mem[...], kv[which, :, cols_of_tile(tile)]).astype(LOW)
            at = pl.ds(pl.multiple_of(which * D + tile * 256, 256), 256)
            for e in range(8):
                g_expand[e % 2, e // 2, :, at] = out[96 * e : 96 * e + 96]
            return carry

        lax.fori_loop(0, 3, key_part, 0)

    key_parts(0)
    for r in range(1, 4):
        across_mem(zin.at[r - 1], zin.at[r - 1], 0, r).wait_recv()
    mine = rows_of_image(z)
    grads[3, mine, :] = (
        zsend[3].astype(WIDE) + zin[0].astype(WIDE) + zin[1].astype(WIDE) + zin[2].astype(WIDE)
    ).astype(LOW)
    for r in range(1, 4):
        one = across_mem(grads.at[3, mine], grads.at[3, mine], 1, r)
        one.start()
        pushed.append(one)
    key_parts(1)
    r_keys.core_stage()

    def finals(fin, out, place):
        pltpu.make_async_copy(fin, out, local_sems.at[place]).start()
        one = pltpu.make_async_remote_copy(
            fin, out, fin_sems.at[0, place], fin_sems.at[1, place], device_id=(d, zp), device_id_type=MESH
        )
        one.start()
        return one

    ended = []
    key_weight, value_weight = slot(CK), slot(CV)
    for i in range(images):
        at = pl.ds(i * mem_rows, mem_rows)
        if i >= 2:
            pltpu.make_async_copy(mout.at[i % 2], o_mem.at[at], mout_sems.at[i % 2]).wait()

        def body(tile, carry):
            span = cols_of_tile(tile)
            mout[i % 2, :, span] = (
                mm_nt(kv[0, at, :], key_weight[span, :]) + mm_nt(kv[1, at, :], value_weight[span, :])
            ).astype(LOW)
            return carry

        lax.fori_loop(0, 3, body, 0)
        pltpu.make_async_copy(mout.at[i % 2], o_mem.at[at], mout_sems.at[i % 2]).start()
        if i == 1:
            r_keys.chip_stage()
    freed(CK)
    freed(CV)
    def wide_parts(place, grad, core_in, chip_in, left, right, tiles):
        def body(tile, carry):
            out = mm_tn(left(), right(cols_of_tile(tile))).astype(LOW)
            for e in range(8):
                grad[e % 2, e // 2, :, cols_of_tile(tile)] = out[96 * e : 96 * e + 96]
            return carry

        lax.fori_loop(0, tiles, body, 0)

    def half_parts(grad, left, right):
        half = pl.ds(pl.multiple_of(q * 384, 384), 384)
        out = mm_tn(left, right(half)).astype(LOW)
        for e in range(8):
            grad[e % 2, e // 2] = out[96 * e : 96 * e + 96]

    r_co = reduce_at(3, g_co, c_co, t_co)
    half_parts(g_co, acts[6], lambda at: grads[1, :, at])
    r_co.core_stage()
    for r in range(1, 4):
        back = lax.rem(z + 4 - r, 4)
        across_mem(grads.at[3, rows_of_image(back)], grads.at[3, rows_of_image(back)], 1, r).wait_recv()
    r_co.chip_stage()
    ended.append(finals(f_expand, o_expand.at[q], 0))

    def add_back(src, piece):
        weight = slot(piece)

        def body(tile, carry):
            span = cols_of_tile(tile)
            wide[0, :, span] = wide[0, :, span] + mm_nt(src(), weight[span, :])
            return carry

        lax.fori_loop(0, 3, body, 0)
        freed(piece)

    add_back(lambda: grads[3], CQ)
    have("u1")
    norm_back(0, lambda at: wide[0, at, :], 0, 2)
    for r in range(1, 8):
        one = pltpu.make_async_remote_copy(
            nsum, nin.at[r - 1], nsems.at[0, r - 1], nsems.at[1, r - 1],
            device_id=(dpeers[r - 1], z), device_id_type=MESH,
        )
        one.start()
        pushed.append(one)
    have("tok")

    def either(place, grad, core_in, chip_in, lefts, rights):
        reducer = reduce_at(place, grad, core_in, chip_in)
        for parity in range(2):

            @pl.when(q == parity)
            def _():
                wide_parts(place, grad, core_in, chip_in, lefts[parity], rights[parity], 3)

        reducer.core_stage()
        return reducer

    r_mid = either(
        4, g_mid, c_mid, t_mid,
        (lambda: acts[4], lambda: acts[3]),
        (lambda at: grads[3, :, at], lambda at: grads[2, :, at]),
    )
    through(2, SO, 0)
    have("ps")
    r_mid.chip_stage()
    f_contract[...] = r_contract.total().astype(LOW)
    ended.append(finals(f_contract, o_contract.at[q], 1))

    def self_image(i, carry):
        at = rows_of_image(i)
        for hp in range(PAIRS):
            lanes = pl.ds(hp * 128, 128)
            query = two_heads(acts[0, at, lanes])
            above = two_heads(grads[0, at, lanes])
            attn = acts[3, at, lanes].astype(WIDE)
            row = jnp.sum(above.astype(WIDE) * jnp.concatenate([attn, attn], axis=0), axis=-1, keepdims=True)
            probs = ps[i, hp]
            keys, values = acts[1, at, lanes], acts[2, at, lanes]
            inner = mm_nt(above, values)
            scores = (probs.astype(WIDE) * (inner - row)).astype(LOW)
            acts[0, at, lanes] = (one_pair(mm(scores, keys)) * 0.125).astype(LOW)
            acts[1, at, lanes] = mm_tn(scores, query).astype(LOW)
            acts[2, at, lanes] = mm_tn(probs, above).astype(LOW)
        return carry

    lax.fori_loop(0, images, self_image, 0)
    r_late = either(
        5, g_late, c_late, t_late,
        (lambda: tok[...], lambda: tok[...]),
        (lambda at: acts[0, :, at], lambda at: acts[2, :, at]),
    )
    r_last = reduce_at(6, g_last, c_last, t_last)
    half_parts(g_last, tok[...], lambda at: acts[1, :, at])
    r_last.core_stage()
    r_late.chip_stage()
    r_last.chip_stage()
    quarter = 24
    keys_total = r_keys.total()
    for part in range(4):
        k_out[part] = keys_total[quarter * part : quarter * part + quarter].astype(LOW)
    for r in range(1, 4):
        one = pltpu.make_async_remote_copy(
            k_out.at[others[r - 1]], k_in.at[r - 1], ksems.at[0, r - 1], ksems.at[1, r - 1],
            device_id=(d, others[r - 1]), device_id_type=MESH,
        )
        one.start()
        pushed.append(one)
    f_co[...] = r_co.total().astype(LOW)
    ended.append(finals(f_co, o_co.at[q], 2))
    f_mid[...] = r_mid.total().astype(LOW)
    ended.append(finals(f_mid, o_mid.at[q], 3))
    add_back(lambda: acts[0], SQ)
    add_back(lambda: acts[1], SK)
    add_back(lambda: acts[2], SV)
    pltpu.make_async_copy(wide.at[0], o_in, load.at[15]).start()
    f_late[...] = r_late.total().astype(LOW)
    ended.append(finals(f_late, o_late.at[q], 4))
    f_last[...] = r_last.total().astype(LOW)
    ended.append(finals(f_last, o_last.at[q], 5))
    sums = nsum[...]
    for r in range(1, 8):
        pltpu.make_async_remote_copy(
            nsum, nin.at[r - 1], nsems.at[0, r - 1], nsems.at[1, r - 1],
            device_id=(dpeers[r - 1], z), device_id_type=MESH,
        ).wait_recv()
        sums = sums + nin[r - 1]
    o_norms[...] = sums
    total = k_out[z].astype(WIDE)
    for r in range(1, 4):
        pltpu.make_async_remote_copy(
            k_in.at[r - 1], k_in.at[r - 1], ksems.at[0, r - 1], ksems.at[1, r - 1],
            device_id=(d, others[r - 1]), device_id_type=MESH,
        ).wait_recv()
        total = total + k_in[r - 1].astype(WIDE)
    o_keys[...] = total
    for i in range(2, 4):
        at = pl.ds(i * mem_rows, mem_rows)
        pltpu.make_async_copy(mout.at[i % 2], o_mem.at[at], mout_sems.at[i % 2]).wait()
    pltpu.make_async_copy(wide.at[0], o_in, load.at[15]).wait()
    fins = (f_expand, f_contract, f_co, f_mid, f_late, f_last)
    outs = [(out.at[q], out.at[1 - q]) for out in (o_expand, o_contract, o_co, o_mid, o_late, o_last)]
    for place, (fin, (out, theirs)) in enumerate(zip(fins, outs)):
        pltpu.make_async_copy(fin, out, local_sems.at[place]).wait()
        ended[place].wait_send()
        pltpu.make_async_remote_copy(
            fin, theirs, fin_sems.at[0, place], fin_sems.at[1, place], device_id=(d, zp), device_id_type=MESH
        ).wait_recv()
    for one in pushed:
        one.wait_send()
    for reducer in (r_contract, r_keys, r_co, r_mid, r_late, r_last):
        reducer.settle()


def backward(gains, cot, tok, mem, saved, images, queries, mem_rows):
    full, acts, ffn, us, inv, kv, pc, ps, wst = saved
    rows = images * QP
    tokens = images * mem_rows
    shape = jax.ShapeDtypeStruct
    outs = (
        shape((2, 96, 1536), LOW),
        shape((2, 384, 384), LOW),
        shape((2, 96, 384), LOW),
        shape((2, 96, D), LOW),
        shape((2, 96, D), LOW),
        shape((2, 96, 384), LOW),
        shape((24, 1536), WIDE),
        shape((tokens, D), LOW),
        shape((rows, D), WIDE),
        shape((8, D), WIDE),
    )
    dma = pltpu.SemaphoreType.DMA
    vmem = pltpu.VMEM
    return pl.pallas_call(
        functools.partial(backward_kernel, images, queries, mem_rows),
        out_shape=outs,
        in_specs=[INNER] * 3 + [ANY] * 12,
        out_specs=[ANY] * 6 + [INNER] + [ANY] * 2 + [INNER],
        scratch_shapes=[
            vmem((rows, D), LOW),
            vmem((rows, D), LOW),
            vmem((tokens, D), LOW),
            vmem((4, D, D), LOW),
            vmem((8, rows, D), LOW),
            vmem((2, rows, FF), LOW),
            vmem((2, rows, D), WIDE),
            vmem((rows, 128), WIDE),
            vmem((2, tokens, D), LOW),
            vmem((2, PAIRS, 2 * QP, mem_rows), LOW),
            vmem((images, PAIRS, 2 * QP, QP), LOW),
            vmem((images, QP, 128), WIDE),
            vmem((1, rows, D), WIDE),
            vmem((4, rows, D), LOW),
            vmem((8, D), WIDE),
            vmem((7, 8, D), WIDE),
            vmem((4, QP, D), LOW),
            vmem((3, QP, D), LOW),
            vmem((2, mem_rows, D), LOW),
            vmem((2, 4, 96, 1536), LOW),
            vmem((2, 4, 384, 384), LOW),
            vmem((2, 4, 96, 384), LOW),
            vmem((2, 4, 96, D), LOW),
            vmem((2, 4, 96, D), LOW),
            vmem((2, 4, 96, 384), LOW),
            vmem((4, 96, 1536), LOW),
            vmem((4, 384, 384), LOW),
            vmem((4, 96, 384), LOW),
            vmem((4, 96, D), LOW),
            vmem((4, 96, D), LOW),
            vmem((4, 96, 384), LOW),
            vmem((4, 96, 1536), LOW),
            vmem((3, 96, 1536), LOW),
            vmem((3, 384, 384), LOW),
            vmem((3, 96, 384), LOW),
            vmem((3, 96, D), LOW),
            vmem((3, 96, D), LOW),
            vmem((3, 96, 384), LOW),
            vmem((3, 96, 1536), LOW),
            vmem((96, 1536), LOW),
            vmem((384, 384), LOW),
            vmem((96, 384), LOW),
            vmem((96, D), LOW),
            vmem((96, D), LOW),
            vmem((96, 384), LOW),
            vmem((4, 24, 1536), LOW),
            vmem((3, 24, 1536), LOW),
            dma((16,)),
            dma((4,)),
            dma((2,)),
            dma((2,)),
            dma((2, 7, 1)),
            dma((2, 7, 3)),
            dma((2, 6)),
            dma((6,)),
            dma((2, 3)),
            dma((2, 2, 3)),
            dma((2, 7)),
        ],
        compiler_params=pltpu.CompilerParams(
            collective_id=1, has_side_effects=True, vmem_limit_bytes=VMEM_BYTES
        ),
        name="backward",
    )(*gains, cot, tok, mem, *saved)


def fused_on_device(
    inputs,
    memory,
    lengths,
    self_query,
    self_key,
    self_value,
    self_out,
    cross_query,
    cross_key,
    cross_value,
    cross_out,
    expand_weight,
    contract_weight,
    gain_one,
    shift_one,
    gain_two,
    shift_two,
    gain_three,
    shift_three,
    cotangent,
):
    images, queries, width = inputs.shape
    mem_rows = memory.shape[1]
    norms = (gain_one, shift_one, gain_two, shift_two, gain_three, shift_three)
    shards = (self_query, self_key, self_value, self_out, cross_query, cross_key, cross_value, cross_out, expand_weight, contract_weight)

    def padded(values):
        wider = jnp.pad(values, ((0, 0), (0, QP - queries), (0, 0)))
        return wider.reshape(images * QP, width)

    def cut(values):
        return values.reshape(images, QP, width)[:, :queries]

    tokens = padded(inputs)
    memory_flat = memory.reshape(images * mem_rows, width)
    result, full, acts, ffn, us, inv, kv, pc, ps, wst = forward(
        inputs, memory_flat, lengths, norms, shards, images, queries, mem_rows
    )
    spread, contracted, co, mid, late, last, keys, memory_grad, input_grad, sums = backward(
        norms[::2], padded(cotangent), tokens, memory_flat, (full, acts, ffn, us, inv, kv, pc, ps, wst),
        images, queries, mem_rows,
    )
    share = self_query.shape[0]
    sums = lax.dynamic_slice(sums, (0, lax.axis_index("dp") * share), (8, share))

    def beside(halves):
        return jnp.concatenate([halves[0], halves[1]], axis=1).astype(WIDE)

    return (
        cut(result),
        cut(input_grad),
        memory_grad.reshape(memory.shape).astype(WIDE),
        late[0].astype(WIDE),
        beside(last),
        late[1].astype(WIDE),
        mid[1].astype(WIDE),
        mid[0].astype(WIDE),
        keys[:, :width],
        keys[:, width:],
        beside(co),
        beside(spread),
        beside(contracted),
        *[sums[place] for place in range(6)],
    )


def solution(mesh):
    fused = mesh.shape["dp"] == 8 and mesh.shape["mem"] == 4

    rows = P("dp", None)
    image = P("dp", None, None)
    token = P("dp", "mem", None)
    both = P(("dp", "mem"), None)
    return jax.shard_map(
        fused_on_device if fused else on_device,
        mesh=mesh,
        in_specs=(image, token, P("dp"), *[rows] * 10, *[P()] * 6, image),
        out_specs=(image, image, token, *[rows] * 5, both, both, *[rows] * 3, *[P("dp")] * 6),
        check_vma=False,
    )
```

```python
import functools
import jax
import jax.numpy as jnp
from jax import lax
from jax.experimental import pallas as pl
from jax.experimental.pallas import tpu as pltpu
from jax.sharding import PartitionSpec as P

H = 12
LOW = jnp.bfloat16
WIDE = jnp.float32


def contract(a, b, dims):
    return lax.dot_general(a, b, (dims, ((), ())), preferred_element_type=WIDE)


def project(values, weight):
    return contract(values, weight, ((1,), (0,)))


def back_project(grads, weight):
    return contract(grads, weight, ((1,), (1,)))


def weight_grad(left, right):
    return contract(left, right, ((0,), (0,)))


def heads_of(values, images):
    rows, width = values.shape
    return values.reshape(images, rows // images, H, width // H)


def norm_forward(resid, gain, shift):
    center = resid - jnp.mean(resid, axis=-1, keepdims=True)
    inverse = lax.rsqrt(jnp.mean(center * center, axis=-1, keepdims=True) + 1e-05)
    normed = center * inverse
    return (normed * gain + shift, normed, inverse)


def norm_backward(incoming, normed, inverse, gain):
    scaled = incoming * gain
    grad_in = inverse * (
        scaled
        - jnp.mean(scaled, axis=-1, keepdims=True)
        - normed * jnp.mean(scaled * normed, axis=-1, keepdims=True)
    )
    return (grad_in, jnp.sum(incoming * normed, axis=0), jnp.sum(incoming, axis=0))


def scores_of(query, keys):
    return jnp.einsum("bqhe,bkhe->bhqk", query, keys, preferred_element_type=WIDE) * 0.125


def mix(probs, values):
    return jnp.einsum("bhqk,bkhe->bqhe", probs, values, preferred_element_type=WIDE)


def mix_back(probs, grads):
    return jnp.einsum("bhqk,bqhe->bkhe", probs, grads, preferred_element_type=WIDE)


def attention_backward(probs, attn, grad_attn, query, keys, values):
    row = jnp.sum(grad_attn.astype(WIDE) * attn.astype(WIDE), axis=-1).transpose(0, 2, 1)[..., None]
    grad_probs = jnp.einsum("bqhe,bkhe->bhqk", grad_attn, values, preferred_element_type=WIDE)
    grad_scores = (probs * (grad_probs - row)).astype(LOW)
    grad_query = mix(grad_scores, keys) * 0.125
    grad_keys = mix_back(grad_scores, query) * 0.125
    grad_values = mix_back(probs.astype(LOW), grad_attn)
    return (grad_query, grad_keys, grad_values)


def gelu_tanh(values):
    return jax.nn.gelu(values, approximate=True)


def on_device(
    inputs,
    memory,
    lengths,
    self_query,
    self_key,
    self_value,
    self_out,
    cross_query,
    cross_key,
    cross_value,
    cross_out,
    expand_weight,
    contract_weight,
    gain_one,
    shift_one,
    gain_two,
    shift_two,
    gain_three,
    shift_three,
    cotangent,
):
    images, queries, width = inputs.shape
    mem_rows = memory.shape[1]
    rows = images * queries
    share = self_query.shape[0]
    parts = width // share
    squares = (self_query, self_key, self_value, self_out, cross_query, cross_key, cross_value, cross_out)
    packed = lax.all_gather(jnp.stack(squares), "dp", axis=1, tiled=True)
    expand_full = lax.all_gather(expand_weight, "dp", axis=0, tiled=True)
    contract_full = lax.all_gather(contract_weight, "dp", axis=0, tiled=True)
    (query_full, key_full, value_full, out_full, cquery_full, ckey_full, cvalue_full, cout_full) = packed
    tokens = inputs.reshape(rows, width)
    memory_flat = memory.reshape(images * mem_rows, width)
    incoming = cotangent.reshape(rows, width).astype(WIDE)

    def joined(values):
        return values.reshape(-1, width)

    query_heads = heads_of(project(tokens, query_full).astype(LOW), images)
    key_heads = heads_of(project(tokens, key_full).astype(LOW), images)
    value_heads = heads_of(project(tokens, value_full).astype(LOW), images)
    self_raw = scores_of(query_heads, key_heads)
    self_exp = jnp.exp(self_raw - jnp.max(self_raw, axis=-1, keepdims=True))
    self_probs = self_exp / jnp.sum(self_exp, axis=-1, keepdims=True)
    self_attn = joined(mix(self_probs.astype(LOW), value_heads)).astype(LOW)
    first, normed_one, inverse_one = norm_forward(
        tokens.astype(WIDE) + project(self_attn, out_full), gain_one, shift_one
    )
    first_low = first.astype(LOW)
    cross_q = heads_of(project(first_low, cquery_full).astype(LOW), images)
    cross_k = heads_of(project(memory_flat, ckey_full).astype(LOW), images)
    cross_v = heads_of(project(memory_flat, cvalue_full).astype(LOW), images)
    places = lax.axis_index("mem") * mem_rows + jnp.arange(mem_rows, dtype=jnp.int32)
    valid = (places[None, :] < lengths[:, None])[:, None, None, :]
    cross_raw = jnp.where(valid, scores_of(cross_q, cross_k), -1e30)
    top = lax.pmax(jnp.max(cross_raw, axis=-1, keepdims=True), "mem")
    cross_exp = jnp.where(valid, jnp.exp(cross_raw - top), 0.0)
    total = lax.psum(jnp.sum(cross_exp, axis=-1, keepdims=True), "mem")
    cross_probs = cross_exp / total
    cross_attn = lax.psum(joined(mix(cross_probs.astype(LOW), cross_v)).astype(LOW), "mem")
    second, normed_two, inverse_two = norm_forward(
        first + project(cross_attn, cout_full), gain_two, shift_two
    )
    second_low = second.astype(LOW)
    pre_act = project(second_low, expand_full)
    activ, gelu_pull = jax.vjp(gelu_tanh, pre_act)
    activ_low = activ.astype(LOW)
    result, normed_three, inverse_three = norm_forward(
        second + project(activ_low, contract_full), gain_three, shift_three
    )
    grad_three, gain_three_part, shift_three_part = norm_backward(
        incoming, normed_three, inverse_three, gain_three
    )
    grad_ffn = grad_three.astype(LOW)

    def scattered(part, axes="dp"):
        return lax.psum_scatter(part, axes, scatter_dimension=0, tiled=True).astype(WIDE)

    contract_grad = scattered(weight_grad(activ_low, grad_ffn).astype(LOW))
    grad_pre = gelu_pull(back_project(grad_ffn, contract_full))[0].astype(LOW)
    expand_grad = scattered(weight_grad(second_low, grad_pre).astype(LOW))
    grad_second = grad_three + back_project(grad_pre, expand_full)
    grad_two, gain_two_part, shift_two_part = norm_backward(
        grad_second, normed_two, inverse_two, gain_two
    )
    grad_cross = grad_two.astype(LOW)
    cout_part = weight_grad(cross_attn, grad_cross)
    grad_cattn = heads_of(back_project(grad_cross, cout_full).astype(LOW), images)
    part_cquery, grad_ckey, grad_cvalue = attention_backward(
        cross_probs, heads_of(cross_attn, images), grad_cattn, cross_q, cross_k, cross_v
    )
    grad_cquery = lax.psum(joined(part_cquery).astype(LOW), "mem")
    grad_ckey = joined(grad_ckey).astype(LOW)
    grad_cvalue = joined(grad_cvalue).astype(LOW)
    kv_grad = scattered(
        jnp.concatenate(
            [weight_grad(memory_flat, grad_ckey), weight_grad(memory_flat, grad_cvalue)], axis=1
        ).astype(LOW),
        ("dp", "mem"),
    )
    memory_grad = back_project(grad_ckey, ckey_full) + back_project(grad_cvalue, cvalue_full)
    cquery_part = weight_grad(first_low, grad_cquery)
    grad_first = grad_two + back_project(grad_cquery, cquery_full)
    grad_one, gain_one_part, shift_one_part = norm_backward(
        grad_first, normed_one, inverse_one, gain_one
    )
    grad_self = grad_one.astype(LOW)
    out_part = weight_grad(self_attn, grad_self)
    grad_sattn = heads_of(back_project(grad_self, out_full).astype(LOW), images)
    grad_query, grad_key, grad_value = (
        joined(grad).astype(LOW)
        for grad in attention_backward(
            self_probs, heads_of(self_attn, images), grad_sattn, query_heads, key_heads, value_heads
        )
    )
    input_grad = (
        grad_one
        + back_project(grad_query, query_full)
        + back_project(grad_key, key_full)
        + back_project(grad_value, value_full)
    )
    norm_parts = jnp.stack(
        [gain_one_part, shift_one_part, gain_two_part, shift_two_part, gain_three_part, shift_three_part], axis=1
    )
    rest = scattered(
        jnp.concatenate(
            [
                weight_grad(tokens, grad_query),
                weight_grad(tokens, grad_key),
                weight_grad(tokens, grad_value),
                out_part,
                cquery_part,
                cout_part,
                jnp.pad(norm_parts, ((0, 0), (0, 122))),
            ],
            axis=1,
        ).astype(LOW)
    )
    squares_grad = [rest[:, place * width : (place + 1) * width] for place in range(6)]
    norms_grad = [rest[:, 6 * width + place] for place in range(6)]
    return (
        result.reshape(inputs.shape),
        input_grad.reshape(inputs.shape),
        memory_grad.reshape(memory.shape),
        *squares_grad[:5],
        kv_grad[:, :width],
        kv_grad[:, width:],
        squares_grad[5],
        expand_grad,
        contract_grad,
        *norms_grad,
    )


MESH = pl.DeviceIdType.MESH
ANY = pl.BlockSpec(memory_space=pl.ANY)
INNER = pl.BlockSpec(memory_space=pltpu.VMEM)
SCALAR = pl.BlockSpec(memory_space=pltpu.SMEM)
D = 768
FF = 3072
PAIRS = 6
QP = 112
PIECES = 16
SQ, SK, SV, SO, CK, CV, CQ, CO, EX, CT = 0, 1, 2, 3, 4, 5, 6, 7, 8, 12
WINDOW = 2
FIRST_DUE = 7.0
UNIT_TIME = 3.5
EXCHANGE_TIME = 16.0
VMEM_BYTES = 60 * 2**20


def mm(a, b):
    return lax.dot_general(a, b, (((1,), (0,)), ((), ())), preferred_element_type=WIDE)


def mm_nt(a, b):
    return lax.dot_general(a, b, (((1,), (1,)), ((), ())), preferred_element_type=WIDE)


def mm_tn(a, b):
    return lax.dot_general(a, b, (((0,), (0,)), ((), ())), preferred_element_type=WIDE)


def low_lanes(shape):
    return lax.broadcasted_iota(jnp.int32, shape, 1) < 64


def two_heads(pair):
    lower = low_lanes(pair.shape)
    nought = jnp.zeros_like(pair)
    return jnp.concatenate([jnp.where(lower, pair, nought), jnp.where(lower, nought, pair)], axis=0)


def one_pair(both):
    rows = both.shape[0] // 2
    upper = both[rows:]
    return jnp.where(low_lanes(upper.shape), both[:rows], upper)


def places():
    d = lax.axis_index("dp")
    c = lax.rem(d, 2)
    x = lax.rem(d // 2, 2)
    y = d // 4
    other = d + 1 - 2 * c
    beside = d + 2 - 4 * x
    above = d + 4 - 8 * y
    across = beside + 4 - 8 * y
    return d, other, beside, above, across


def weight_row(piece, owner):
    if isinstance(piece, int) and piece >= CT:
        return pl.multiple_of(CT * D + owner * 384 + (piece - CT) * 96, 96)
    return pl.multiple_of(piece * D + owner * 96, 96)


UNITS = ((SQ, SK), (SV,), (CK, CV), (SO,), (CQ,), (CO,), (8,), (9,), (10,), (11,), (12,), (13,), (14,), (15,))
LAG = 2


class Gather:
    def __init__(self, shards, full, local, send, recv, saved, save):
        self.shards, self.full, self.saved, self.save = shards, full, saved, save
        self.local, self.send, self.recv = local, send, recv
        self.d, self.other, self.beside, self.above, self.across = places()
        self.z = lax.axis_index("mem")
        self.q = lax.rem(self.z, 2)
        self.near = self.z + 1 - 2 * self.q
        self.sent = []
        self.role = {}
        self.done = 0
        self.clock = 0.0
        self.landed = [False] * PIECES
        self.unit_of = {piece: place for place, unit in enumerate(UNITS) for piece in unit}

    def at(self, piece, owner):
        return self.full.at[pl.ds(weight_row(piece, owner), 96)]

    def own(self, piece):
        if piece < EX:
            return self.shards[piece]
        if piece < CT:
            return self.shards[EX].at[:, pl.ds((piece - EX) * D, D)]
        return self.shards[EX + 1].at[pl.ds((piece - CT) * 96, 96)]

    def copy(self, src, piece, owner, kind, target, note):
        return pltpu.make_async_remote_copy(
            src,
            self.at(piece, owner),
            self.send.at[piece, note],
            self.recv.at[piece, kind],
            device_id=target,
            device_id_type=MESH,
        )

    def push(self, src, piece, owner, kind, target):
        one = self.copy(src, piece, owner, kind, (target, self.z), kind)
        one.start()
        self.sent.append(one)

    def lend(self, piece, owner, kind):
        one = self.copy(self.at(piece, owner), piece, owner, kind, (self.d, self.near), 7 + kind)
        one.start()
        self.sent.append(one)

    def arrived(self, piece, kind):
        self.copy(self.at(piece, self.d), piece, self.d, kind, (self.other, self.z), kind).wait_recv()

    def roles(self, unit):
        if unit not in self.role:
            first, second = unit
            mine = first + self.q * (second - first)
            self.role[unit] = (mine, first + second - mine)
        return self.role[unit]

    def local_copy(self, piece):
        return pltpu.make_async_copy(self.own(piece), self.at(piece, self.d), self.local.at[piece])

    def start(self, place):
        if place >= len(UNITS):
            return
        unit = UNITS[place]
        if len(unit) == 1:
            piece = unit[0]
            src = self.own(piece)
            self.local_copy(piece).start()
        else:
            piece, theirs = self.roles(unit)
            src = self.at(piece, self.d)
            self.push(self.at(theirs, self.d), theirs, self.d, 3, self.other)
        self.push(src, piece, self.d, 0, self.beside)
        self.push(src, piece, self.d, 1, self.above)
        self.push(src, piece, self.d, 3, self.other)

    def prepare(self):
        for unit in UNITS:
            if len(unit) == 2:
                for piece in unit:
                    self.local_copy(piece).start()

    def begin(self):
        for unit in UNITS:
            if len(unit) == 2:
                for piece in unit:
                    self.local_copy(piece).wait()
        for place in range(WINDOW):
            self.start(place)

    def relay(self, place):
        unit = UNITS[place]
        piece = unit[0] if len(unit) == 1 else self.roles(unit)[0]
        for kind, owner, side, target in ((0, self.beside, 0, self.above), (1, self.above, 1, self.beside)):
            self.arrived(piece, kind)
            if place % 2 == side:
                self.push(self.at(piece, owner), piece, owner, 2, target)
            self.push(self.at(piece, owner), piece, owner, 4 + kind, self.other)
            if len(unit) == 2:
                self.lend(piece, owner, kind)

    def finish(self, place):
        unit = UNITS[place]
        piece = unit[0] if len(unit) == 1 else self.roles(unit)[0]
        self.arrived(piece, 2)
        self.push(self.at(piece, self.across), piece, self.across, 6, self.other)
        if len(unit) == 2:
            self.lend(piece, self.across, 2)

    def borrow(self, place):
        unit = UNITS[place]
        if len(unit) == 2:
            piece = self.roles(unit)[1]
            for kind, owner in enumerate((self.beside, self.above, self.across)):
                self.arrived(piece, kind)
                self.push(self.at(piece, owner), piece, owner, 4 + kind, self.other)

    def step(self):
        place = self.done
        if place >= len(UNITS) + LAG:
            return
        self.done += 1
        if place < len(UNITS):
            self.relay(place)
            self.start(place + WINDOW)
        if 1 <= place <= len(UNITS):
            self.finish(place - 1)
        if place >= LAG:
            self.borrow(place - LAG)

    def due(self, place):
        return FIRST_DUE + UNIT_TIME * place

    def spend(self, time):
        self.wait_for(self.clock + time)

    def wait_for(self, clock):
        self.clock = max(self.clock, clock)
        while self.done < len(UNITS) + LAG and self.due(self.done) <= self.clock:
            self.step()

    def upto(self, count):
        while self.done < min(count, len(UNITS) + LAG):
            self.clock = max(self.clock, self.due(self.done))
            self.step()

    def ready(self, piece):
        place = self.unit_of[piece]
        self.upto(place + 1 + (1 if len(UNITS[place]) == 1 else LAG))
        if self.landed[piece]:
            return
        self.landed[piece] = True
        if len(UNITS[place]) == 1:
            self.local_copy(piece).wait()
        for kind in range(3, 7):
            self.arrived(piece, kind)
        if piece < CT:
            self.save(self.full.at[pl.ds(piece * D, D)], self.saved.at[pl.ds(piece * D, D)])

    def close(self):
        for one in self.sent:
            one.wait_send()


def greet(targets):
    barrier = pltpu.get_barrier_semaphore()
    for target in targets:
        pl.semaphore_signal(barrier, 1, device_id=target, device_id_type=MESH)
    pl.semaphore_wait(barrier, len(targets))


def norm_rows(resid, gain, shift):
    center = resid - jnp.mean(resid, axis=-1, keepdims=True)
    inverse = lax.rsqrt(jnp.mean(center * center, axis=-1, keepdims=True) + 1e-05)
    normed = center * inverse
    return normed * gain + shift, normed, inverse


def forward_kernel(images, queries, mem_rows, *refs):
    (raw, mem, lens, *rest) = refs
    norms, rest = rest[:6], rest[6:]
    shards = rest[:10]
    (o_result, o_full, o_acts, o_ffn, o_us, o_inv, o_kv, o_pc, o_ps, o_wst) = rest[10:20]
    (
        full, acts, ffn, us, inv, kv, pc, ps, wst, tok, wide, stats, osend, orecv, lsend, lrecv, fst,
        local, send, recv, zsend, zrecv, keep,
    ) = rest[20:]
    rows = images * QP
    z = lax.axis_index("mem")
    d = lax.axis_index("dp")
    kept = []

    def save(src, dst):
        one = pltpu.make_async_copy(src, dst, keep.at[len(kept)])
        one.start()
        kept.append(one)

    gather = Gather(shards, full, local, send, recv, o_full, save)
    others = [lax.rem(z + r, 4) for r in range(1, 4)]
    gather.prepare()
    greet(
        [(gather.other, z), (gather.beside, z), (gather.above, z)] + [(d, other) for other in others]
    )
    gather.begin()
    blank = jnp.zeros((QP - queries, D), LOW)
    for i in range(images):
        tok[pl.ds(i * QP, QP), :] = jnp.concatenate([raw[i], blank], axis=0)

    def weight(piece, tile):
        return full[pl.ds(piece * D, D), cols(tile)]

    def cols(tile):
        return pl.ds(pl.multiple_of(tile * 256, 256), 256)

    def image(i):
        return pl.ds(pl.multiple_of(i * QP, QP), QP)

    def project_rows(src, piece, dst, scale):
        def body(tile, carry):
            out = mm(src[...], weight(piece, tile)).astype(LOW)
            if scale != 1.0:
                out = out * jnp.asarray(scale, LOW)
            acts[dst, :, cols(tile)] = out
            return carry

        lax.fori_loop(0, 3, body, 0, unroll=True)

    gather.ready(SQ)
    project_rows(tok, SQ, 0, 0.125)
    gather.ready(SK)
    project_rows(tok, SK, 1, 1.0)
    gather.ready(SV)
    project_rows(tok, SV, 2, 1.0)

    gather.spend(2.0)
    for i in range(images):
        at = image(i)
        valid = lax.broadcasted_iota(jnp.int32, (2 * QP, QP), 1) < queries

        def self_pair(hp, carry):
            lanes = pl.ds(pl.multiple_of(hp * 128, 128), 128)
            scores = mm_nt(two_heads(acts[0, at, lanes]), acts[1, at, lanes])
            scores = jnp.where(valid, scores, -1e30)
            grown = jnp.exp(scores - jnp.max(scores, axis=-1, keepdims=True))
            probs = (grown / jnp.sum(grown, axis=-1, keepdims=True)).astype(LOW)
            ps[i, hp] = probs
            acts[3, at, lanes] = one_pair(mm(probs, acts[2, at, lanes])).astype(LOW)
            return carry

        lax.fori_loop(0, PAIRS, self_pair, 0, unroll=True)
        gather.spend(1.0)

    def memory_rows(piece, dst):
        for tile in range(3):
            kv[dst, :, cols(tile)] = mm(mem[...], weight(piece, tile)).astype(LOW)
            gather.spend(0.7)

    def add_branch(src, piece, base):
        def body(tile, carry):
            wide[0, :, cols(tile)] = base(cols(tile)) + mm(acts[src], weight(piece, tile))
            return carry

        lax.fori_loop(0, 3, body, 0, unroll=True)

    def normalize(which, low_dst):
        def body(i, carry):
            at = image(i)
            gain, shift = norms[2 * which][...][None, :], norms[2 * which + 1][...][None, :]
            out, normed, inverse = norm_rows(wide[0, at, :], gain, shift)
            us[which, at, :] = normed
            lane = lax.broadcasted_iota(jnp.int32, (QP, 128), 1)
            inv[at, :] = jnp.where(lane == which, inverse, inv[at, :])
            wide[1, at, :] = out
            if low_dst is not None:
                acts[low_dst, at, :] = out.astype(LOW)
            return carry

        lax.fori_loop(0, images, body, 0)

    inv[...] = jnp.zeros_like(inv)
    gather.ready(SO)
    add_branch(3, SO, lambda at: tok[:, at].astype(WIDE))
    normalize(0, 4)
    gather.spend(1.6)
    save(us.at[0], o_us.at[0])
    gather.ready(CK)
    memory_rows(CK, 0)
    gather.ready(CV)
    memory_rows(CV, 1)
    save(kv, o_kv)
    save(ps, o_ps)
    gather.ready(CQ)
    project_rows(acts.at[4], CQ, 5, 0.125)

    pushed = []

    def pass_on(src, dst, kind, r):
        one = pltpu.make_async_remote_copy(
            src, dst, zsend.at[kind, r - 1], zrecv.at[kind, r - 1],
            device_id=(d, others[r - 1]), device_id_type=MESH,
        )
        one.start()
        pushed.append(one)

    def taken(ref, kind, r):
        pltpu.make_async_remote_copy(
            ref, ref, zsend.at[kind, r - 1], zrecv.at[kind, r - 1],
            device_id=(d, others[r - 1]), device_id_type=MESH,
        ).wait_recv()

    lane = lax.broadcasted_iota(jnp.int32, (QP, 128), 1)

    def turned(tall):
        return jnp.concatenate([tall, jnp.zeros((128 - QP, 128), WIDE)], axis=0).T[:16]

    def returned(flat):
        return jnp.concatenate([flat, jnp.zeros((112, 128), WIDE)], axis=0).T[:QP]

    for turn in range(4):
        i = others[turn] if turn < 3 else z
        at = image(i)
        tokens = pl.ds(pl.multiple_of(i * mem_rows, mem_rows), mem_rows)
        place = z * mem_rows + lax.broadcasted_iota(jnp.int32, (2 * QP, mem_rows), 1)
        valid = place < lens[i]

        def pair(hp, noted):
            lanes = pl.ds(pl.multiple_of(hp * 128, 128), 128)
            scores = mm_nt(two_heads(acts[5, at, lanes]), kv[0, tokens, lanes])
            scores = jnp.where(valid, scores, -1e30)
            top = jnp.max(scores, axis=-1, keepdims=True)
            grown = jnp.where(valid, jnp.exp(scores - top), 0.0)
            total = jnp.sum(grown, axis=-1, keepdims=True)
            shrink = jnp.where(total > 0.0, 1.0 / total, 0.0)
            probs = grown.astype(LOW)
            pc[i, hp] = probs
            osend[turn, :, lanes] = one_pair(mm(probs, kv[1, tokens, lanes]) * shrink).astype(LOW)
            for half in range(2):
                span = slice(half * QP, half * QP + QP)
                noted = jnp.where(lane == 2 * hp + half, top[span], noted)
                noted = jnp.where(lane == 64 + 2 * hp + half, total[span], noted)
            return noted

        noted = lax.fori_loop(0, PAIRS, pair, jnp.zeros((QP, 128), WIDE), unroll=True)
        stats[i] = noted
        total = pltpu.roll(noted, 64, 1)
        lsend[turn] = turned(jnp.where(total > 0.0, noted + jnp.log(total), -1e30))
        if turn < 3:
            pass_on(osend.at[turn], orecv.at[turn], 0, turn + 1)
            pass_on(lsend.at[turn], lrecv.at[turn], 1, turn + 1)
        gather.spend(1.9)
    save(pc, o_pc)
    gather.wait_for(gather.clock + EXCHANGE_TIME - 5.0)
    for r in range(1, 4):
        taken(orecv.at[r - 1], 0, r)
        taken(lrecv.at[r - 1], 1, r)
    noted = [lsend[3], lrecv[0], lrecv[1], lrecv[2]]
    top = functools.reduce(jnp.maximum, noted)
    level = top + jnp.log(sum(jnp.exp(one - top) for one in noted))
    fst[z] = level
    share = [returned(jnp.exp(one - level)) for one in noted]
    lower = low_lanes((QP, 128))
    mine = image(z)
    for hp in range(PAIRS):
        lanes = pl.ds(hp * 128, 128)
        joined = jnp.zeros((QP, 128), WIDE)
        for r in range(4):
            spread = jnp.where(
                lower, share[r][:, 2 * hp : 2 * hp + 1], share[r][:, 2 * hp + 1 : 2 * hp + 2]
            )
            part = osend[3, :, lanes] if r == 0 else orecv[r - 1, :, lanes]
            joined = joined + spread * part.astype(WIDE)
        acts[6, mine, lanes] = joined.astype(LOW)
    for r in range(1, 4):
        pass_on(acts.at[6, mine], acts.at[6, mine], 2, r)
        pass_on(fst.at[z], fst.at[z], 3, r)
    gather.wait_for(gather.clock + EXCHANGE_TIME)
    gather.ready(CO)
    for r in range(1, 4):
        back = lax.rem(z + 4 - r, 4)
        taken(acts.at[6, image(back)], 2, r)
        taken(fst.at[back], 3, r)
    for i in range(images):
        wst[i] = jnp.exp(stats[i] - returned(fst[i]))
    save(wst, o_wst)
    add_branch(6, CO, lambda at: wide[1, :, at])
    normalize(1, 7)
    save(us.at[1], o_us.at[1])
    save(acts, o_acts)

    def expand(block):
        def body(tile, carry):
            pre = mm(acts[7], full[pl.ds((EX + block) * D, D), cols(tile)])
            root = 0.7978845608028654
            square = pre * pre
            bend = jnp.tanh(root * (pre + 0.044715 * (pre * square)))
            half = 0.5 * (1.0 + bend)
            slope = half + (0.5 * root) * pre * (1.0 - bend * bend) * (1.0 + 0.134145 * square)
            at = pl.ds(pl.multiple_of(block * D + tile * 256, 256), 256)
            ffn[0, :, at] = (pre * half).astype(LOW)
            ffn[1, :, at] = slope.astype(LOW)
            return carry

        lax.fori_loop(0, 3, body, 0, unroll=True)

    for block in range(4):
        gather.ready(EX + block)
        expand(block)
        gather.spend(1.2)
    save(ffn, o_ffn)
    for block in range(4):
        gather.ready(CT + block)
    save(full.at[pl.ds(CT * D, FF)], o_full.at[pl.ds(CT * D, FF)])

    def contract(tile, carry):
        wide[0, :, cols(tile)] = wide[1, :, cols(tile)] + mm(
            ffn[0], full[pl.ds(CT * D, FF), cols(tile)]
        )
        return carry

    lax.fori_loop(0, 3, contract, 0, unroll=True)
    normalize(2, None)
    save(wide.at[1], o_result)
    save(us.at[2], o_us.at[2])
    save(inv, o_inv)
    for one in pushed:
        one.wait_send()
    gather.close()
    for one in kept:
        one.wait()


def forward(tok, mem, lens, norms, shards, images, queries, mem_rows):
    rows = images * QP
    shape = jax.ShapeDtypeStruct
    tokens = images * mem_rows
    outs = (
        shape((rows, D), WIDE),
        shape((PIECES * D, D), LOW),
        shape((8, rows, D), LOW),
        shape((2, rows, FF), LOW),
        shape((3, rows, D), WIDE),
        shape((rows, 128), WIDE),
        shape((2, tokens, D), LOW),
        shape((images, PAIRS, 2 * QP, mem_rows), LOW),
        shape((images, PAIRS, 2 * QP, QP), LOW),
        shape((images, QP, 128), WIDE),
    )
    dma = pltpu.SemaphoreType.DMA
    return pl.pallas_call(
        functools.partial(forward_kernel, images, queries, mem_rows),
        out_shape=outs,
        in_specs=[INNER, INNER, SCALAR] + [INNER] * 6 + [ANY] * 10,
        out_specs=[ANY] * len(outs),
        scratch_shapes=[
            *[pltpu.VMEM(one.shape, one.dtype) for one in outs[1:]],
            pltpu.VMEM((rows, D), LOW),
            pltpu.VMEM((2, rows, D), WIDE),
            pltpu.VMEM((images, QP, 128), WIDE),
            pltpu.VMEM((4, QP, D), LOW),
            pltpu.VMEM((3, QP, D), LOW),
            pltpu.VMEM((4, 16, 128), WIDE),
            pltpu.VMEM((3, 16, 128), WIDE),
            pltpu.VMEM((images, 16, 128), WIDE),
            dma((PIECES,)),
            dma((PIECES, 10)),
            dma((PIECES, 7)),
            dma((4, 3)),
            dma((4, 3)),
            dma((28,)),
        ],
        compiler_params=pltpu.CompilerParams(
            collective_id=0, has_side_effects=True, vmem_limit_bytes=VMEM_BYTES
        ),
        name="forward",
    )(tok, mem, lens, *norms, *(shards[place] for place in (0, 1, 2, 3, 5, 6, 4, 7, 8, 9)))


def rows_of_image(i):
    return pl.ds(pl.multiple_of(i * QP, QP), QP)


def cols_of_tile(tile):
    return pl.ds(pl.multiple_of(tile * 256, 256), 256)


class Reduce:
    def __init__(self, where, turn, grad, core_in, chip_in, core_sems, chip_sems):
        self.where, self.turn = where, turn
        self.grad, self.core_in, self.chip_in = grad, core_in, chip_in
        self.core_sems, self.chip_sems = core_sems, chip_sems
        self.sent = []
        d, other, beside, above, across = where
        self.c = lax.rem(d, 2)
        self.z = lax.axis_index("mem")

    def copy(self, src, dst, sems, place, target):
        return pltpu.make_async_remote_copy(
            src, dst, sems.at[0, self.turn, place], sems.at[1, self.turn, place],
            device_id=(target, self.z), device_id_type=MESH,
        )

    def core_stage(self):
        one = self.copy(self.grad.at[1 - self.c], self.core_in, self.core_sems, 0, self.where[1])
        one.start()
        self.sent.append(one)

    def chip_stage(self):
        self.copy(self.core_in, self.core_in, self.core_sems, 0, self.where[1]).wait_recv()
        for chip in range(4):
            both = self.grad[self.c, chip].astype(WIDE) + self.core_in[chip].astype(WIDE)
            self.grad[self.c, chip] = both.astype(LOW)
        for place, target in enumerate(self.where[2:]):
            one = self.copy(
                self.grad.at[self.c, target // 2], self.chip_in.at[place], self.chip_sems, place, target
            )
            one.start()
            self.sent.append(one)

    def total(self):
        own = self.grad[self.c, self.where[0] // 2].astype(WIDE)
        for place, target in enumerate(self.where[2:]):
            self.copy(
                self.chip_in.at[place], self.chip_in.at[place], self.chip_sems, place, target
            ).wait_recv()
            own = own + self.chip_in[place].astype(WIDE)
        return own

    def settle(self):
        for one in self.sent:
            one.wait_send()
        self.sent = []


def backward_kernel(images, queries, mem_rows, *refs):
    (
        h_gain_one, h_gain_two, h_gain_three, h_cot, h_tok, h_mem, h_full, h_acts, h_ffn, h_us, h_inv, h_kv, h_pc, h_ps, h_wst,
    ) = refs[:15]
    (o_expand, o_contract, o_co, o_mid, o_late, o_last, o_keys, o_mem, o_in, o_norms) = refs[15:25]
    (
        cot, tok, mem, slots, acts, ffn, us, inv, kv, pc, ps, wst, wide, grads, nsum, nin,
        zsend, zin, mout,
        g_expand, g_contract, g_co, g_mid, g_late, g_last, c_expand, c_contract, c_co, c_mid, c_late, c_last, c_keys,
        t_expand, t_contract, t_co, t_mid, t_late, t_last, t_keys,
        f_expand, f_contract, f_co, f_mid, f_late, f_last, k_out, k_in,
        load, slot_sems, pc_sems, mout_sems, core_sems, chip_sems, fin_sems, local_sems, ksems, zsems, nsems,
    ) = refs[25:]
    z = lax.axis_index("mem")
    d = lax.axis_index("dp")
    where = places()
    q = lax.rem(z, 2)
    zp = z + 1 - 2 * q
    others = [lax.rem(z + r, 4) for r in range(1, 4)]
    dpeers = [lax.rem(d + r, 8) for r in range(1, 8)]

    gains = (h_gain_one, h_gain_two, h_gain_three)
    loads = {}
    waited = set()

    def fetch(name, src, dst):
        one = pltpu.make_async_copy(src, dst, load.at[len(loads)])
        one.start()
        loads[name] = one

    order = [CT, CT + 1, CT + 2, CT + 3, EX, EX + 1, EX + 2, EX + 3, CO, CK, CV, CQ, SO, SQ, SK, SV]
    depth = 4

    def slot_copy(turn):
        return pltpu.make_async_copy(
            h_full.at[pl.ds(order[turn] * D, D)], slots.at[turn % depth], slot_sems.at[turn % depth]
        )

    def prefetch(turn):
        if turn < len(order):
            slot_copy(turn).start()

    fetch("cot", h_cot, cot)
    fetch("u3", h_us.at[2], us.at[0])
    fetch("inv", h_inv, inv)
    prefetch(0)
    fetch("gp", h_ffn.at[1], ffn.at[1])

    def have(name):
        if name not in waited:
            waited.add(name)
            loads[name].wait()

    def pc_copy(turn):
        i = lax.rem(z + turn + 1, 4)
        return pltpu.make_async_copy(h_pc.at[i], pc.at[turn % 2], pc_sems.at[turn % 2])

    greet([(peer, z) for peer in dpeers] + [(d, other) for other in others])

    nsum[...] = jnp.zeros_like(nsum)

    def norm_back(which, incoming, slot, low_dst):
        def body(i, carry):
            at = rows_of_image(i)
            above = incoming(at)
            unit = us[slot, at, :]
            inverse = inv[at, which : which + 1]
            scaled = above * gains[which][...][None, :]
            first = jnp.mean(scaled, axis=-1, keepdims=True)
            second = jnp.mean(scaled * unit, axis=-1, keepdims=True)
            grad = inverse * (scaled - first - unit * second)
            wide[0, at, :] = grad
            grads[low_dst, at, :] = grad.astype(LOW)
            row = 2 * which
            nsum[row : row + 1, :] += jnp.sum(above * unit, axis=0, keepdims=True)
            nsum[row + 1 : row + 2, :] += jnp.sum(above, axis=0, keepdims=True)
            return carry

        lax.fori_loop(0, images, body, 0)

    turn_of = {piece: turn for turn, piece in enumerate(order)}

    def slot(piece):
        turn = turn_of[piece]
        slot_copy(turn).wait()
        return slots.at[turn % depth]

    def freed(piece):
        prefetch(turn_of[piece] + depth)

    for name in ("cot", "inv", "u3"):
        have(name)
    norm_back(2, lambda at: cot[at, :].astype(WIDE), 0, 0)
    for turn in range(1, depth):
        prefetch(turn)
    fetch("second_low", h_acts.at[7], acts.at[7])
    have("gp")
    for block in range(4):
        weight = slot(CT + block)

        def body(tile, carry):
            at = pl.ds(pl.multiple_of(block * D + tile * 256, 256), 256)
            back = mm_nt(grads[0], weight[cols_of_tile(tile), :])
            ffn[1, :, at] = (back * ffn[1, :, at].astype(WIDE)).astype(LOW)
            return carry

        lax.fori_loop(0, 3, body, 0, unroll=True)
        freed(CT + block)

    def reduce_at(place, grad, core_in, chip_in):
        return Reduce(where, place, grad, core_in, chip_in, core_sems, chip_sems)

    fetch("u2", h_us.at[1], us.at[1])
    fetch("kv", h_kv, kv)
    fetch("wst", h_wst, wst)
    fetch("acts", h_acts.at[pl.ds(0, 7)], acts.at[pl.ds(0, 7)])
    pc_copy(0).start()
    pc_copy(1).start()
    have("second_low")
    r_expand = reduce_at(0, g_expand, c_expand, t_expand)

    def expand_part(tile, carry):
        at = pl.ds(pl.multiple_of(q * 1536 + tile * 256, 256), 256)
        out = mm_tn(acts[7], ffn[1, :, at]).astype(LOW)
        for e in range(8):
            g_expand[e % 2, e // 2, :, cols_of_tile(tile)] = out[96 * e : 96 * e + 96]
        return carry

    lax.fori_loop(0, 6, expand_part, 0)
    r_expand.core_stage()
    for block in range(4):
        weight = slot(EX + block)

        def body(tile, carry):
            at = cols_of_tile(tile)
            back = mm_nt(ffn[1, :, pl.ds(block * D, D)], weight[at, :])
            wide[0, :, at] = wide[0, :, at] + back
            return carry

        lax.fori_loop(0, 3, body, 0, unroll=True)
        freed(EX + block)
        if block == 2:
            r_expand.chip_stage()
    have("u2")
    norm_back(1, lambda at: wide[0, at, :], 1, 1)

    def through(src, piece, dst):
        weight = slot(piece)

        def body(tile, carry):
            grads[dst, :, cols_of_tile(tile)] = mm_nt(grads[src], weight[cols_of_tile(tile), :]).astype(LOW)
            return carry

        lax.fori_loop(0, 3, body, 0, unroll=True)
        freed(piece)

    fetch("act", h_ffn.at[0], ffn.at[0])
    fetch("mem", h_mem, mem)
    fetch("u1", h_us.at[0], us.at[0])
    fetch("ps", h_ps, ps)
    fetch("tok", h_tok, tok)
    through(1, CO, 2)
    have("kv")
    have("wst")
    have("acts")
    pushed = []

    def across_mem(src, dst, kind, r):
        return pltpu.make_async_remote_copy(
            src, dst, zsems.at[0, kind, r - 1], zsems.at[1, kind, r - 1],
            device_id=(d, others[r - 1]), device_id_type=MESH,
        )

    for turn in range(4):
        i = lax.rem(z + turn + 1, 4)
        pc_copy(turn).wait()
        at = rows_of_image(i)
        tokens = pl.ds(pl.multiple_of(i * mem_rows, mem_rows), mem_rows)
        factors = wst[i]

        def pair(hp, carry):
            lanes = pl.ds(pl.multiple_of(hp * 128, 128), 128)
            query = two_heads(acts[5, at, lanes])
            above = two_heads(grads[2, at, lanes])
            attn = acts[6, at, lanes].astype(WIDE)
            row = jnp.sum(above.astype(WIDE) * jnp.concatenate([attn, attn], axis=0), axis=-1, keepdims=True)
            lane = lax.broadcasted_iota(jnp.int32, (QP, 128), 1)
            factor = jnp.concatenate(
                [
                    jnp.sum(jnp.where(lane == 2 * hp + half, factors, 0.0), axis=-1, keepdims=True)
                    for half in range(2)
                ],
                axis=0,
            )
            probs = pc[turn % 2, hp].astype(WIDE) * factor
            keys, values = kv[0, tokens, lanes], kv[1, tokens, lanes]
            inner = mm_nt(above, values)
            scores = (probs * (inner - row)).astype(LOW)
            zsend[turn, :, lanes] = (one_pair(mm(scores, keys)) * 0.125).astype(LOW)
            kv[0, tokens, lanes] = mm_tn(scores, query).astype(LOW)
            kv[1, tokens, lanes] = mm_tn(probs.astype(LOW), above).astype(LOW)
            return carry

        lax.fori_loop(0, PAIRS, pair, 0, unroll=True)
        if turn < 2:
            pc_copy(turn + 2).start()
        if turn < 3:
            one = across_mem(zsend.at[turn], zin.at[turn], 0, turn + 1)
            one.start()
            pushed.append(one)
        if turn == 1:
            have("act")
            r_contract = reduce_at(1, g_contract, c_contract, t_contract)

            def contract_part(e, carry):
                at = pl.ds(pl.multiple_of(e * 384, 384), 384)
                half = pl.ds(pl.multiple_of(q * 384, 384), 384)
                g_contract[lax.rem(e, 2), e // 2] = mm_tn(ffn[0, :, at], grads[0, :, half]).astype(LOW)
                return carry

            lax.fori_loop(0, 8, contract_part, 0)
            r_contract.core_stage()
        if turn == 3:
            r_contract.chip_stage()

    have("mem")
    f_expand[...] = r_expand.total().astype(LOW)
    r_expand.settle()
    r_keys = reduce_at(2, g_expand, c_keys, t_keys)

    def key_parts(which):
        def key_part(tile, carry):
            out = mm_tn(mem[...], kv[which, :, cols_of_tile(tile)]).astype(LOW)
            at = pl.ds(pl.multiple_of(which * D + tile * 256, 256), 256)
            for e in range(8):
                g_expand[e % 2, e // 2, :, at] = out[96 * e : 96 * e + 96]
            return carry

        lax.fori_loop(0, 3, key_part, 0, unroll=True)

    key_parts(0)
    for r in range(1, 4):
        across_mem(zin.at[r - 1], zin.at[r - 1], 0, r).wait_recv()
    mine = rows_of_image(z)
    grads[3, mine, :] = (
        zsend[3].astype(WIDE) + zin[0].astype(WIDE) + zin[1].astype(WIDE) + zin[2].astype(WIDE)
    ).astype(LOW)
    for r in range(1, 4):
        one = across_mem(grads.at[3, mine], grads.at[3, mine], 1, r)
        one.start()
        pushed.append(one)
    key_parts(1)
    r_keys.core_stage()

    def finals(fin, out, place):
        pltpu.make_async_copy(fin, out, local_sems.at[place]).start()
        one = pltpu.make_async_remote_copy(
            fin, out, fin_sems.at[0, place], fin_sems.at[1, place], device_id=(d, zp), device_id_type=MESH
        )
        one.start()
        return one

    ended = []
    key_weight, value_weight = slot(CK), slot(CV)
    for i in range(images):
        at = pl.ds(i * mem_rows, mem_rows)
        if i >= 2:
            pltpu.make_async_copy(mout.at[i % 2], o_mem.at[at], mout_sems.at[i % 2]).wait()

        def body(tile, carry):
            span = cols_of_tile(tile)
            mout[i % 2, :, span] = (
                mm_nt(kv[0, at, :], key_weight[span, :]) + mm_nt(kv[1, at, :], value_weight[span, :])
            ).astype(LOW)
            return carry

        lax.fori_loop(0, 3, body, 0, unroll=True)
        pltpu.make_async_copy(mout.at[i % 2], o_mem.at[at], mout_sems.at[i % 2]).start()
        if i == 1:
            r_keys.chip_stage()
    freed(CK)
    freed(CV)
    def wide_parts(place, grad, core_in, chip_in, left, right, tiles):
        def body(tile, carry):
            out = mm_tn(left(), right(cols_of_tile(tile))).astype(LOW)
            for e in range(8):
                grad[e % 2, e // 2, :, cols_of_tile(tile)] = out[96 * e : 96 * e + 96]
            return carry

        lax.fori_loop(0, tiles, body, 0)

    def half_parts(grad, left, right):
        half = pl.ds(pl.multiple_of(q * 384, 384), 384)
        out = mm_tn(left, right(half)).astype(LOW)
        for e in range(8):
            grad[e % 2, e // 2] = out[96 * e : 96 * e + 96]

    r_co = reduce_at(3, g_co, c_co, t_co)
    half_parts(g_co, acts[6], lambda at: grads[1, :, at])
    r_co.core_stage()
    for r in range(1, 4):
        back = lax.rem(z + 4 - r, 4)
        across_mem(grads.at[3, rows_of_image(back)], grads.at[3, rows_of_image(back)], 1, r).wait_recv()
    r_co.chip_stage()
    ended.append(finals(f_expand, o_expand.at[q], 0))

    def add_back(src, piece):
        weight = slot(piece)

        def body(tile, carry):
            span = cols_of_tile(tile)
            wide[0, :, span] = wide[0, :, span] + mm_nt(src(), weight[span, :])
            return carry

        lax.fori_loop(0, 3, body, 0, unroll=True)
        freed(piece)

    add_back(lambda: grads[3], CQ)
    have("u1")
    norm_back(0, lambda at: wide[0, at, :], 0, 2)
    for r in range(1, 8):
        one = pltpu.make_async_remote_copy(
            nsum, nin.at[r - 1], nsems.at[0, r - 1], nsems.at[1, r - 1],
            device_id=(dpeers[r - 1], z), device_id_type=MESH,
        )
        one.start()
        pushed.append(one)
    have("tok")

    def either(place, grad, core_in, chip_in, lefts, rights):
        reducer = reduce_at(place, grad, core_in, chip_in)
        for parity in range(2):

            @pl.when(q == parity)
            def _():
                wide_parts(place, grad, core_in, chip_in, lefts[parity], rights[parity], 3)

        reducer.core_stage()
        return reducer

    r_mid = either(
        4, g_mid, c_mid, t_mid,
        (lambda: acts[4], lambda: acts[3]),
        (lambda at: grads[3, :, at], lambda at: grads[2, :, at]),
    )
    through(2, SO, 0)
    have("ps")
    r_mid.chip_stage()
    f_contract[...] = r_contract.total().astype(LOW)
    ended.append(finals(f_contract, o_contract.at[q], 1))

    def self_image(i, carry):
        at = rows_of_image(i)
        for hp in range(PAIRS):
            lanes = pl.ds(hp * 128, 128)
            query = two_heads(acts[0, at, lanes])
            above = two_heads(grads[0, at, lanes])
            attn = acts[3, at, lanes].astype(WIDE)
            row = jnp.sum(above.astype(WIDE) * jnp.concatenate([attn, attn], axis=0), axis=-1, keepdims=True)
            probs = ps[i, hp]
            keys, values = acts[1, at, lanes], acts[2, at, lanes]
            inner = mm_nt(above, values)
            scores = (probs.astype(WIDE) * (inner - row)).astype(LOW)
            acts[0, at, lanes] = (one_pair(mm(scores, keys)) * 0.125).astype(LOW)
            acts[1, at, lanes] = mm_tn(scores, query).astype(LOW)
            acts[2, at, lanes] = mm_tn(probs, above).astype(LOW)
        return carry

    lax.fori_loop(0, images, self_image, 0)
    r_late = either(
        5, g_late, c_late, t_late,
        (lambda: tok[...], lambda: tok[...]),
        (lambda at: acts[0, :, at], lambda at: acts[2, :, at]),
    )
    r_last = reduce_at(6, g_last, c_last, t_last)
    half_parts(g_last, tok[...], lambda at: acts[1, :, at])
    r_last.core_stage()
    r_late.chip_stage()
    r_last.chip_stage()
    quarter = 24
    keys_total = r_keys.total()
    for part in range(4):
        k_out[part] = keys_total[quarter * part : quarter * part + quarter].astype(LOW)
    for r in range(1, 4):
        one = pltpu.make_async_remote_copy(
            k_out.at[others[r - 1]], k_in.at[r - 1], ksems.at[0, r - 1], ksems.at[1, r - 1],
            device_id=(d, others[r - 1]), device_id_type=MESH,
        )
        one.start()
        pushed.append(one)
    f_co[...] = r_co.total().astype(LOW)
    ended.append(finals(f_co, o_co.at[q], 2))
    f_mid[...] = r_mid.total().astype(LOW)
    ended.append(finals(f_mid, o_mid.at[q], 3))
    add_back(lambda: acts[0], SQ)
    add_back(lambda: acts[1], SK)
    add_back(lambda: acts[2], SV)
    pltpu.make_async_copy(wide.at[0], o_in, load.at[15]).start()
    f_late[...] = r_late.total().astype(LOW)
    ended.append(finals(f_late, o_late.at[q], 4))
    f_last[...] = r_last.total().astype(LOW)
    ended.append(finals(f_last, o_last.at[q], 5))
    sums = nsum[...]
    for r in range(1, 8):
        pltpu.make_async_remote_copy(
            nsum, nin.at[r - 1], nsems.at[0, r - 1], nsems.at[1, r - 1],
            device_id=(dpeers[r - 1], z), device_id_type=MESH,
        ).wait_recv()
        sums = sums + nin[r - 1]
    o_norms[...] = sums
    total = k_out[z].astype(WIDE)
    for r in range(1, 4):
        pltpu.make_async_remote_copy(
            k_in.at[r - 1], k_in.at[r - 1], ksems.at[0, r - 1], ksems.at[1, r - 1],
            device_id=(d, others[r - 1]), device_id_type=MESH,
        ).wait_recv()
        total = total + k_in[r - 1].astype(WIDE)
    o_keys[...] = total
    for i in range(2, 4):
        at = pl.ds(i * mem_rows, mem_rows)
        pltpu.make_async_copy(mout.at[i % 2], o_mem.at[at], mout_sems.at[i % 2]).wait()
    pltpu.make_async_copy(wide.at[0], o_in, load.at[15]).wait()
    fins = (f_expand, f_contract, f_co, f_mid, f_late, f_last)
    outs = [(out.at[q], out.at[1 - q]) for out in (o_expand, o_contract, o_co, o_mid, o_late, o_last)]
    for place, (fin, (out, theirs)) in enumerate(zip(fins, outs)):
        pltpu.make_async_copy(fin, out, local_sems.at[place]).wait()
        ended[place].wait_send()
        pltpu.make_async_remote_copy(
            fin, theirs, fin_sems.at[0, place], fin_sems.at[1, place], device_id=(d, zp), device_id_type=MESH
        ).wait_recv()
    for one in pushed:
        one.wait_send()
    for reducer in (r_contract, r_keys, r_co, r_mid, r_late, r_last):
        reducer.settle()


def backward(gains, cot, tok, mem, saved, images, queries, mem_rows):
    full, acts, ffn, us, inv, kv, pc, ps, wst = saved
    rows = images * QP
    tokens = images * mem_rows
    shape = jax.ShapeDtypeStruct
    outs = (
        shape((2, 96, 1536), LOW),
        shape((2, 384, 384), LOW),
        shape((2, 96, 384), LOW),
        shape((2, 96, D), LOW),
        shape((2, 96, D), LOW),
        shape((2, 96, 384), LOW),
        shape((24, 1536), WIDE),
        shape((tokens, D), LOW),
        shape((rows, D), WIDE),
        shape((8, D), WIDE),
    )
    dma = pltpu.SemaphoreType.DMA
    vmem = pltpu.VMEM
    return pl.pallas_call(
        functools.partial(backward_kernel, images, queries, mem_rows),
        out_shape=outs,
        in_specs=[INNER] * 3 + [ANY] * 12,
        out_specs=[ANY] * 6 + [INNER] + [ANY] * 2 + [INNER],
        scratch_shapes=[
            vmem((rows, D), LOW),
            vmem((rows, D), LOW),
            vmem((tokens, D), LOW),
            vmem((4, D, D), LOW),
            vmem((8, rows, D), LOW),
            vmem((2, rows, FF), LOW),
            vmem((2, rows, D), WIDE),
            vmem((rows, 128), WIDE),
            vmem((2, tokens, D), LOW),
            vmem((2, PAIRS, 2 * QP, mem_rows), LOW),
            vmem((images, PAIRS, 2 * QP, QP), LOW),
            vmem((images, QP, 128), WIDE),
            vmem((1, rows, D), WIDE),
            vmem((4, rows, D), LOW),
            vmem((8, D), WIDE),
            vmem((7, 8, D), WIDE),
            vmem((4, QP, D), LOW),
            vmem((3, QP, D), LOW),
            vmem((2, mem_rows, D), LOW),
            vmem((2, 4, 96, 1536), LOW),
            vmem((2, 4, 384, 384), LOW),
            vmem((2, 4, 96, 384), LOW),
            vmem((2, 4, 96, D), LOW),
            vmem((2, 4, 96, D), LOW),
            vmem((2, 4, 96, 384), LOW),
            vmem((4, 96, 1536), LOW),
            vmem((4, 384, 384), LOW),
            vmem((4, 96, 384), LOW),
            vmem((4, 96, D), LOW),
            vmem((4, 96, D), LOW),
            vmem((4, 96, 384), LOW),
            vmem((4, 96, 1536), LOW),
            vmem((3, 96, 1536), LOW),
            vmem((3, 384, 384), LOW),
            vmem((3, 96, 384), LOW),
            vmem((3, 96, D), LOW),
            vmem((3, 96, D), LOW),
            vmem((3, 96, 384), LOW),
            vmem((3, 96, 1536), LOW),
            vmem((96, 1536), LOW),
            vmem((384, 384), LOW),
            vmem((96, 384), LOW),
            vmem((96, D), LOW),
            vmem((96, D), LOW),
            vmem((96, 384), LOW),
            vmem((4, 24, 1536), LOW),
            vmem((3, 24, 1536), LOW),
            dma((16,)),
            dma((4,)),
            dma((2,)),
            dma((2,)),
            dma((2, 7, 1)),
            dma((2, 7, 3)),
            dma((2, 6)),
            dma((6,)),
            dma((2, 3)),
            dma((2, 2, 3)),
            dma((2, 7)),
        ],
        compiler_params=pltpu.CompilerParams(
            collective_id=1, has_side_effects=True, vmem_limit_bytes=VMEM_BYTES
        ),
        name="backward",
    )(*gains, cot, tok, mem, *saved)


def fused_on_device(
    inputs,
    memory,
    lengths,
    self_query,
    self_key,
    self_value,
    self_out,
    cross_query,
    cross_key,
    cross_value,
    cross_out,
    expand_weight,
    contract_weight,
    gain_one,
    shift_one,
    gain_two,
    shift_two,
    gain_three,
    shift_three,
    cotangent,
):
    images, queries, width = inputs.shape
    mem_rows = memory.shape[1]
    norms = (gain_one, shift_one, gain_two, shift_two, gain_three, shift_three)
    shards = (self_query, self_key, self_value, self_out, cross_query, cross_key, cross_value, cross_out, expand_weight, contract_weight)

    def padded(values):
        wider = jnp.pad(values, ((0, 0), (0, QP - queries), (0, 0)))
        return wider.reshape(images * QP, width)

    def cut(values):
        return values.reshape(images, QP, width)[:, :queries]

    tokens = padded(inputs)
    memory_flat = memory.reshape(images * mem_rows, width)
    result, full, acts, ffn, us, inv, kv, pc, ps, wst = forward(
        inputs, memory_flat, lengths, norms, shards, images, queries, mem_rows
    )
    spread, contracted, co, mid, late, last, keys, memory_grad, input_grad, sums = backward(
        norms[::2], padded(cotangent), tokens, memory_flat, (full, acts, ffn, us, inv, kv, pc, ps, wst),
        images, queries, mem_rows,
    )
    share = self_query.shape[0]
    sums = lax.dynamic_slice(sums, (0, lax.axis_index("dp") * share), (8, share))

    def beside(halves):
        return jnp.concatenate([halves[0], halves[1]], axis=1).astype(WIDE)

    return (
        cut(result),
        cut(input_grad),
        memory_grad.reshape(memory.shape).astype(WIDE),
        late[0].astype(WIDE),
        beside(last),
        late[1].astype(WIDE),
        mid[1].astype(WIDE),
        mid[0].astype(WIDE),
        keys[:, :width],
        keys[:, width:],
        beside(co),
        beside(spread),
        beside(contracted),
        *[sums[place] for place in range(6)],
    )


def solution(mesh):
    fused = mesh.shape["dp"] == 8 and mesh.shape["mem"] == 4

    rows = P("dp", None)
    image = P("dp", None, None)
    token = P("dp", "mem", None)
    both = P(("dp", "mem"), None)
    return jax.shard_map(
        fused_on_device if fused else on_device,
        mesh=mesh,
        in_specs=(image, token, P("dp"), *[rows] * 10, *[P()] * 6, image),
        out_specs=(image, image, token, *[rows] * 5, both, both, *[rows] * 3, *[P("dp")] * 6),
        check_vma=False,
    )
```

```python
import functools
import jax
import jax.numpy as jnp
from jax import lax
from jax.experimental import pallas as pl
from jax.experimental.pallas import tpu as pltpu
from jax.sharding import PartitionSpec as P

H = 12
LOW = jnp.bfloat16
WIDE = jnp.float32


def contract(a, b, dims):
    return lax.dot_general(a, b, (dims, ((), ())), preferred_element_type=WIDE)


def project(values, weight):
    return contract(values, weight, ((1,), (0,)))


def back_project(grads, weight):
    return contract(grads, weight, ((1,), (1,)))


def weight_grad(left, right):
    return contract(left, right, ((0,), (0,)))


def heads_of(values, images):
    rows, width = values.shape
    return values.reshape(images, rows // images, H, width // H)


def norm_forward(resid, gain, shift):
    center = resid - jnp.mean(resid, axis=-1, keepdims=True)
    inverse = lax.rsqrt(jnp.mean(center * center, axis=-1, keepdims=True) + 1e-05)
    normed = center * inverse
    return (normed * gain + shift, normed, inverse)


def norm_backward(incoming, normed, inverse, gain):
    scaled = incoming * gain
    grad_in = inverse * (
        scaled
        - jnp.mean(scaled, axis=-1, keepdims=True)
        - normed * jnp.mean(scaled * normed, axis=-1, keepdims=True)
    )
    return (grad_in, jnp.sum(incoming * normed, axis=0), jnp.sum(incoming, axis=0))


def scores_of(query, keys):
    return jnp.einsum("bqhe,bkhe->bhqk", query, keys, preferred_element_type=WIDE) * 0.125


def mix(probs, values):
    return jnp.einsum("bhqk,bkhe->bqhe", probs, values, preferred_element_type=WIDE)


def mix_back(probs, grads):
    return jnp.einsum("bhqk,bqhe->bkhe", probs, grads, preferred_element_type=WIDE)


def attention_backward(probs, attn, grad_attn, query, keys, values):
    row = jnp.sum(grad_attn.astype(WIDE) * attn.astype(WIDE), axis=-1).transpose(0, 2, 1)[..., None]
    grad_probs = jnp.einsum("bqhe,bkhe->bhqk", grad_attn, values, preferred_element_type=WIDE)
    grad_scores = (probs * (grad_probs - row)).astype(LOW)
    grad_query = mix(grad_scores, keys) * 0.125
    grad_keys = mix_back(grad_scores, query) * 0.125
    grad_values = mix_back(probs.astype(LOW), grad_attn)
    return (grad_query, grad_keys, grad_values)


def gelu_tanh(values):
    return jax.nn.gelu(values, approximate=True)


def on_device(
    inputs,
    memory,
    lengths,
    self_query,
    self_key,
    self_value,
    self_out,
    cross_query,
    cross_key,
    cross_value,
    cross_out,
    expand_weight,
    contract_weight,
    gain_one,
    shift_one,
    gain_two,
    shift_two,
    gain_three,
    shift_three,
    cotangent,
):
    images, queries, width = inputs.shape
    mem_rows = memory.shape[1]
    rows = images * queries
    share = self_query.shape[0]
    parts = width // share
    squares = (self_query, self_key, self_value, self_out, cross_query, cross_key, cross_value, cross_out)
    packed = lax.all_gather(jnp.stack(squares), "dp", axis=1, tiled=True)
    expand_full = lax.all_gather(expand_weight, "dp", axis=0, tiled=True)
    contract_full = lax.all_gather(contract_weight, "dp", axis=0, tiled=True)
    (query_full, key_full, value_full, out_full, cquery_full, ckey_full, cvalue_full, cout_full) = packed
    tokens = inputs.reshape(rows, width)
    memory_flat = memory.reshape(images * mem_rows, width)
    incoming = cotangent.reshape(rows, width).astype(WIDE)

    def joined(values):
        return values.reshape(-1, width)

    query_heads = heads_of(project(tokens, query_full).astype(LOW), images)
    key_heads = heads_of(project(tokens, key_full).astype(LOW), images)
    value_heads = heads_of(project(tokens, value_full).astype(LOW), images)
    self_raw = scores_of(query_heads, key_heads)
    self_exp = jnp.exp(self_raw - jnp.max(self_raw, axis=-1, keepdims=True))
    self_probs = self_exp / jnp.sum(self_exp, axis=-1, keepdims=True)
    self_attn = joined(mix(self_probs.astype(LOW), value_heads)).astype(LOW)
    first, normed_one, inverse_one = norm_forward(
        tokens.astype(WIDE) + project(self_attn, out_full), gain_one, shift_one
    )
    first_low = first.astype(LOW)
    cross_q = heads_of(project(first_low, cquery_full).astype(LOW), images)
    cross_k = heads_of(project(memory_flat, ckey_full).astype(LOW), images)
    cross_v = heads_of(project(memory_flat, cvalue_full).astype(LOW), images)
    places = lax.axis_index("mem") * mem_rows + jnp.arange(mem_rows, dtype=jnp.int32)
    valid = (places[None, :] < lengths[:, None])[:, None, None, :]
    cross_raw = jnp.where(valid, scores_of(cross_q, cross_k), -1e30)
    top = lax.pmax(jnp.max(cross_raw, axis=-1, keepdims=True), "mem")
    cross_exp = jnp.where(valid, jnp.exp(cross_raw - top), 0.0)
    total = lax.psum(jnp.sum(cross_exp, axis=-1, keepdims=True), "mem")
    cross_probs = cross_exp / total
    cross_attn = lax.psum(joined(mix(cross_probs.astype(LOW), cross_v)).astype(LOW), "mem")
    second, normed_two, inverse_two = norm_forward(
        first + project(cross_attn, cout_full), gain_two, shift_two
    )
    second_low = second.astype(LOW)
    pre_act = project(second_low, expand_full)
    activ, gelu_pull = jax.vjp(gelu_tanh, pre_act)
    activ_low = activ.astype(LOW)
    result, normed_three, inverse_three = norm_forward(
        second + project(activ_low, contract_full), gain_three, shift_three
    )
    grad_three, gain_three_part, shift_three_part = norm_backward(
        incoming, normed_three, inverse_three, gain_three
    )
    grad_ffn = grad_three.astype(LOW)

    def scattered(part, axes="dp"):
        return lax.psum_scatter(part, axes, scatter_dimension=0, tiled=True).astype(WIDE)

    contract_grad = scattered(weight_grad(activ_low, grad_ffn).astype(LOW))
    grad_pre = gelu_pull(back_project(grad_ffn, contract_full))[0].astype(LOW)
    expand_grad = scattered(weight_grad(second_low, grad_pre).astype(LOW))
    grad_second = grad_three + back_project(grad_pre, expand_full)
    grad_two, gain_two_part, shift_two_part = norm_backward(
        grad_second, normed_two, inverse_two, gain_two
    )
    grad_cross = grad_two.astype(LOW)
    cout_part = weight_grad(cross_attn, grad_cross)
    grad_cattn = heads_of(back_project(grad_cross, cout_full).astype(LOW), images)
    part_cquery, grad_ckey, grad_cvalue = attention_backward(
        cross_probs, heads_of(cross_attn, images), grad_cattn, cross_q, cross_k, cross_v
    )
    grad_cquery = lax.psum(joined(part_cquery).astype(LOW), "mem")
    grad_ckey = joined(grad_ckey).astype(LOW)
    grad_cvalue = joined(grad_cvalue).astype(LOW)
    kv_grad = scattered(
        jnp.concatenate(
            [weight_grad(memory_flat, grad_ckey), weight_grad(memory_flat, grad_cvalue)], axis=1
        ).astype(LOW),
        ("dp", "mem"),
    )
    memory_grad = back_project(grad_ckey, ckey_full) + back_project(grad_cvalue, cvalue_full)
    cquery_part = weight_grad(first_low, grad_cquery)
    grad_first = grad_two + back_project(grad_cquery, cquery_full)
    grad_one, gain_one_part, shift_one_part = norm_backward(
        grad_first, normed_one, inverse_one, gain_one
    )
    grad_self = grad_one.astype(LOW)
    out_part = weight_grad(self_attn, grad_self)
    grad_sattn = heads_of(back_project(grad_self, out_full).astype(LOW), images)
    grad_query, grad_key, grad_value = (
        joined(grad).astype(LOW)
        for grad in attention_backward(
            self_probs, heads_of(self_attn, images), grad_sattn, query_heads, key_heads, value_heads
        )
    )
    input_grad = (
        grad_one
        + back_project(grad_query, query_full)
        + back_project(grad_key, key_full)
        + back_project(grad_value, value_full)
    )
    norm_parts = jnp.stack(
        [gain_one_part, shift_one_part, gain_two_part, shift_two_part, gain_three_part, shift_three_part], axis=1
    )
    rest = scattered(
        jnp.concatenate(
            [
                weight_grad(tokens, grad_query),
                weight_grad(tokens, grad_key),
                weight_grad(tokens, grad_value),
                out_part,
                cquery_part,
                cout_part,
                jnp.pad(norm_parts, ((0, 0), (0, 122))),
            ],
            axis=1,
        ).astype(LOW)
    )
    squares_grad = [rest[:, place * width : (place + 1) * width] for place in range(6)]
    norms_grad = [rest[:, 6 * width + place] for place in range(6)]
    return (
        result.reshape(inputs.shape),
        input_grad.reshape(inputs.shape),
        memory_grad.reshape(memory.shape),
        *squares_grad[:5],
        kv_grad[:, :width],
        kv_grad[:, width:],
        squares_grad[5],
        expand_grad,
        contract_grad,
        *norms_grad,
    )


MESH = pl.DeviceIdType.MESH
ANY = pl.BlockSpec(memory_space=pl.ANY)
INNER = pl.BlockSpec(memory_space=pltpu.VMEM)
SCALAR = pl.BlockSpec(memory_space=pltpu.SMEM)
D = 768
FF = 3072
PAIRS = 6
QP = 112
PIECES = 16
SQ, SK, SV, SO, CK, CV, CQ, CO, EX, CT = 0, 1, 2, 3, 4, 5, 6, 7, 8, 12
WINDOW = 2
FIRST_DUE = 7.0
UNIT_TIME = 3.5
EXCHANGE_TIME = 13.0
VMEM_BYTES = 60 * 2**20


def mm(a, b):
    return lax.dot_general(a, b, (((1,), (0,)), ((), ())), preferred_element_type=WIDE)


def mm_nt(a, b):
    return lax.dot_general(a, b, (((1,), (1,)), ((), ())), preferred_element_type=WIDE)


def mm_tn(a, b):
    return lax.dot_general(a, b, (((0,), (0,)), ((), ())), preferred_element_type=WIDE)


def low_lanes(shape):
    return lax.broadcasted_iota(jnp.int32, shape, 1) < 64


def two_heads(pair):
    lower = low_lanes(pair.shape)
    nought = jnp.zeros_like(pair)
    return jnp.concatenate([jnp.where(lower, pair, nought), jnp.where(lower, nought, pair)], axis=0)


def one_pair(both):
    rows = both.shape[0] // 2
    upper = both[rows:]
    return jnp.where(low_lanes(upper.shape), both[:rows], upper)


def places():
    d = lax.axis_index("dp")
    c = lax.rem(d, 2)
    x = lax.rem(d // 2, 2)
    y = d // 4
    other = d + 1 - 2 * c
    beside = d + 2 - 4 * x
    above = d + 4 - 8 * y
    across = beside + 4 - 8 * y
    return d, other, beside, above, across


def weight_row(piece, owner):
    if isinstance(piece, int) and piece >= CT:
        return pl.multiple_of(CT * D + owner * 384 + (piece - CT) * 96, 96)
    return pl.multiple_of(piece * D + owner * 96, 96)


UNITS = ((SQ, SK), (SV,), (CK, CV), (SO,), (CQ,), (CO,), (8,), (9,), (10,), (11,), (12,), (13,), (14,), (15,))
LAG = 2


class Gather:
    def __init__(self, shards, full, local, send, recv, saved, save):
        self.shards, self.full, self.saved, self.save = shards, full, saved, save
        self.local, self.send, self.recv = local, send, recv
        self.d, self.other, self.beside, self.above, self.across = places()
        self.z = lax.axis_index("mem")
        self.q = lax.rem(self.z, 2)
        self.near = self.z + 1 - 2 * self.q
        self.sent = []
        self.role = {}
        self.done = 0
        self.clock = 0.0
        self.landed = [False] * PIECES
        self.unit_of = {piece: place for place, unit in enumerate(UNITS) for piece in unit}

    def at(self, piece, owner):
        return self.full.at[pl.ds(weight_row(piece, owner), 96)]

    def own(self, piece):
        if piece < EX:
            return self.shards[piece]
        if piece < CT:
            return self.shards[EX].at[:, pl.ds((piece - EX) * D, D)]
        return self.shards[EX + 1].at[pl.ds((piece - CT) * 96, 96)]

    def copy(self, src, piece, owner, kind, target, note):
        return pltpu.make_async_remote_copy(
            src,
            self.at(piece, owner),
            self.send.at[piece, note],
            self.recv.at[piece, kind],
            device_id=target,
            device_id_type=MESH,
        )

    def push(self, src, piece, owner, kind, target):
        one = self.copy(src, piece, owner, kind, (target, self.z), kind)
        one.start()
        self.sent.append(one)

    def lend(self, piece, owner, kind):
        one = self.copy(self.at(piece, owner), piece, owner, kind, (self.d, self.near), 7 + kind)
        one.start()
        self.sent.append(one)

    def arrived(self, piece, kind):
        self.copy(self.at(piece, self.d), piece, self.d, kind, (self.other, self.z), kind).wait_recv()

    def roles(self, unit):
        if unit not in self.role:
            first, second = unit
            mine = first + self.q * (second - first)
            self.role[unit] = (mine, first + second - mine)
        return self.role[unit]

    def local_copy(self, piece):
        return pltpu.make_async_copy(self.own(piece), self.at(piece, self.d), self.local.at[piece])

    def start(self, place):
        if place >= len(UNITS):
            return
        unit = UNITS[place]
        if len(unit) == 1:
            piece = unit[0]
            src = self.own(piece)
            self.local_copy(piece).start()
        else:
            piece, theirs = self.roles(unit)
            src = self.at(piece, self.d)
            self.push(self.at(theirs, self.d), theirs, self.d, 3, self.other)
        self.push(src, piece, self.d, 0, self.beside)
        self.push(src, piece, self.d, 1, self.above)
        self.push(src, piece, self.d, 3, self.other)

    def prepare(self):
        for unit in UNITS:
            if len(unit) == 2:
                for piece in unit:
                    self.local_copy(piece).start()

    def begin(self):
        for unit in UNITS:
            if len(unit) == 2:
                for piece in unit:
                    self.local_copy(piece).wait()
        for place in range(WINDOW):
            self.start(place)

    def relay(self, place):
        unit = UNITS[place]
        piece = unit[0] if len(unit) == 1 else self.roles(unit)[0]
        for kind, owner, side, target in ((0, self.beside, 0, self.above), (1, self.above, 1, self.beside)):
            self.arrived(piece, kind)
            if place % 2 == side:
                self.push(self.at(piece, owner), piece, owner, 2, target)
            self.push(self.at(piece, owner), piece, owner, 4 + kind, self.other)
            if len(unit) == 2:
                self.lend(piece, owner, kind)

    def finish(self, place):
        unit = UNITS[place]
        piece = unit[0] if len(unit) == 1 else self.roles(unit)[0]
        self.arrived(piece, 2)
        self.push(self.at(piece, self.across), piece, self.across, 6, self.other)
        if len(unit) == 2:
            self.lend(piece, self.across, 2)

    def borrow(self, place):
        unit = UNITS[place]
        if len(unit) == 2:
            piece = self.roles(unit)[1]
            for kind, owner in enumerate((self.beside, self.above, self.across)):
                self.arrived(piece, kind)
                self.push(self.at(piece, owner), piece, owner, 4 + kind, self.other)

    def step(self):
        place = self.done
        if place >= len(UNITS) + LAG:
            return
        self.done += 1
        if place < len(UNITS):
            self.relay(place)
            self.start(place + WINDOW)
        if 1 <= place <= len(UNITS):
            self.finish(place - 1)
        if place >= LAG:
            self.borrow(place - LAG)

    def due(self, place):
        return FIRST_DUE + UNIT_TIME * place

    def spend(self, time):
        self.wait_for(self.clock + time)

    def wait_for(self, clock):
        self.clock = max(self.clock, clock)
        while self.done < len(UNITS) + LAG and self.due(self.done) <= self.clock:
            self.step()

    def upto(self, count):
        while self.done < min(count, len(UNITS) + LAG):
            self.clock = max(self.clock, self.due(self.done))
            self.step()

    def ready(self, piece):
        place = self.unit_of[piece]
        self.upto(place + 1 + (1 if len(UNITS[place]) == 1 else LAG))
        if self.landed[piece]:
            return
        self.landed[piece] = True
        if len(UNITS[place]) == 1:
            self.local_copy(piece).wait()
        for kind in range(3, 7):
            self.arrived(piece, kind)
        if piece < CT:
            self.save(self.full.at[pl.ds(piece * D, D)], self.saved.at[pl.ds(piece * D, D)])

    def close(self):
        for one in self.sent:
            one.wait_send()


def greet(targets):
    barrier = pltpu.get_barrier_semaphore()
    for target in targets:
        pl.semaphore_signal(barrier, 1, device_id=target, device_id_type=MESH)
    pl.semaphore_wait(barrier, len(targets))


def norm_rows(resid, gain, shift):
    center = resid - jnp.mean(resid, axis=-1, keepdims=True)
    inverse = lax.rsqrt(jnp.mean(center * center, axis=-1, keepdims=True) + 1e-05)
    normed = center * inverse
    return normed * gain + shift, normed, inverse


def forward_kernel(images, queries, mem_rows, *refs):
    (raw, mem, lens, *rest) = refs
    norms, rest = rest[:6], rest[6:]
    shards = rest[:10]
    (o_result, o_full, o_acts, o_ffn, o_us, o_inv, o_kv, o_pc, o_ps, o_wst) = rest[10:20]
    (
        full, acts, ffn, us, inv, kv, pc, ps, wst, tok, wide, stats, osend, orecv, lsend, lrecv, fst,
        local, send, recv, zsend, zrecv, keep,
    ) = rest[20:]
    rows = images * QP
    z = lax.axis_index("mem")
    d = lax.axis_index("dp")
    kept = []

    def save(src, dst):
        one = pltpu.make_async_copy(src, dst, keep.at[len(kept)])
        one.start()
        kept.append(one)

    gather = Gather(shards, full, local, send, recv, o_full, save)
    others = [lax.rem(z + r, 4) for r in range(1, 4)]
    gather.prepare()
    greet(
        [(gather.other, z), (gather.beside, z), (gather.above, z)] + [(d, other) for other in others]
    )
    gather.begin()
    blank = jnp.zeros((QP - queries, D), LOW)
    for i in range(images):
        tok[pl.ds(i * QP, QP), :] = jnp.concatenate([raw[i], blank], axis=0)

    def weight(piece, tile):
        return full[pl.ds(piece * D, D), cols(tile)]

    def cols(tile):
        return pl.ds(pl.multiple_of(tile * 256, 256), 256)

    def image(i):
        return pl.ds(pl.multiple_of(i * QP, QP), QP)

    def project_rows(src, piece, dst, scale):
        def body(tile, carry):
            out = mm(src[...], weight(piece, tile)).astype(LOW)
            if scale != 1.0:
                out = out * jnp.asarray(scale, LOW)
            acts[dst, :, cols(tile)] = out
            return carry

        lax.fori_loop(0, 3, body, 0, unroll=True)

    gather.ready(SQ)
    project_rows(tok, SQ, 0, 0.125)
    gather.ready(SK)
    project_rows(tok, SK, 1, 1.0)
    gather.ready(SV)
    project_rows(tok, SV, 2, 1.0)

    gather.spend(2.0)
    for i in range(images):
        at = image(i)
        valid = lax.broadcasted_iota(jnp.int32, (2 * QP, QP), 1) < queries

        def self_pair(hp, carry):
            lanes = pl.ds(pl.multiple_of(hp * 128, 128), 128)
            scores = mm_nt(two_heads(acts[0, at, lanes]), acts[1, at, lanes])
            scores = jnp.where(valid, scores, -1e30)
            grown = jnp.exp(scores - jnp.max(scores, axis=-1, keepdims=True))
            probs = (grown / jnp.sum(grown, axis=-1, keepdims=True)).astype(LOW)
            ps[i, hp] = probs
            acts[3, at, lanes] = one_pair(mm(probs, acts[2, at, lanes])).astype(LOW)
            return carry

        lax.fori_loop(0, PAIRS, self_pair, 0, unroll=True)
        gather.spend(1.0)

    def memory_rows(piece, dst):
        for tile in range(3):
            kv[dst, :, cols(tile)] = mm(mem[...], weight(piece, tile)).astype(LOW)
            gather.spend(0.7)

    def add_branch(src, piece, base):
        def body(tile, carry):
            wide[0, :, cols(tile)] = base(cols(tile)) + mm(acts[src], weight(piece, tile))
            return carry

        lax.fori_loop(0, 3, body, 0, unroll=True)

    def normalize(which, low_dst):
        def body(i, carry):
            at = image(i)
            gain, shift = norms[2 * which][...][None, :], norms[2 * which + 1][...][None, :]
            out, normed, inverse = norm_rows(wide[0, at, :], gain, shift)
            us[which, at, :] = normed
            lane = lax.broadcasted_iota(jnp.int32, (QP, 128), 1)
            inv[at, :] = jnp.where(lane == which, inverse, inv[at, :])
            wide[1, at, :] = out
            if low_dst is not None:
                acts[low_dst, at, :] = out.astype(LOW)
            return carry

        lax.fori_loop(0, images, body, 0)

    inv[...] = jnp.zeros_like(inv)
    gather.ready(SO)
    add_branch(3, SO, lambda at: tok[:, at].astype(WIDE))
    normalize(0, 4)
    gather.spend(1.6)
    save(us.at[0], o_us.at[0])
    gather.ready(CK)
    memory_rows(CK, 0)
    gather.ready(CV)
    memory_rows(CV, 1)
    save(kv, o_kv)
    save(ps, o_ps)
    gather.ready(CQ)
    project_rows(acts.at[4], CQ, 5, 0.125)

    pushed = []

    def pass_on(src, dst, kind, r):
        one = pltpu.make_async_remote_copy(
            src, dst, zsend.at[kind, r - 1], zrecv.at[kind, r - 1],
            device_id=(d, others[r - 1]), device_id_type=MESH,
        )
        one.start()
        pushed.append(one)

    def taken(ref, kind, r):
        pltpu.make_async_remote_copy(
            ref, ref, zsend.at[kind, r - 1], zrecv.at[kind, r - 1],
            device_id=(d, others[r - 1]), device_id_type=MESH,
        ).wait_recv()

    lane = lax.broadcasted_iota(jnp.int32, (QP, 128), 1)

    def turned(tall):
        return jnp.concatenate([tall, jnp.zeros((128 - QP, 128), WIDE)], axis=0).T[:16]

    def returned(flat):
        return jnp.concatenate([flat, jnp.zeros((112, 128), WIDE)], axis=0).T[:QP]

    for turn in range(4):
        i = others[turn] if turn < 3 else z
        at = image(i)
        tokens = pl.ds(pl.multiple_of(i * mem_rows, mem_rows), mem_rows)
        place = z * mem_rows + lax.broadcasted_iota(jnp.int32, (2 * QP, mem_rows), 1)
        valid = place < lens[i]

        def pair(hp, noted):
            lanes = pl.ds(pl.multiple_of(hp * 128, 128), 128)
            scores = mm_nt(two_heads(acts[5, at, lanes]), kv[0, tokens, lanes])
            scores = jnp.where(valid, scores, -1e30)
            top = jnp.max(scores, axis=-1, keepdims=True)
            grown = jnp.where(valid, jnp.exp(scores - top), 0.0)
            total = jnp.sum(grown, axis=-1, keepdims=True)
            shrink = jnp.where(total > 0.0, 1.0 / total, 0.0)
            probs = grown.astype(LOW)
            pc[i, hp] = probs
            osend[turn, :, lanes] = one_pair(mm(probs, kv[1, tokens, lanes]) * shrink).astype(LOW)
            for half in range(2):
                span = slice(half * QP, half * QP + QP)
                noted = jnp.where(lane == 2 * hp + half, top[span], noted)
                noted = jnp.where(lane == 64 + 2 * hp + half, total[span], noted)
            return noted

        noted = lax.fori_loop(0, PAIRS, pair, jnp.zeros((QP, 128), WIDE), unroll=True)
        stats[i] = noted
        total = pltpu.roll(noted, 64, 1)
        lsend[turn] = turned(jnp.where(total > 0.0, noted + jnp.log(total), -1e30))
        if turn < 3:
            pass_on(osend.at[turn], orecv.at[turn], 0, turn + 1)
            pass_on(lsend.at[turn], lrecv.at[turn], 1, turn + 1)
        gather.spend(1.9)
    save(pc, o_pc)
    gather.wait_for(gather.clock + EXCHANGE_TIME - 5.0)
    for r in range(1, 4):
        taken(orecv.at[r - 1], 0, r)
        taken(lrecv.at[r - 1], 1, r)
    noted = [lsend[3], lrecv[0], lrecv[1], lrecv[2]]
    top = functools.reduce(jnp.maximum, noted)
    level = top + jnp.log(sum(jnp.exp(one - top) for one in noted))
    fst[z] = level
    share = [returned(jnp.exp(one - level)) for one in noted]
    lower = low_lanes((QP, 128))
    mine = image(z)
    for hp in range(PAIRS):
        lanes = pl.ds(hp * 128, 128)
        joined = jnp.zeros((QP, 128), WIDE)
        for r in range(4):
            spread = jnp.where(
                lower, share[r][:, 2 * hp : 2 * hp + 1], share[r][:, 2 * hp + 1 : 2 * hp + 2]
            )
            part = osend[3, :, lanes] if r == 0 else orecv[r - 1, :, lanes]
            joined = joined + spread * part.astype(WIDE)
        acts[6, mine, lanes] = joined.astype(LOW)
    for r in range(1, 4):
        pass_on(acts.at[6, mine], acts.at[6, mine], 2, r)
        pass_on(fst.at[z], fst.at[z], 3, r)
    gather.wait_for(gather.clock + EXCHANGE_TIME)
    gather.ready(CO)
    for r in range(1, 4):
        back = lax.rem(z + 4 - r, 4)
        taken(acts.at[6, image(back)], 2, r)
        taken(fst.at[back], 3, r)
    for i in range(images):
        wst[i] = jnp.exp(stats[i] - returned(fst[i]))
    save(wst, o_wst)
    add_branch(6, CO, lambda at: wide[1, :, at])
    normalize(1, 7)
    save(us.at[1], o_us.at[1])
    save(acts, o_acts)

    def expand(block):
        def body(tile, carry):
            pre = mm(acts[7], full[pl.ds((EX + block) * D, D), cols(tile)])
            root = 0.7978845608028654
            square = pre * pre
            bend = jnp.tanh(root * (pre + 0.044715 * (pre * square)))
            half = 0.5 * (1.0 + bend)
            slope = half + (0.5 * root) * pre * (1.0 - bend * bend) * (1.0 + 0.134145 * square)
            at = pl.ds(pl.multiple_of(block * D + tile * 256, 256), 256)
            ffn[0, :, at] = (pre * half).astype(LOW)
            ffn[1, :, at] = slope.astype(LOW)
            return carry

        lax.fori_loop(0, 3, body, 0, unroll=True)

    for block in range(4):
        gather.ready(EX + block)
        expand(block)
        gather.spend(1.2)
    save(ffn, o_ffn)
    for block in range(4):
        gather.ready(CT + block)
    save(full.at[pl.ds(CT * D, FF)], o_full.at[pl.ds(CT * D, FF)])

    def contract(tile, carry):
        wide[0, :, cols(tile)] = wide[1, :, cols(tile)] + mm(
            ffn[0], full[pl.ds(CT * D, FF), cols(tile)]
        )
        return carry

    lax.fori_loop(0, 3, contract, 0, unroll=True)
    normalize(2, None)
    save(wide.at[1], o_result)
    save(us.at[2], o_us.at[2])
    save(inv, o_inv)
    for one in pushed:
        one.wait_send()
    gather.close()
    for one in kept:
        one.wait()


def forward(tok, mem, lens, norms, shards, images, queries, mem_rows):
    rows = images * QP
    shape = jax.ShapeDtypeStruct
    tokens = images * mem_rows
    outs = (
        shape((rows, D), WIDE),
        shape((PIECES * D, D), LOW),
        shape((8, rows, D), LOW),
        shape((2, rows, FF), LOW),
        shape((3, rows, D), WIDE),
        shape((rows, 128), WIDE),
        shape((2, tokens, D), LOW),
        shape((images, PAIRS, 2 * QP, mem_rows), LOW),
        shape((images, PAIRS, 2 * QP, QP), LOW),
        shape((images, QP, 128), WIDE),
    )
    dma = pltpu.SemaphoreType.DMA
    return pl.pallas_call(
        functools.partial(forward_kernel, images, queries, mem_rows),
        out_shape=outs,
        in_specs=[INNER, INNER, SCALAR] + [INNER] * 6 + [ANY] * 10,
        out_specs=[ANY] * len(outs),
        scratch_shapes=[
            *[pltpu.VMEM(one.shape, one.dtype) for one in outs[1:]],
            pltpu.VMEM((rows, D), LOW),
            pltpu.VMEM((2, rows, D), WIDE),
            pltpu.VMEM((images, QP, 128), WIDE),
            pltpu.VMEM((4, QP, D), LOW),
            pltpu.VMEM((3, QP, D), LOW),
            pltpu.VMEM((4, 16, 128), WIDE),
            pltpu.VMEM((3, 16, 128), WIDE),
            pltpu.VMEM((images, 16, 128), WIDE),
            dma((PIECES,)),
            dma((PIECES, 10)),
            dma((PIECES, 7)),
            dma((4, 3)),
            dma((4, 3)),
            dma((28,)),
        ],
        compiler_params=pltpu.CompilerParams(
            collective_id=0, has_side_effects=True, vmem_limit_bytes=VMEM_BYTES
        ),
        name="forward",
    )(tok, mem, lens, *norms, *(shards[place] for place in (0, 1, 2, 3, 5, 6, 4, 7, 8, 9)))


def rows_of_image(i):
    return pl.ds(pl.multiple_of(i * QP, QP), QP)


def cols_of_tile(tile):
    return pl.ds(pl.multiple_of(tile * 256, 256), 256)


class Reduce:
    def __init__(self, where, turn, grad, core_in, chip_in, core_sems, chip_sems):
        self.where, self.turn = where, turn
        self.grad, self.core_in, self.chip_in = grad, core_in, chip_in
        self.core_sems, self.chip_sems = core_sems, chip_sems
        self.sent = []
        d, other, beside, above, across = where
        self.c = lax.rem(d, 2)
        self.z = lax.axis_index("mem")

    def copy(self, src, dst, sems, place, target):
        return pltpu.make_async_remote_copy(
            src, dst, sems.at[0, self.turn, place], sems.at[1, self.turn, place],
            device_id=(target, self.z), device_id_type=MESH,
        )

    def core_stage(self):
        one = self.copy(self.grad.at[1 - self.c], self.core_in, self.core_sems, 0, self.where[1])
        one.start()
        self.sent.append(one)

    def chip_stage(self):
        self.copy(self.core_in, self.core_in, self.core_sems, 0, self.where[1]).wait_recv()
        for chip in range(4):
            both = self.grad[self.c, chip].astype(WIDE) + self.core_in[chip].astype(WIDE)
            self.grad[self.c, chip] = both.astype(LOW)
        for place, target in enumerate(self.where[2:]):
            one = self.copy(
                self.grad.at[self.c, target // 2], self.chip_in.at[place], self.chip_sems, place, target
            )
            one.start()
            self.sent.append(one)

    def total(self):
        own = self.grad[self.c, self.where[0] // 2].astype(WIDE)
        for place, target in enumerate(self.where[2:]):
            self.copy(
                self.chip_in.at[place], self.chip_in.at[place], self.chip_sems, place, target
            ).wait_recv()
            own = own + self.chip_in[place].astype(WIDE)
        return own

    def settle(self):
        for one in self.sent:
            one.wait_send()
        self.sent = []


def backward_kernel(images, queries, mem_rows, *refs):
    (
        h_gain_one, h_gain_two, h_gain_three, h_cot, h_tok, h_mem, h_full, h_acts, h_ffn, h_us, h_inv, h_kv, h_pc, h_ps, h_wst,
    ) = refs[:15]
    (o_expand, o_contract, o_co, o_mid, o_late, o_last, o_keys, o_mem, o_in, o_norms) = refs[15:25]
    (
        cot, tok, mem, slots, acts, ffn, us, inv, kv, pc, ps, wst, wide, grads, nsum, nin,
        zsend, zin, mout,
        g_expand, g_contract, g_co, g_mid, g_late, g_last, c_expand, c_contract, c_co, c_mid, c_late, c_last, c_keys,
        t_expand, t_contract, t_co, t_mid, t_late, t_last, t_keys,
        f_expand, f_contract, f_co, f_mid, f_late, f_last, k_out, k_in,
        load, slot_sems, pc_sems, mout_sems, core_sems, chip_sems, fin_sems, local_sems, ksems, zsems, nsems,
    ) = refs[25:]
    z = lax.axis_index("mem")
    d = lax.axis_index("dp")
    where = places()
    q = lax.rem(z, 2)
    zp = z + 1 - 2 * q
    others = [lax.rem(z + r, 4) for r in range(1, 4)]
    dpeers = [lax.rem(d + r, 8) for r in range(1, 8)]

    gains = (h_gain_one, h_gain_two, h_gain_three)
    loads = {}
    waited = set()

    def fetch(name, src, dst):
        one = pltpu.make_async_copy(src, dst, load.at[len(loads)])
        one.start()
        loads[name] = one

    order = [CT, CT + 1, CT + 2, CT + 3, EX, EX + 1, EX + 2, EX + 3, CO, CK, CV, CQ, SO, SQ, SK, SV]
    depth = 4

    def slot_copy(turn):
        return pltpu.make_async_copy(
            h_full.at[pl.ds(order[turn] * D, D)], slots.at[turn % depth], slot_sems.at[turn % depth]
        )

    def prefetch(turn):
        if turn < len(order):
            slot_copy(turn).start()

    fetch("cot", h_cot, cot)
    fetch("u3", h_us.at[2], us.at[0])
    fetch("inv", h_inv, inv)
    prefetch(0)
    fetch("gp", h_ffn.at[1], ffn.at[1])

    def have(name):
        if name not in waited:
            waited.add(name)
            loads[name].wait()

    def pc_copy(turn):
        i = lax.rem(z + turn + 1, 4)
        return pltpu.make_async_copy(h_pc.at[i], pc.at[turn % 2], pc_sems.at[turn % 2])

    greet([(peer, z) for peer in dpeers] + [(d, other) for other in others])

    nsum[...] = jnp.zeros_like(nsum)

    def norm_back(which, incoming, slot, low_dst):
        def body(i, carry):
            at = rows_of_image(i)
            above = incoming(at)
            unit = us[slot, at, :]
            inverse = inv[at, which : which + 1]
            scaled = above * gains[which][...][None, :]
            first = jnp.mean(scaled, axis=-1, keepdims=True)
            second = jnp.mean(scaled * unit, axis=-1, keepdims=True)
            grad = inverse * (scaled - first - unit * second)
            wide[0, at, :] = grad
            grads[low_dst, at, :] = grad.astype(LOW)
            row = 2 * which
            nsum[row : row + 1, :] += jnp.sum(above * unit, axis=0, keepdims=True)
            nsum[row + 1 : row + 2, :] += jnp.sum(above, axis=0, keepdims=True)
            return carry

        lax.fori_loop(0, images, body, 0)

    turn_of = {piece: turn for turn, piece in enumerate(order)}

    def slot(piece):
        turn = turn_of[piece]
        slot_copy(turn).wait()
        return slots.at[turn % depth]

    def freed(piece):
        prefetch(turn_of[piece] + depth)

    for name in ("cot", "inv", "u3"):
        have(name)
    norm_back(2, lambda at: cot[at, :].astype(WIDE), 0, 0)
    for turn in range(1, depth):
        prefetch(turn)
    fetch("second_low", h_acts.at[7], acts.at[7])
    have("gp")
    for block in range(4):
        weight = slot(CT + block)

        def body(tile, carry):
            at = pl.ds(pl.multiple_of(block * D + tile * 256, 256), 256)
            back = mm_nt(grads[0], weight[cols_of_tile(tile), :])
            ffn[1, :, at] = (back * ffn[1, :, at].astype(WIDE)).astype(LOW)
            return carry

        lax.fori_loop(0, 3, body, 0, unroll=True)
        freed(CT + block)

    def reduce_at(place, grad, core_in, chip_in):
        return Reduce(where, place, grad, core_in, chip_in, core_sems, chip_sems)

    fetch("u2", h_us.at[1], us.at[1])
    fetch("kv", h_kv, kv)
    fetch("wst", h_wst, wst)
    fetch("acts", h_acts.at[pl.ds(0, 7)], acts.at[pl.ds(0, 7)])
    pc_copy(0).start()
    pc_copy(1).start()
    have("second_low")
    r_expand = reduce_at(0, g_expand, c_expand, t_expand)

    def expand_part(tile, carry):
        at = pl.ds(pl.multiple_of(q * 1536 + tile * 256, 256), 256)
        out = mm_tn(acts[7], ffn[1, :, at]).astype(LOW)
        for e in range(8):
            g_expand[e % 2, e // 2, :, cols_of_tile(tile)] = out[96 * e : 96 * e + 96]
        return carry

    lax.fori_loop(0, 6, expand_part, 0, unroll=2)
    r_expand.core_stage()
    for block in range(4):
        weight = slot(EX + block)

        def body(tile, carry):
            at = cols_of_tile(tile)
            back = mm_nt(ffn[1, :, pl.ds(block * D, D)], weight[at, :])
            wide[0, :, at] = wide[0, :, at] + back
            return carry

        lax.fori_loop(0, 3, body, 0, unroll=True)
        freed(EX + block)
        if block == 2:
            r_expand.chip_stage()
    have("u2")
    norm_back(1, lambda at: wide[0, at, :], 1, 1)

    def through(src, piece, dst):
        weight = slot(piece)

        def body(tile, carry):
            grads[dst, :, cols_of_tile(tile)] = mm_nt(grads[src], weight[cols_of_tile(tile), :]).astype(LOW)
            return carry

        lax.fori_loop(0, 3, body, 0, unroll=True)
        freed(piece)

    fetch("act", h_ffn.at[0], ffn.at[0])
    fetch("mem", h_mem, mem)
    fetch("u1", h_us.at[0], us.at[0])
    fetch("ps", h_ps, ps)
    fetch("tok", h_tok, tok)
    through(1, CO, 2)
    have("kv")
    have("wst")
    have("acts")
    pushed = []

    def across_mem(src, dst, kind, r):
        return pltpu.make_async_remote_copy(
            src, dst, zsems.at[0, kind, r - 1], zsems.at[1, kind, r - 1],
            device_id=(d, others[r - 1]), device_id_type=MESH,
        )

    for turn in range(4):
        i = lax.rem(z + turn + 1, 4)
        pc_copy(turn).wait()
        at = rows_of_image(i)
        tokens = pl.ds(pl.multiple_of(i * mem_rows, mem_rows), mem_rows)
        factors = wst[i]

        def pair(hp, carry):
            lanes = pl.ds(pl.multiple_of(hp * 128, 128), 128)
            query = two_heads(acts[5, at, lanes])
            above = two_heads(grads[2, at, lanes])
            attn = acts[6, at, lanes].astype(WIDE)
            row = jnp.sum(above.astype(WIDE) * jnp.concatenate([attn, attn], axis=0), axis=-1, keepdims=True)
            lane = lax.broadcasted_iota(jnp.int32, (QP, 128), 1)
            factor = jnp.concatenate(
                [
                    jnp.sum(jnp.where(lane == 2 * hp + half, factors, 0.0), axis=-1, keepdims=True)
                    for half in range(2)
                ],
                axis=0,
            )
            probs = pc[turn % 2, hp].astype(WIDE) * factor
            keys, values = kv[0, tokens, lanes], kv[1, tokens, lanes]
            inner = mm_nt(above, values)
            scores = (probs * (inner - row)).astype(LOW)
            zsend[turn, :, lanes] = (one_pair(mm(scores, keys)) * 0.125).astype(LOW)
            kv[0, tokens, lanes] = mm_tn(scores, query).astype(LOW)
            kv[1, tokens, lanes] = mm_tn(probs.astype(LOW), above).astype(LOW)
            return carry

        lax.fori_loop(0, PAIRS, pair, 0, unroll=True)
        if turn < 2:
            pc_copy(turn + 2).start()
        if turn < 3:
            one = across_mem(zsend.at[turn], zin.at[turn], 0, turn + 1)
            one.start()
            pushed.append(one)
        if turn == 1:
            have("act")
            r_contract = reduce_at(1, g_contract, c_contract, t_contract)

            def contract_part(e, carry):
                at = pl.ds(pl.multiple_of(e * 384, 384), 384)
                half = pl.ds(pl.multiple_of(q * 384, 384), 384)
                g_contract[lax.rem(e, 2), e // 2] = mm_tn(ffn[0, :, at], grads[0, :, half]).astype(LOW)
                return carry

            lax.fori_loop(0, 8, contract_part, 0, unroll=2)
            r_contract.core_stage()
        if turn == 3:
            r_contract.chip_stage()

    have("mem")
    f_expand[...] = r_expand.total().astype(LOW)
    r_expand.settle()
    r_keys = reduce_at(2, g_expand, c_keys, t_keys)

    def key_parts(which):
        def key_part(tile, carry):
            out = mm_tn(mem[...], kv[which, :, cols_of_tile(tile)]).astype(LOW)
            at = pl.ds(pl.multiple_of(which * D + tile * 256, 256), 256)
            for e in range(8):
                g_expand[e % 2, e // 2, :, at] = out[96 * e : 96 * e + 96]
            return carry

        lax.fori_loop(0, 3, key_part, 0, unroll=True)

    key_parts(0)
    for r in range(1, 4):
        across_mem(zin.at[r - 1], zin.at[r - 1], 0, r).wait_recv()
    mine = rows_of_image(z)
    grads[3, mine, :] = (
        zsend[3].astype(WIDE) + zin[0].astype(WIDE) + zin[1].astype(WIDE) + zin[2].astype(WIDE)
    ).astype(LOW)
    for r in range(1, 4):
        one = across_mem(grads.at[3, mine], grads.at[3, mine], 1, r)
        one.start()
        pushed.append(one)
    key_parts(1)
    r_keys.core_stage()

    def finals(fin, out, place):
        pltpu.make_async_copy(fin, out, local_sems.at[place]).start()
        one = pltpu.make_async_remote_copy(
            fin, out, fin_sems.at[0, place], fin_sems.at[1, place], device_id=(d, zp), device_id_type=MESH
        )
        one.start()
        return one

    ended = []
    key_weight, value_weight = slot(CK), slot(CV)
    for i in range(images):
        at = pl.ds(i * mem_rows, mem_rows)
        if i >= 2:
            pltpu.make_async_copy(mout.at[i % 2], o_mem.at[at], mout_sems.at[i % 2]).wait()

        def body(tile, carry):
            span = cols_of_tile(tile)
            mout[i % 2, :, span] = (
                mm_nt(kv[0, at, :], key_weight[span, :]) + mm_nt(kv[1, at, :], value_weight[span, :])
            ).astype(LOW)
            return carry

        lax.fori_loop(0, 3, body, 0, unroll=True)
        pltpu.make_async_copy(mout.at[i % 2], o_mem.at[at], mout_sems.at[i % 2]).start()
        if i == 1:
            r_keys.chip_stage()
    freed(CK)
    freed(CV)
    def wide_parts(place, grad, core_in, chip_in, left, right, tiles):
        def body(tile, carry):
            out = mm_tn(left(), right(cols_of_tile(tile))).astype(LOW)
            for e in range(8):
                grad[e % 2, e // 2, :, cols_of_tile(tile)] = out[96 * e : 96 * e + 96]
            return carry

        lax.fori_loop(0, tiles, body, 0, unroll=True)

    def half_parts(grad, left, right):
        half = pl.ds(pl.multiple_of(q * 384, 384), 384)
        out = mm_tn(left, right(half)).astype(LOW)
        for e in range(8):
            grad[e % 2, e // 2] = out[96 * e : 96 * e + 96]

    r_co = reduce_at(3, g_co, c_co, t_co)
    half_parts(g_co, acts[6], lambda at: grads[1, :, at])
    r_co.core_stage()
    for r in range(1, 4):
        back = lax.rem(z + 4 - r, 4)
        across_mem(grads.at[3, rows_of_image(back)], grads.at[3, rows_of_image(back)], 1, r).wait_recv()
    r_co.chip_stage()
    ended.append(finals(f_expand, o_expand.at[q], 0))

    def add_back(src, piece):
        weight = slot(piece)

        def body(tile, carry):
            span = cols_of_tile(tile)
            wide[0, :, span] = wide[0, :, span] + mm_nt(src(), weight[span, :])
            return carry

        lax.fori_loop(0, 3, body, 0, unroll=True)
        freed(piece)

    add_back(lambda: grads[3], CQ)
    have("u1")
    norm_back(0, lambda at: wide[0, at, :], 0, 2)
    for r in range(1, 8):
        one = pltpu.make_async_remote_copy(
            nsum, nin.at[r - 1], nsems.at[0, r - 1], nsems.at[1, r - 1],
            device_id=(dpeers[r - 1], z), device_id_type=MESH,
        )
        one.start()
        pushed.append(one)
    have("tok")

    def either(place, grad, core_in, chip_in, lefts, rights):
        reducer = reduce_at(place, grad, core_in, chip_in)
        for parity in range(2):

            @pl.when(q == parity)
            def _():
                wide_parts(place, grad, core_in, chip_in, lefts[parity], rights[parity], 3)

        reducer.core_stage()
        return reducer

    r_mid = either(
        4, g_mid, c_mid, t_mid,
        (lambda: acts[4], lambda: acts[3]),
        (lambda at: grads[3, :, at], lambda at: grads[2, :, at]),
    )
    through(2, SO, 0)
    have("ps")
    r_mid.chip_stage()
    f_contract[...] = r_contract.total().astype(LOW)
    ended.append(finals(f_contract, o_contract.at[q], 1))

    def self_image(i, carry):
        at = rows_of_image(i)
        for hp in range(PAIRS):
            lanes = pl.ds(hp * 128, 128)
            query = two_heads(acts[0, at, lanes])
            above = two_heads(grads[0, at, lanes])
            attn = acts[3, at, lanes].astype(WIDE)
            row = jnp.sum(above.astype(WIDE) * jnp.concatenate([attn, attn], axis=0), axis=-1, keepdims=True)
            probs = ps[i, hp]
            keys, values = acts[1, at, lanes], acts[2, at, lanes]
            inner = mm_nt(above, values)
            scores = (probs.astype(WIDE) * (inner - row)).astype(LOW)
            acts[0, at, lanes] = (one_pair(mm(scores, keys)) * 0.125).astype(LOW)
            acts[1, at, lanes] = mm_tn(scores, query).astype(LOW)
            acts[2, at, lanes] = mm_tn(probs, above).astype(LOW)
        return carry

    lax.fori_loop(0, images, self_image, 0)
    r_late = either(
        5, g_late, c_late, t_late,
        (lambda: tok[...], lambda: tok[...]),
        (lambda at: acts[0, :, at], lambda at: acts[2, :, at]),
    )
    r_last = reduce_at(6, g_last, c_last, t_last)
    half_parts(g_last, tok[...], lambda at: acts[1, :, at])
    r_last.core_stage()
    r_late.chip_stage()
    r_last.chip_stage()
    quarter = 24
    keys_total = r_keys.total()
    for part in range(4):
        k_out[part] = keys_total[quarter * part : quarter * part + quarter].astype(LOW)
    for r in range(1, 4):
        one = pltpu.make_async_remote_copy(
            k_out.at[others[r - 1]], k_in.at[r - 1], ksems.at[0, r - 1], ksems.at[1, r - 1],
            device_id=(d, others[r - 1]), device_id_type=MESH,
        )
        one.start()
        pushed.append(one)
    f_co[...] = r_co.total().astype(LOW)
    ended.append(finals(f_co, o_co.at[q], 2))
    f_mid[...] = r_mid.total().astype(LOW)
    ended.append(finals(f_mid, o_mid.at[q], 3))
    add_back(lambda: acts[0], SQ)
    add_back(lambda: acts[1], SK)
    add_back(lambda: acts[2], SV)
    pltpu.make_async_copy(wide.at[0], o_in, load.at[15]).start()
    f_late[...] = r_late.total().astype(LOW)
    ended.append(finals(f_late, o_late.at[q], 4))
    f_last[...] = r_last.total().astype(LOW)
    ended.append(finals(f_last, o_last.at[q], 5))
    sums = nsum[...]
    for r in range(1, 8):
        pltpu.make_async_remote_copy(
            nsum, nin.at[r - 1], nsems.at[0, r - 1], nsems.at[1, r - 1],
            device_id=(dpeers[r - 1], z), device_id_type=MESH,
        ).wait_recv()
        sums = sums + nin[r - 1]
    o_norms[...] = sums
    total = k_out[z].astype(WIDE)
    for r in range(1, 4):
        pltpu.make_async_remote_copy(
            k_in.at[r - 1], k_in.at[r - 1], ksems.at[0, r - 1], ksems.at[1, r - 1],
            device_id=(d, others[r - 1]), device_id_type=MESH,
        ).wait_recv()
        total = total + k_in[r - 1].astype(WIDE)
    o_keys[...] = total
    for i in range(2, 4):
        at = pl.ds(i * mem_rows, mem_rows)
        pltpu.make_async_copy(mout.at[i % 2], o_mem.at[at], mout_sems.at[i % 2]).wait()
    pltpu.make_async_copy(wide.at[0], o_in, load.at[15]).wait()
    fins = (f_expand, f_contract, f_co, f_mid, f_late, f_last)
    outs = [(out.at[q], out.at[1 - q]) for out in (o_expand, o_contract, o_co, o_mid, o_late, o_last)]
    for place, (fin, (out, theirs)) in enumerate(zip(fins, outs)):
        pltpu.make_async_copy(fin, out, local_sems.at[place]).wait()
        ended[place].wait_send()
        pltpu.make_async_remote_copy(
            fin, theirs, fin_sems.at[0, place], fin_sems.at[1, place], device_id=(d, zp), device_id_type=MESH
        ).wait_recv()
    for one in pushed:
        one.wait_send()
    for reducer in (r_contract, r_keys, r_co, r_mid, r_late, r_last):
        reducer.settle()


def backward(gains, cot, tok, mem, saved, images, queries, mem_rows):
    full, acts, ffn, us, inv, kv, pc, ps, wst = saved
    rows = images * QP
    tokens = images * mem_rows
    shape = jax.ShapeDtypeStruct
    outs = (
        shape((2, 96, 1536), LOW),
        shape((2, 384, 384), LOW),
        shape((2, 96, 384), LOW),
        shape((2, 96, D), LOW),
        shape((2, 96, D), LOW),
        shape((2, 96, 384), LOW),
        shape((24, 1536), WIDE),
        shape((tokens, D), LOW),
        shape((rows, D), WIDE),
        shape((8, D), WIDE),
    )
    dma = pltpu.SemaphoreType.DMA
    vmem = pltpu.VMEM
    return pl.pallas_call(
        functools.partial(backward_kernel, images, queries, mem_rows),
        out_shape=outs,
        in_specs=[INNER] * 3 + [ANY] * 12,
        out_specs=[ANY] * 6 + [INNER] + [ANY] * 2 + [INNER],
        scratch_shapes=[
            vmem((rows, D), LOW),
            vmem((rows, D), LOW),
            vmem((tokens, D), LOW),
            vmem((4, D, D), LOW),
            vmem((8, rows, D), LOW),
            vmem((2, rows, FF), LOW),
            vmem((2, rows, D), WIDE),
            vmem((rows, 128), WIDE),
            vmem((2, tokens, D), LOW),
            vmem((2, PAIRS, 2 * QP, mem_rows), LOW),
            vmem((images, PAIRS, 2 * QP, QP), LOW),
            vmem((images, QP, 128), WIDE),
            vmem((1, rows, D), WIDE),
            vmem((4, rows, D), LOW),
            vmem((8, D), WIDE),
            vmem((7, 8, D), WIDE),
            vmem((4, QP, D), LOW),
            vmem((3, QP, D), LOW),
            vmem((2, mem_rows, D), LOW),
            vmem((2, 4, 96, 1536), LOW),
            vmem((2, 4, 384, 384), LOW),
            vmem((2, 4, 96, 384), LOW),
            vmem((2, 4, 96, D), LOW),
            vmem((2, 4, 96, D), LOW),
            vmem((2, 4, 96, 384), LOW),
            vmem((4, 96, 1536), LOW),
            vmem((4, 384, 384), LOW),
            vmem((4, 96, 384), LOW),
            vmem((4, 96, D), LOW),
            vmem((4, 96, D), LOW),
            vmem((4, 96, 384), LOW),
            vmem((4, 96, 1536), LOW),
            vmem((3, 96, 1536), LOW),
            vmem((3, 384, 384), LOW),
            vmem((3, 96, 384), LOW),
            vmem((3, 96, D), LOW),
            vmem((3, 96, D), LOW),
            vmem((3, 96, 384), LOW),
            vmem((3, 96, 1536), LOW),
            vmem((96, 1536), LOW),
            vmem((384, 384), LOW),
            vmem((96, 384), LOW),
            vmem((96, D), LOW),
            vmem((96, D), LOW),
            vmem((96, 384), LOW),
            vmem((4, 24, 1536), LOW),
            vmem((3, 24, 1536), LOW),
            dma((16,)),
            dma((4,)),
            dma((2,)),
            dma((2,)),
            dma((2, 7, 1)),
            dma((2, 7, 3)),
            dma((2, 6)),
            dma((6,)),
            dma((2, 3)),
            dma((2, 2, 3)),
            dma((2, 7)),
        ],
        compiler_params=pltpu.CompilerParams(
            collective_id=1, has_side_effects=True, vmem_limit_bytes=VMEM_BYTES
        ),
        name="backward",
    )(*gains, cot, tok, mem, *saved)


def fused_on_device(
    inputs,
    memory,
    lengths,
    self_query,
    self_key,
    self_value,
    self_out,
    cross_query,
    cross_key,
    cross_value,
    cross_out,
    expand_weight,
    contract_weight,
    gain_one,
    shift_one,
    gain_two,
    shift_two,
    gain_three,
    shift_three,
    cotangent,
):
    images, queries, width = inputs.shape
    mem_rows = memory.shape[1]
    norms = (gain_one, shift_one, gain_two, shift_two, gain_three, shift_three)
    shards = (self_query, self_key, self_value, self_out, cross_query, cross_key, cross_value, cross_out, expand_weight, contract_weight)

    def padded(values):
        wider = jnp.pad(values, ((0, 0), (0, QP - queries), (0, 0)))
        return wider.reshape(images * QP, width)

    def cut(values):
        return values.reshape(images, QP, width)[:, :queries]

    tokens = padded(inputs)
    memory_flat = memory.reshape(images * mem_rows, width)
    result, full, acts, ffn, us, inv, kv, pc, ps, wst = forward(
        inputs, memory_flat, lengths, norms, shards, images, queries, mem_rows
    )
    spread, contracted, co, mid, late, last, keys, memory_grad, input_grad, sums = backward(
        norms[::2], padded(cotangent), tokens, memory_flat, (full, acts, ffn, us, inv, kv, pc, ps, wst),
        images, queries, mem_rows,
    )
    share = self_query.shape[0]
    sums = lax.dynamic_slice(sums, (0, lax.axis_index("dp") * share), (8, share))

    def beside(halves):
        return jnp.concatenate([halves[0], halves[1]], axis=1).astype(WIDE)

    return (
        cut(result),
        cut(input_grad),
        memory_grad.reshape(memory.shape).astype(WIDE),
        late[0].astype(WIDE),
        beside(last),
        late[1].astype(WIDE),
        mid[1].astype(WIDE),
        mid[0].astype(WIDE),
        keys[:, :width],
        keys[:, width:],
        beside(co),
        beside(spread),
        beside(contracted),
        *[sums[place] for place in range(6)],
    )


def solution(mesh):
    fused = mesh.shape["dp"] == 8 and mesh.shape["mem"] == 4

    rows = P("dp", None)
    image = P("dp", None, None)
    token = P("dp", "mem", None)
    both = P(("dp", "mem"), None)
    return jax.shard_map(
        fused_on_device if fused else on_device,
        mesh=mesh,
        in_specs=(image, token, P("dp"), *[rows] * 10, *[P()] * 6, image),
        out_specs=(image, image, token, *[rows] * 5, both, both, *[rows] * 3, *[P("dp")] * 6),
        check_vma=False,
    )
```
